32 devices in a mesh: grp: 4 (over x, core), dom: 8 (over z, y).
Axes of the slice: x: 2, y: 2, z: 4, core: 2. Of those that a mesh axis runs over, the one named last changes fastest.
Arguments:
- cell_index: int32 [3, 65536], P(None, ('grp', 'dom')), may hold values from 0 to 255, as said below
- offsets: float32 [3, 65536], P(None, ('grp', 'dom')), may hold values from -0.5 to 0.5
- species: int32 [65536], P(('grp', 'dom')), may hold values from 0 to 7
- pair_blocks: int32 [128, 2], P(('grp', 'dom')), may hold values from 0 to 47, as said below
- counts: int32 [32], P(('grp', 'dom')), may hold values from 1 to 4, as said below
- background: float32 [256, 256, 256], P('dom', 'grp'), may hold values from -0.12 to 0.12
- species_embed: float32 [8, 256], replicated, may hold values from -6 to 6
- neighbour_embed: float32 [8, 256], replicated, may hold values from -6 to 6
- w_radial: float32 [8, 256], replicated, may hold values from -2 to 2
- w_hidden: bfloat16 [256, 256], replicated, may hold values from -0.375 to 0.375
- w_charge: bfloat16 [256], replicated, may hold values from -0.375 to 0.375
- w_energy: bfloat16 [256], replicated, may hold values from -0.375 to 0.375
Outputs:
- site_energy: float32 [65536], P(('grp', 'dom'))
- electric_field: float32 [3, 65536], P(None, ('grp', 'dom'))
- charges: float32 [65536], P(('grp', 'dom'))
The draws below stay inside these ranges and needn't reach their ends.
Inputs may be any that keep to these rules, and one draw needn't show every extreme that they name: `cell_index`: atoms of domain k = g * 8 + d (atoms k * 2048 on) have a first index in [32 d, 32 d + 32) and a second in [64 g, 64 g + 64). Atom block b of a domain lies in second-index tile b mod 4 of width 64 / 4 and third-index tile b // 4 of width 256 / 4. `pair_blocks`: the i block is one of the domain's 16 blocks; the j block indexes the 48 extended blocks and lies in the same or an adjacent tile of its domain. `counts`: some device has exactly 4 live slots in every draw.
All inputs are finite; a program needn't handle non-finite values.
Results may differ from the reference program's by a relative error of at most 0.0003.
The reference program's roundings to bfloat16 on the way count: a program that leaves them out, or rounds other values in their place, can miss the bound.
Values sent between devices are 32-bit elements; how exact they have to be, the bound alone decides.
A program may use at most 128 MiB of HBM per device.

```python
import math
import jax
import jax.numpy as jnp
import numpy as np
from jax import lax

G = 256
D = 256
NBASIS = 8
NSPEC = 8
BLOCK = 128
A_DEV = 2048
PB_CAP = 4
NB = 16
SLAB = 32
QY = 64
ATOMS = 65536
PAIRS = 128
N_GRP = 4
N_DOM = 8


def draw_cell_index(key, part):
    atom_ids = jnp.arange(ATOMS, dtype=jnp.int32)
    device_ids = atom_ids // A_DEV
    group_ids = device_ids // N_DOM
    domain_ids = device_ids % N_DOM
    block_ids = atom_ids % A_DEV // BLOCK
    tiles_z = NB // 4
    tile_y_len = QY // 4
    tile_z_len = G // tiles_z
    key_x, key_y, key_z = jax.random.split(jax.random.fold_in(key, 11), 3)
    coord_x = SLAB * domain_ids + jax.random.randint(key_x, (ATOMS,), 0, SLAB)
    coord_y = QY * group_ids + block_ids % 4 * tile_y_len + jax.random.randint(key_y, (ATOMS,), 0, tile_y_len)
    coord_z = block_ids // 4 * tile_z_len + jax.random.randint(key_z, (ATOMS,), 0, tile_z_len)
    return jnp.stack([coord_x, coord_y, coord_z], axis=0).astype(jnp.int32)


def draw_pair_blocks(key, part):
    key_i, key_side, key_dy, key_dz = jax.random.split(jax.random.fold_in(key, 23), 4)
    block_i = jax.random.randint(key_i, (PAIRS,), 0, NB)
    side_ids = jax.random.randint(key_side, (PAIRS,), 0, 3)
    delta_y = jax.random.randint(key_dy, (PAIRS,), -1, 2)
    delta_z = jax.random.randint(key_dz, (PAIRS,), -1, 2)
    tiles_z = NB // 4
    tile_y = jnp.clip(block_i % 4 + delta_y, 0, 3)
    tile_z = (block_i // 4 + delta_z + tiles_z) % tiles_z
    block_j = side_ids * NB + tile_z * 4 + tile_y
    return jnp.stack([block_i, block_j], axis=1).astype(jnp.int32)


def draw_counts(key, part):
    device_total = PAIRS // PB_CAP
    key_a, key_b, key_top = jax.random.split(jax.random.fold_in(key, 37), 3)
    first_draw = jax.random.randint(key_a, (device_total,), 1, PB_CAP + 1)
    second_draw = jax.random.randint(key_b, (device_total,), 1, PB_CAP + 1)
    live_slots = jnp.minimum(first_draw, second_draw)
    busiest = jax.random.randint(key_top, (), 0, device_total)
    live_slots = jnp.where(jnp.arange(device_total, dtype=jnp.int32) == busiest, PB_CAP, live_slots)
    return live_slots.astype(jnp.int32)


def draw_background(key, part):
    inner_key = jax.random.fold_in(key, 51)
    return jnp.clip(0.02 * jax.random.normal(inner_key, (G, G, G), jnp.float32), -0.12, 0.12)


def set_ends(array, rng, least, top_value):
    longest = array.shape.index(max(array.shape))
    spots = []
    for shift in (0, 1):
        where = [jax.random.randint(jax.random.fold_in(rng, axis), (), 0, length) for axis, length in enumerate(array.shape)]
        where[longest] = (where[longest] + shift) % array.shape[longest]
        spots.append(tuple(where))
    return array.at[spots[0]].set(least).at[spots[1]].set(top_value)


def levels(stream_key, extent, cuts, least, largest):
    factor_of, own = 1.0, jax.random.fold_in(stream_key, 6)
    for axis_at, blocks in cuts:
        steps = jnp.exp(jax.random.uniform(jax.random.fold_in(own, axis_at), (blocks,), jnp.float32, least / len(cuts), largest / len(cuts)))
        factor_of = factor_of * jnp.repeat(steps, extent[axis_at] // blocks).reshape([-1 if axis == axis_at else 1 for axis in range(len(extent))])
    return factor_of


def cumulative_ranks(number_of, skew):
    portions = [(1 << 20) // math.isqrt(rank ** skew) + 1 for rank in range(1, number_of + 1)]
    width = 1 + sum(portions) // (1 << 30)
    return np.cumsum(np.array([max(1, weight // width) for weight in portions]))


def ranked(own_key, extent, number_of, skew):
    grid = cumulative_ranks(number_of, skew)
    pick = jax.random.randint(jax.random.fold_in(own_key, 1), extent, 0, int(grid[number_of - 1]))
    rank = jnp.searchsorted(jnp.asarray(grid, jnp.int32), pick, side="right")
    return jax.random.permutation(jax.random.fold_in(own_key, 2), number_of)[rank].astype(jnp.int32)


def scatter_about(rng, dims, scale, limit, kind=jnp.bfloat16):
    return jnp.clip(scale * jax.random.normal(rng, dims, jnp.float32), -limit, limit).astype(kind)


def setup_inputs(seed: int = 0) -> dict:
    splits = jax.random.split(jax.random.key(seed), 13)
    return {
        "cell_index": draw_cell_index(jax.random.fold_in(splits[12], 71), 0),
        "offsets": jnp.clip(jax.random.uniform(splits[1], (3, ATOMS), jnp.float32, -0.5, 0.5) * levels(splits[1], (3, ATOMS), ((1, 32),), -0.4, 0.0), -0.5, 0.5),
        "species": set_ends(ranked(splits[2], (ATOMS,), NSPEC, 2), jax.random.fold_in(splits[2], 3), 0, NSPEC - 1).astype(jnp.int32),
        "pair_blocks": draw_pair_blocks(jax.random.fold_in(splits[12], 71), 0),
        "counts": draw_counts(jax.random.fold_in(splits[12], 71), 0),
        "background": draw_background(jax.random.fold_in(splits[12], 71), 0),
        "species_embed": scatter_about(splits[6], (NSPEC, D), 1.0, 6.0, jnp.float32),
        "neighbour_embed": scatter_about(splits[7], (NSPEC, D), 1.0, 6.0, jnp.float32),
        "w_radial": scatter_about(splits[8], (NBASIS, D), NBASIS ** -0.5, 2.0, jnp.float32),
        "w_hidden": scatter_about(splits[9], (D, D), D ** -0.5, 0.375),
        "w_charge": scatter_about(splits[10], (D,), D ** -0.5, 0.375),
        "w_energy": scatter_about(splits[11], (D,), D ** -0.5, 0.375),
    }


CUTOFF = 6.0
EWALD = 1.0
HIGHEST = lax.Precision.HIGHEST

def spline_weights(frac):
    return ((0.5 - frac) * (0.5 - frac) * 0.5, 0.75 - frac * frac, (0.5 + frac) * (0.5 + frac) * 0.5)

def spline_slopes(frac):
    return (frac - 0.5, -2.0 * frac, 0.5 + frac)

def green_table(freq_x, freq_y, freq_z):

    def signed(frequency):
        return jnp.where(frequency < G // 2, frequency, frequency - G)
    signed_x = signed(freq_x)
    signed_y = signed(freq_y)
    signed_z = signed(freq_z)
    squares = signed_x * signed_x + signed_y * signed_y + signed_z * signed_z
    wave_sq = squares.astype(jnp.float32) * (2.0 * math.pi / G * (2.0 * math.pi / G))
    safe_sq = jnp.where(squares > 0, wave_sq, 1.0)
    return jnp.where(squares > 0, 4.0 * math.pi * jnp.exp(-wave_sq / (4.0 * EWALD * EWALD)) / safe_sq, 0.0)

def pair_terms(pos_i, pos_j, embed_i, embed_j, self_mask, w_radial, w_hidden, w_charge, w_energy):
    separation = pos_j[:, None, :] - pos_i[:, :, None]
    half_box = 0.5 * G
    separation = jnp.where(separation > half_box, separation - G, jnp.where(separation < -half_box, separation + G, separation))
    distance = jnp.sqrt(lax.optimization_barrier(jnp.sum(separation * separation, axis=0)))
    scaled = distance / CUTOFF
    inside = 1.0 - scaled * scaled
    envelope = jnp.where(scaled < 1.0, inside * inside, 0.0)
    envelope = jnp.where(self_mask, 0.0, envelope)
    orders = jnp.arange(1, NBASIS + 1).astype(jnp.float32)
    radial = jnp.sinc(scaled[:, :, None] * orders)
    hidden_pre = jnp.einsum('ijn,nd->ijd', radial, w_radial, precision=HIGHEST) + embed_i[:, None, :] + embed_j[None, :, :]
    edge_feat = jax.nn.silu(hidden_pre).astype(jnp.bfloat16).reshape(-1, w_radial.shape[1])
    charge_pair = jnp.dot(edge_feat, w_charge, preferred_element_type=jnp.float32).reshape(envelope.shape)
    latent = jax.nn.silu(jnp.dot(edge_feat, w_hidden, preferred_element_type=jnp.float32)).astype(jnp.bfloat16)
    energy_pair = jnp.dot(latent, w_energy, preferred_element_type=jnp.float32).reshape(envelope.shape)
    return (lax.optimization_barrier(jnp.sum(envelope * energy_pair, axis=1)), lax.optimization_barrier(jnp.sum(envelope * charge_pair, axis=1)))

def reference(cell_index, offsets, species, pair_blocks, counts, background, species_embed, neighbour_embed, w_radial, w_hidden, w_charge, w_energy):
    positions = cell_index.astype(jnp.float32) + offsets
    device_count = N_GRP * N_DOM
    block_count = A_DEV // BLOCK

    def one_device(device):
        group_id = device // N_DOM
        domain_id = device % N_DOM
        left_dev = group_id * N_DOM + (domain_id + N_DOM - 1) % N_DOM
        right_dev = group_id * N_DOM + (domain_id + 1) % N_DOM

        def slice_pos(owner):
            return lax.dynamic_slice_in_dim(positions, (owner * A_DEV).astype(jnp.int32), A_DEV, 1)

        def slice_spec(owner):
            return lax.dynamic_slice_in_dim(species, (owner * A_DEV).astype(jnp.int32), A_DEV, 0)
        own_pos = slice_pos(device)
        ext_pos = jnp.concatenate([slice_pos(left_dev), own_pos, slice_pos(right_dev)], axis=1)
        own_embed = species_embed[slice_spec(device)]
        ext_embed = neighbour_embed[jnp.concatenate([slice_spec(left_dev), slice_spec(device), slice_spec(right_dev)], axis=0)]
        diagonal = jnp.arange(BLOCK, dtype=jnp.int32)[:, None] == jnp.arange(BLOCK, dtype=jnp.int32)[None, :]

        def visit_slot(slot_num, running):
            energy_acc, charge_acc = running
            row_id = (device * PB_CAP + slot_num).astype(jnp.int32)
            block_i = pair_blocks[row_id, 0]
            block_j = pair_blocks[row_id, 1]
            start_i = (block_i * BLOCK).astype(jnp.int32)
            start_j = (block_j * BLOCK).astype(jnp.int32)
            pos_i = lax.dynamic_slice_in_dim(own_pos, start_i, BLOCK, 1)
            pos_j = lax.dynamic_slice_in_dim(ext_pos, start_j, BLOCK, 1)
            embed_i = lax.dynamic_slice_in_dim(own_embed, start_i, BLOCK, 0)
            embed_j = lax.dynamic_slice_in_dim(ext_embed, start_j, BLOCK, 0)
            self_mask = (block_j == block_count + block_i) & diagonal
            energy_blk, charge_blk = pair_terms(pos_i, pos_j, embed_i, embed_j, self_mask, w_radial, w_hidden, w_charge, w_energy)
            energy_acc = lax.dynamic_update_slice_in_dim(energy_acc, lax.dynamic_slice_in_dim(energy_acc, start_i, BLOCK, 0) + energy_blk, start_i, 0)
            charge_acc = lax.dynamic_update_slice_in_dim(charge_acc, lax.dynamic_slice_in_dim(charge_acc, start_i, BLOCK, 0) + charge_blk, start_i, 0)
            return (energy_acc, charge_acc)
        blank_row = jnp.zeros((A_DEV,), jnp.float32)
        return lax.fori_loop(jnp.int32(0), counts[device], visit_slot, (blank_row, blank_row))
    energies, charges = lax.map(one_device, jnp.arange(device_count, dtype=jnp.int32))
    energies = energies.reshape(-1)
    charges = charges.reshape(-1)
    weights_x = spline_weights(offsets[0])
    weights_y = spline_weights(offsets[1])
    weights_z = spline_weights(offsets[2])
    slopes_x = spline_slopes(offsets[0])
    slopes_y = spline_slopes(offsets[1])
    slopes_z = spline_slopes(offsets[2])
    index_lists = []
    value_lists = []
    for step_x in range(3):
        for step_y in range(3):
            for step_z in range(3):
                point_x = (cell_index[0] + (step_x - 1)) % G
                point_y = (cell_index[1] + (step_y - 1)) % G
                point_z = (cell_index[2] + (step_z - 1)) % G
                index_lists.append((point_x, point_y, point_z))
                value_lists.append(weights_x[step_x] * weights_y[step_y] * weights_z[step_z] * charges)
    all_x = jnp.concatenate([entry[0] for entry in index_lists])
    all_y = jnp.concatenate([entry[1] for entry in index_lists])
    all_z = jnp.concatenate([entry[2] for entry in index_lists])
    density = background.at[all_x, all_y, all_z].add(jnp.concatenate(value_lists))
    frequency = jnp.arange(G, dtype=jnp.int32)
    green_vals = green_table(frequency[:, None, None], frequency[None, :, None], frequency[None, None, :])
    potential_grid = jnp.real(jnp.fft.ifftn(jnp.fft.fftn(density) * green_vals)).astype(jnp.float32)
    potential = jnp.zeros_like(charges)
    grad_x = jnp.zeros_like(charges)
    grad_y = jnp.zeros_like(charges)
    grad_z = jnp.zeros_like(charges)
    counter = 0
    for step_x in range(3):
        for step_y in range(3):
            for step_z in range(3):
                point_x, point_y, point_z = index_lists[counter]
                counter = counter + 1
                sampled = potential_grid[point_x, point_y, point_z]
                potential = potential + weights_x[step_x] * weights_y[step_y] * weights_z[step_z] * sampled
                grad_x = grad_x + slopes_x[step_x] * weights_y[step_y] * weights_z[step_z] * sampled
                grad_y = grad_y + weights_x[step_x] * slopes_y[step_y] * weights_z[step_z] * sampled
                grad_z = grad_z + weights_x[step_x] * weights_y[step_y] * slopes_z[step_z] * sampled
    electric_field = -jnp.stack([grad_x, grad_y, grad_z], axis=0)
    site_energy = energies + 0.5 * charges * potential
    return (site_energy, electric_field, charges)
```

```python
import functools
import math

import jax
import jax.numpy as jnp
import ml_dtypes
import numpy as np
from jax import lax
from jax.experimental import pallas as pl
from jax.experimental.pallas import tpu as pltpu
from jax.sharding import PartitionSpec as P

G = 256
NBASIS = 8
NSPEC = 8
BLOCK = 128
TILES_Y = 4
CUTOFF = 6.0
EWALD = 1.0
VMEM_BYTES = 56 << 20
KC = 16
PL = BLOCK // KC

BF = jnp.bfloat16
F32 = jnp.float32


def np_split(table):
    table = np.asarray(table, np.float32)
    high = table.astype(ml_dtypes.bfloat16)
    low = (table - high.astype(np.float32)).astype(ml_dtypes.bfloat16)
    return high, low


def hartley(points):
    phase = (np.arange(G)[:, None] * np.asarray(points)[None, :]) % G
    angle = phase.astype(np.float64) * (2.0 * math.pi / G)
    return np.cos(angle) + np.sin(angle)


def split2(x):
    high = x.astype(BF)
    low = (x - high.astype(F32)).astype(BF)
    return high, low


def dot_nn(a, b):
    return lax.dot_general(a, b, (((1,), (0,)), ((), ())), preferred_element_type=F32)


def dot_nt(a, b):
    return lax.dot_general(a, b, (((1,), (1,)), ((), ())), preferred_element_type=F32)


def dot3(dot, a, b):
    return dot(a[0], b[0]) + (dot(a[0], b[1]) + dot(a[1], b[0]))


def split3(x):
    one = x.astype(BF).astype(F32)
    two = (x - one).astype(BF).astype(F32)
    three = (x - one - two).astype(BF).astype(F32)
    return one, two, three


def pair_kernel(
    slots,
    live,
    left,
    own,
    right,
    radial_w,
    kind_i_w,
    kind_j_w,
    hidden_w,
    charge_w,
    energy_w,
    energy,
    charge,
    ext,
    wcat,
    whid,
    rank_s,
    theta_s,
    env_s,
    kind_s,
    *,
    step,
):
    blocks = energy.shape[0]
    atoms = own.shape[1]
    energy[...] = jnp.zeros_like(energy)
    charge[...] = jnp.zeros_like(charge)
    ext[:, :atoms] = left[...]
    ext[:, atoms : 2 * atoms] = own[...]
    ext[:, 2 * atoms :] = right[...]
    width = hidden_w.shape[0]
    r1, r2, r3 = split3(radial_w[...])
    table = jnp.concatenate(
        [
            *(r1, r2, r3, r1, r2, r1),
            *split3(kind_j_w[...]),
            *split3(kind_i_w[...]),
            jnp.zeros((BLOCK - 12 * NBASIS, width), F32),
        ],
        axis=0,
    )
    wcat[...] = (0.5 * table).T.astype(BF)
    whid[...] = (0.5 * hidden_w[...].astype(F32)).T.astype(BF)
    wq = jnp.broadcast_to(charge_w[...].astype(F32), (16, width)).astype(BF)
    we = jnp.broadcast_to(energy_w[...].astype(F32), (16, width)).astype(BF)
    half = 0.5 * G
    row8 = lax.broadcasted_iota(jnp.int32, (NSPEC, BLOCK), 0).astype(F32)
    sub = lax.broadcasted_iota(jnp.int32, (BLOCK, BLOCK), 0)
    lane = lax.broadcasted_iota(jnp.int32, (BLOCK, BLOCK), 1)
    earlier = (lane < sub).astype(F32).astype(BF)
    spare = jnp.zeros((BLOCK - 12 * NBASIS, BLOCK), F32)

    def slot_body(slot, unused):
        bi = slots[slot, 0]
        bj = slots[slot, 1]
        ri = own[:, pl.ds(pl.multiple_of(bi * BLOCK, BLOCK), BLOCK)]
        rj = ext[:, pl.ds(pl.multiple_of(bj * BLOCK, BLOCK), BLOCK)]
        total = jnp.zeros((BLOCK, BLOCK), F32)
        for c in range(3):
            sep = jnp.broadcast_to(rj[c : c + 1, :], (BLOCK, BLOCK)).T - ri[c : c + 1, :]
            sep = jnp.where(sep > half, sep - G, jnp.where(sep < -half, sep + G, sep))
            total = total + sep * sep
        scaled = jnp.sqrt(total) / CUTOFF
        inside = 1.0 - scaled * scaled
        env = jnp.where(scaled < 1.0, inside * inside, 0.0)
        env = jnp.where((sub == lane) & (bj == blocks + bi), 0.0, env)
        used = (env > 0.0).astype(F32)
        rank_s[...] = jnp.where(env > 0.0, dot_nn(earlier, used.astype(BF)), -1.0)
        theta_s[...] = math.pi * jnp.minimum(scaled, 1.0)
        env_s[...] = env
        kind_s[...] = jnp.broadcast_to(rj[3:4, :], (BLOCK, BLOCK)).T
        most = jnp.max(jnp.sum(used, axis=0, keepdims=True)).astype(jnp.int32)
        kind_i = (row8 == ri[3:4, :]).astype(F32)

        def rows_body(it, sums):
            energy_sum, charge_sum = sums
            rank = rank_s[...]
            parts = []
            envs = []
            for k in range(step):
                pick = rank == (it * step + k).astype(F32)
                theta = jnp.sum(jnp.where(pick, theta_s[...], 0.0), axis=0, keepdims=True)
                kind = jnp.sum(jnp.where(pick, kind_s[...], 0.0), axis=0, keepdims=True)
                envs.append(jnp.sum(jnp.where(pick, env_s[...], 0.0), axis=0, keepdims=True))
                phase = theta * (row8 + 1.0)
                small = phase == 0.0
                rad = jnp.where(small, 1.0, jnp.sin(phase) / jnp.where(small, 1.0, phase))
                one, two, three = split3(rad)
                kind_j = (row8 == kind).astype(F32)
                parts.append(
                    jnp.concatenate(
                        [
                            *(one, one, one, two, two, three),
                            *(kind_j, kind_j, kind_j, kind_i, kind_i, kind_i),
                            spare,
                        ],
                        axis=0,
                    ).astype(BF)
                )
            feats = jnp.concatenate(parts, axis=1)
            h = dot_nn(wcat[...], feats)
            edge = (h + h * jnp.tanh(h)).astype(BF)
            cp = dot_nn(wq, edge)
            g = dot_nn(whid[...], edge)
            latent = (g + g * jnp.tanh(g)).astype(BF)
            ep = dot_nn(we, latent)
            for k in range(step):
                cut = slice(k * BLOCK, (k + 1) * BLOCK)
                charge_sum = charge_sum + envs[k] * cp[0:1, cut]
                energy_sum = energy_sum + envs[k] * ep[0:1, cut]
            return energy_sum, charge_sum

        zero = jnp.zeros((1, BLOCK), F32)
        energy_sum, charge_sum = lax.fori_loop(
            0, (most + step - 1) // step, rows_body, (zero, zero)
        )
        where = pl.ds(bi, 1)
        charge[where, :] = charge[where, :] + charge_sum
        energy[where, :] = energy[where, :] + energy_sum
        return unused

    lax.fori_loop(0, live[0], slot_body, 0)


def spline_rows(rows, first, center, frac, wrap, slopes):
    index = lax.broadcasted_iota(jnp.int32, (rows, frac.shape[1]), 0) + first
    if slopes:
        values = (frac - 0.5, -2.0 * frac, 0.5 + frac)
    else:
        values = ((0.5 - frac) * (0.5 - frac) * 0.5, 0.75 - frac * frac, (0.5 + frac) * (0.5 + frac) * 0.5)
    out = jnp.zeros((rows, frac.shape[1]), F32)
    for o in range(3):
        target = center + (o - 1)
        if wrap:
            target = jnp.where(target < 0, target + G, jnp.where(target >= G, target - G, target))
        out = jnp.where(index == target, values[o], out)
    return out


def chunk_blocks(blocks):
    per_tile = blocks // TILES_Y
    return [
        (t, [t + TILES_Y * z for z in range(2 * pair, 2 * pair + 2)])
        for t in range(TILES_Y)
        for pair in range(per_tile // 2)
    ]


def lanes_of(ref, row, pair):
    return jnp.concatenate([ref[row : row + 1, b * BLOCK : (b + 1) * BLOCK] for b in pair], axis=1)


def rows_of(ref, pair):
    return jnp.concatenate([ref[b : b + 1, :] for b in pair], axis=1)


def spread_kernel(local, frac, charge, back, hz_hi, hz_lo, out, acc):
    planes, padded_y, unused_z = acc.shape
    slab, quarter = back.shape[0], back.shape[1]
    window = 24
    tile = quarter // TILES_Y
    acc[...] = jnp.zeros_like(acc)
    acc[1 : slab + 1, 1 : quarter + 1, :] = back[...]
    for t, pair in chunk_blocks(charge.shape[0]):
        wx = spline_rows(planes, 0, lanes_of(local, 0, pair), lanes_of(frac, 0, pair), False, False)
        wy = spline_rows(window, tile * t, lanes_of(local, 1, pair), lanes_of(frac, 1, pair), False, False)
        wz = spline_rows(G, 0, lanes_of(local, 2, pair), lanes_of(frac, 2, pair), True, False)
        wy = wy * rows_of(charge, pair)
        mix = jnp.concatenate([wx[x : x + 1, :] * wy for x in range(planes)], axis=0)
        part = dot3(dot_nt, split2(mix), split2(wz))
        acc[:, tile * t : tile * t + window, :] += part.reshape(planes, window, G)
    table = (hz_hi[...], hz_lo[...])
    for q in range(planes // 2):
        two = split2(acc[2 * q : 2 * q + 2].reshape(2 * padded_y, G))
        out[2 * q : 2 * q + 2] = dot3(dot_nn, two, table).reshape(2, padded_y, G)


def swap_blocks(arrays):
    arrays = list(arrays)
    count = len(arrays)
    width = BLOCK // count
    lane = lax.broadcasted_iota(jnp.int32, arrays[0].shape, arrays[0].ndim - 1)
    bit = 1
    while bit < count:
        upper = (lane // (width * bit)) % 2 == 1
        for i in range(count):
            if i & bit:
                continue
            low, high = arrays[i], arrays[i | bit]
            arrays[i] = jnp.where(upper, pltpu.roll(high, width * bit, low.ndim - 1), low)
            arrays[i | bit] = jnp.where(upper, high, pltpu.roll(low, BLOCK - width * bit, low.ndim - 1))
        bit *= 2
    return arrays


def mesh_kernel(
    data,
    hy_hi,
    hy_lo,
    vy_hi,
    vy_lo,
    hx_hi,
    hx_lo,
    ix_hi,
    ix_lo,
    out,
    halo,
    s1,
    land1,
    ready2,
    land2,
    ready3,
    land3,
    ready4,
    land4,
    green_s,
    hsend,
    hrecv,
    send1,
    recv1,
    send2,
    recv2,
    send3,
    recv3,
    send4,
    recv4,
    loc1,
    loc2,
    loc3,
    loc4,
):
    groups, chunks, tiers, padded_y = s1.shape[:4]
    doms = lax.axis_size("dom")
    slab = tiers * PL
    width_y = G // doms
    lines = doms * tiers
    span = 2
    subs = [(lo, min(lo + span, tiers)) for lo in range(0, tiers, span)]
    me_g, me_d = lax.axis_index("grp"), lax.axis_index("dom")
    mesh_ids = pl.DeviceIdType.MESH
    barrier = pltpu.get_barrier_semaphore()
    order_g = sorted(range(1, groups), key=lambda k: abs(k - groups // 2))
    order_d = sorted(range(1, doms), key=lambda k: abs(k - doms // 2))
    for axis, me, order, count in (("grp", me_g, order_g, groups), ("dom", me_d, order_d, doms)):
        for k in order:
            pl.semaphore_signal(
                barrier, inc=1, device_id={axis: lax.rem(me + k, count)}, device_id_type=mesh_ids
            )
    pl.semaphore_wait(barrier, groups + doms - 2)

    def remote(src, dst, send_sem, recv_sem, axis, peer):
        copy = pltpu.make_async_remote_copy(
            src_ref=src,
            dst_ref=dst,
            send_sem=send_sem,
            recv_sem=recv_sem,
            device_id={axis: peer},
            device_id_type=mesh_ids,
        )
        copy.start()
        return copy

    def local(src, dst, sem):
        copy = pltpu.make_async_copy(src, dst, sem)
        copy.start()
        return copy

    left = lax.rem(me_d + doms - 1, doms)
    right = lax.rem(me_d + 1, doms)

    def edges(low, high, base):
        return [
            remote(low, halo.at[base], hsend.at[base], hrecv.at[base], "dom", left),
            remote(high, halo.at[base + 1], hsend.at[base + 1], hrecv.at[base + 1], "dom", right),
        ]

    pending = []
    border = edges(data.at[0], data.at[slab + 1], 0)
    pending += border

    def cut_tier(t):
        for h in range(2):
            cut = slice(h * BLOCK, (h + 1) * BLOCK)
            planes = []
            for p in range(PL):
                plane = data[1 + t * PL + p, :, cut]
                if t == 0 and p == 0:
                    plane = plane + halo[1, :, cut]
                if t == tiers - 1 and p == PL - 1:
                    plane = plane + halo[0, :, cut]
                planes.append(plane)
            for i, piece in enumerate(swap_blocks(planes)):
                n = h * PL + i
                s1[n // chunks, n % chunks, t] = piece

    for t in range(1, tiers - 1):
        cut_tier(t)
    for copy in border:
        copy.wait_recv()
    cut_tier(0)
    if tiers > 1:
        cut_tier(tiers - 1)

    first = {}
    for c in range(chunks):
        for n, (lo, hi) in enumerate(subs):
            part = pl.ds(lo, hi - lo)
            copies = []
            for k in order_g:
                peer = lax.rem(me_g + k, groups)
                copies.append(
                    remote(
                        s1.at[peer, c, part],
                        land1.at[me_g, c, part],
                        send1.at[c, n, k - 1],
                        recv1.at[c, n, k - 1],
                        "grp",
                        peer,
                    )
                )
            own = local(s1.at[me_g, c, part], land1.at[me_g, c, part], loc1.at[c, n])
            first[c, n] = (own, copies)
            pending += copies

    unit = 2.0 * math.pi / G * (2.0 * math.pi / G)
    shape = (G, 2 * BLOCK)

    def signed(m):
        return jnp.where(m < G // 2, m, m - G)

    mx = signed(lax.broadcasted_iota(jnp.int32, shape, 0))
    lanes = lax.broadcasted_iota(jnp.int32, shape, 1)

    def fill_green(c):
        mz = signed(me_g * (G // groups) + c * KC + lanes % KC)
        base_sq = mx * mx + mz * mz
        for two in range(width_y // (2 * PL)):
            my = signed(me_d * width_y + two * 2 * PL + lanes // KC)
            squares = base_sq + my * my
            wave = squares.astype(F32) * unit
            safe = jnp.where(squares > 0, wave, 1.0)
            green_s[c, two] = jnp.where(
                squares > 0, 4.0 * math.pi * jnp.exp(-wave / (4.0 * EWALD * EWALD)) / safe, 0.0
            ) * (1.0 / (G * G * G))

    def rows_at(d, t, count):
        return pl.ds(d * (tiers * width_y) + t * width_y, count * width_y)

    def exchange_dom(src, dst, c, lo, hi, n, send_sem, recv_sem, loc):
        copies = []
        for k in order_d:
            peer = lax.rem(me_d + k, doms)
            copies.append(
                remote(
                    src.at[c, rows_at(peer, lo, hi - lo)],
                    dst.at[c, rows_at(me_d, lo, hi - lo)],
                    send_sem.at[c, n, k - 1],
                    recv_sem.at[c, n, k - 1],
                    "dom",
                    peer,
                )
            )
        own = local(src.at[c, rows_at(me_d, lo, hi - lo)], dst.at[c, rows_at(me_d, lo, hi - lo)], loc.at[c, n])
        return own, copies

    def arrive(entry):
        own, copies = entry
        own.wait()
        for copy in copies:
            copy.wait_recv()

    forward_y = (hy_hi[...], hy_lo[...])
    second = {}

    def stage_y(c, n):
        lo, hi = subs[n]
        arrive(first[c, n])
        column = jnp.concatenate(
            [
                jnp.concatenate([land1[g, c, t] for g in range(groups)], axis=0)
                for t in range(lo, hi)
            ],
            axis=1,
        )
        result = dot3(dot_nn, forward_y, split2(column))
        for d in range(doms):
            for t in range(lo, hi):
                ready2[c, rows_at(d, t, 1)] = result[
                    d * width_y : (d + 1) * width_y, (t - lo) * BLOCK : (t - lo + 1) * BLOCK
                ]
        second[c, n] = exchange_dom(ready2, land2, c, lo, hi, n, send2, recv2, loc2)
        pending.extend(second[c, n][1])

    forward_x = (hx_hi[...], hx_lo[...])
    back_x = (ix_hi[...], ix_lo[...])
    third = {}

    def stage_x(c):
        for n in range(len(subs)):
            arrive(second[c, n])
        for two in range(width_y // (2 * PL)):
            parts = []
            for h in range(2):
                base = (2 * two + h) * PL
                lines_in = [land2[c, pl.ds(base + j, lines, stride=width_y), :] for j in range(PL)]
                parts.append(jnp.concatenate(swap_blocks(lines_in), axis=0))
            column = jnp.concatenate(parts, axis=1)
            spectrum = dot3(dot_nn, forward_x, split2(column)) * green_s[c, two]
            result = dot3(dot_nn, back_x, split2(spectrum))
            for h in range(2):
                base = (2 * two + h) * PL
                half = [
                    result[p * lines : (p + 1) * lines, h * BLOCK : (h + 1) * BLOCK] for p in range(PL)
                ]
                for j, piece in enumerate(swap_blocks(half)):
                    ready3[c, pl.ds(base + j, lines, stride=width_y), :] = piece
        for n, (lo, hi) in enumerate(subs):
            third[c, n] = exchange_dom(ready3, land3, c, lo, hi, n, send3, recv3, loc3)
            pending.extend(third[c, n][1])

    back_y = (vy_hi[...], vy_lo[...])
    fourth = {}

    def stage_v(c, n):
        lo, hi = subs[n]
        arrive(third[c, n])
        column = jnp.concatenate(
            [
                jnp.concatenate([land3[c, rows_at(d, t, 1)] for d in range(doms)], axis=0)
                for t in range(lo, hi)
            ],
            axis=1,
        )
        result = dot3(dot_nn, back_y, split2(column))
        for g in range(groups):
            for t in range(lo, hi):
                ready4[g, c, t] = result[
                    g * padded_y : (g + 1) * padded_y, (t - lo) * BLOCK : (t - lo + 1) * BLOCK
                ]
        part = pl.ds(lo, hi - lo)
        copies = []
        for k in order_g:
            peer = lax.rem(me_g + k, groups)
            copies.append(
                remote(
                    ready4.at[peer, c, part],
                    land4.at[me_g, c, part],
                    send4.at[c, n, k - 1],
                    recv4.at[c, n, k - 1],
                    "grp",
                    peer,
                )
            )
        own = local(ready4.at[me_g, c, part], land4.at[me_g, c, part], loc4.at[c, n])
        fourth[c, n] = (own, copies)
        pending.extend(copies)

    for c in range(chunks):
        for n in range(len(subs)):
            stage_y(c, n)
        fill_green(c)
    for c in range(chunks):
        stage_x(c)
    for c in range(chunks):
        for n in range(len(subs)):
            stage_v(c, n)
    for entry in fourth.values():
        arrive(entry)
    for t in range(tiers):
        for h in range(2):
            pieces = []
            for i in range(PL):
                n = h * PL + i
                pieces.append(land4[n // chunks, n % chunks, t])
            for p, plane in enumerate(swap_blocks(pieces)):
                out[1 + t * PL + p, :, h * BLOCK : (h + 1) * BLOCK] = plane
    border = edges(out.at[1], out.at[slab], 2)
    for copy in border:
        copy.wait_recv()
    pending += border
    out[0] = halo[3]
    out[slab + 1] = halo[2]
    for copy in pending:
        copy.wait_send()


def mesh_call(data, hy, vy, hx, ix, doms, groups):
    padded_y = data.shape[1]
    slab = data.shape[0] - 2
    tiers = slab // PL
    chunks = G // groups // KC
    width_y = G // doms
    subs = -(-tiers // 2)
    dma = pltpu.SemaphoreType.DMA
    grp_shape = pltpu.VMEM((groups, chunks, tiers, padded_y, BLOCK), F32)
    dom_shape = pltpu.VMEM((chunks, doms * tiers * width_y, BLOCK), F32)
    return pl.pallas_call(
        mesh_kernel,
        out_shape=jax.ShapeDtypeStruct(data.shape, F32),
        in_specs=[VMEM_SPEC] * 9,
        out_specs=VMEM_SPEC,
        scratch_shapes=[
            pltpu.VMEM((4, padded_y, G), F32),
            *[grp_shape] * 2,
            *[dom_shape] * 4,
            *[grp_shape] * 2,
            pltpu.VMEM((chunks, width_y // (2 * PL), G, 2 * BLOCK), F32),
            *[dma((4,))] * 2,
            *[dma((chunks, subs, groups - 1))] * 2,
            *[dma((chunks, subs, doms - 1))] * 4,
            *[dma((chunks, subs, groups - 1))] * 2,
            *[dma((chunks, subs))] * 4,
        ],
        compiler_params=pltpu.CompilerParams(
            vmem_limit_bytes=VMEM_BYTES, collective_id=0, has_side_effects=True
        ),
    )(data, *hy, *vy, *hx, *ix)


def sample_kernel(local, frac, charge, energy, data, hz_hi, hz_lo, site, field, mesh_s):
    planes, padded_y, unused_z = mesh_s.shape
    window = 24
    tile = (padded_y - 8) // TILES_Y
    table = (hz_hi[...], hz_lo[...])
    for q in range(planes // 2):
        two = split2(data[2 * q : 2 * q + 2].reshape(2 * padded_y, G))
        mesh_s[2 * q : 2 * q + 2] = dot3(dot_nn, two, table).reshape(2, padded_y, G)
    for t, pair in chunk_blocks(charge.shape[0]):
        lx, fx = lanes_of(local, 0, pair), lanes_of(frac, 0, pair)
        ly, fy = lanes_of(local, 1, pair), lanes_of(frac, 1, pair)
        lz, fz = lanes_of(local, 2, pair), lanes_of(frac, 2, pair)
        wx = spline_rows(planes, 0, lx, fx, False, False)
        sx = spline_rows(planes, 0, lx, fx, False, True)
        wy = spline_rows(window, tile * t, ly, fy, False, False)
        sy = spline_rows(window, tile * t, ly, fy, False, True)
        wz = spline_rows(G, 0, lz, fz, True, False)
        sz = spline_rows(G, 0, lz, fz, True, True)
        strip = split2(mesh_s[:, tile * t : tile * t + window, :].reshape(planes * window, G))
        along = dot3(dot_nn, strip, split2(wz))
        slope = dot3(dot_nn, strip, split2(sz))
        value_y = jnp.zeros_like(wy)
        grad_y = jnp.zeros_like(wy)
        slope_y = jnp.zeros_like(wy)
        for x in range(planes):
            here = along[x * window : (x + 1) * window]
            value_y = value_y + wx[x : x + 1] * here
            grad_y = grad_y + sx[x : x + 1] * here
            slope_y = slope_y + wx[x : x + 1] * slope[x * window : (x + 1) * window]
        pot = jnp.sum(wy * value_y, axis=0, keepdims=True)
        rows = [
            -jnp.sum(wy * grad_y, axis=0, keepdims=True),
            -jnp.sum(sy * value_y, axis=0, keepdims=True),
            -jnp.sum(wy * slope_y, axis=0, keepdims=True),
        ]
        result = rows_of(energy, pair) + 0.5 * rows_of(charge, pair) * pot
        for k, b in enumerate(pair):
            cut = slice(k * BLOCK, (k + 1) * BLOCK)
            site[b : b + 1, :] = result[:, cut]
            for c in range(3):
                field[c : c + 1, b * BLOCK : (b + 1) * BLOCK] = rows[c][:, cut]


VMEM_SPEC = pl.BlockSpec(memory_space=pltpu.VMEM)
SMEM_SPEC = pl.BlockSpec(memory_space=pltpu.SMEM)


def call(body, outs, scratch, scalars, args):
    specs = [SMEM_SPEC] * scalars + [VMEM_SPEC] * (len(args) - scalars)
    many = isinstance(outs, (list, tuple))
    return pl.pallas_call(
        body,
        out_shape=outs,
        in_specs=specs,
        out_specs=[VMEM_SPEC] * len(outs) if many else VMEM_SPEC,
        scratch_shapes=scratch,
        compiler_params=pltpu.CompilerParams(vmem_limit_bytes=VMEM_BYTES),
    )(*args)


def pair_call(
    pair_blocks, counts, left, record, right, species_embed, neighbour_embed, w_radial, w_hidden, w_charge, w_energy
):
    blocks = record.shape[1] // BLOCK
    width = w_charge.shape[0]
    shape = jax.ShapeDtypeStruct((blocks, BLOCK), F32)
    square = pltpu.VMEM((BLOCK, BLOCK), F32)
    return call(
        functools.partial(pair_kernel, step=4),
        [shape, shape],
        [
            pltpu.VMEM((record.shape[0], 3 * record.shape[1]), F32),
            pltpu.VMEM((width, BLOCK), BF),
            pltpu.VMEM((width, width), BF),
            *[square] * 4,
        ],
        2,
        (
            pair_blocks,
            counts,
            left,
            record,
            right,
            w_radial,
            species_embed,
            neighbour_embed,
            w_hidden,
            w_charge[None, :],
            w_energy[None, :],
        ),
    )


def tables(slab, quarter, doms, groups, padded_y):
    plain = hartley(np.arange(G))
    y_points = np.array([quarter * g - 1 + r for g in range(groups) for r in range(padded_y)]) % G
    y_used = np.array([r < quarter + 2 for g in range(groups) for r in range(padded_y)])
    hy = hartley(y_points) * y_used[None, :]
    x_points = np.array([slab * d + PL * t + p for p in range(PL) for d in range(doms) for t in range(slab // PL)])
    hx = hartley(x_points)
    return [np_split(t) for t in (plain, hy, hy.T, hx, hx.T)]


def on_device(
    cell_index,
    offsets,
    species,
    pair_blocks,
    counts,
    background,
    species_embed,
    neighbour_embed,
    w_radial,
    w_hidden,
    w_charge,
    w_energy,
):
    atoms = cell_index.shape[1]
    blocks = atoms // BLOCK
    doms = lax.axis_size("dom")
    groups = lax.axis_size("grp")
    slab = G // doms
    quarter = G // groups
    planes = slab + 2
    padded_y = quarter + 8
    dom_id = lax.axis_index("dom")
    grp_id = lax.axis_index("grp")
    hz, hy, hy_inv, hx, hx_inv = tables(slab, quarter, doms, groups, padded_y)

    positions = cell_index.astype(F32) + offsets
    record = jnp.concatenate([positions, species.astype(F32)[None, :]], axis=0)
    left = lax.ppermute(record, "dom", [(i, (i + 1) % doms) for i in range(doms)])
    right = lax.ppermute(record, "dom", [((i + 1) % doms, i) for i in range(doms)])
    energies, charges = pair_call(
        pair_blocks,
        counts,
        left,
        record,
        right,
        species_embed,
        neighbour_embed,
        w_radial,
        w_hidden,
        w_charge,
        w_energy,
    )

    origin = jnp.stack([1 - slab * dom_id, 1 - quarter * grp_id, jnp.zeros_like(dom_id)])
    local = cell_index + origin[:, None]
    spec = call(
        spread_kernel,
        jax.ShapeDtypeStruct((planes, padded_y, G), F32),
        [pltpu.VMEM((planes, padded_y, G), F32)],
        0,
        (local, offsets, charges, background, *hz),
    )
    spec = mesh_call(spec, hy, hy_inv, hx, hx_inv, doms, groups)
    site, field = call(
        sample_kernel,
        [jax.ShapeDtypeStruct((blocks, BLOCK), F32), jax.ShapeDtypeStruct((3, atoms), F32)],
        [pltpu.VMEM((planes, padded_y, G), F32)],
        0,
        (local, offsets, charges, energies, spec, *hz),
    )
    return (site.reshape(atoms), field, charges.reshape(atoms))


def solution(mesh):
    return jax.shard_map(
        on_device,
        mesh=mesh,
        in_specs=(
            P(None, ("grp", "dom")),
            P(None, ("grp", "dom")),
            P(("grp", "dom")),
            P(("grp", "dom"), None),
            P(("grp", "dom")),
            P("dom", "grp", None),
            P(),
            P(),
            P(),
            P(),
            P(),
            P(),
        ),
        out_specs=(P(("grp", "dom")), P(None, ("grp", "dom")), P(("grp", "dom"))),
        check_vma=False,
    )
```

```python
import functools
import math

import jax
import jax.numpy as jnp
import ml_dtypes
import numpy as np
from jax import lax
from jax.experimental import pallas as pl
from jax.experimental.pallas import tpu as pltpu
from jax.sharding import PartitionSpec as P

G = 256
NBASIS = 8
NSPEC = 8
BLOCK = 128
TILES_Y = 4
CUTOFF = 6.0
EWALD = 1.0
VMEM_BYTES = 56 << 20
KC = 16
PL = BLOCK // KC

BF = jnp.bfloat16
F32 = jnp.float32


def np_split(table):
    table = np.asarray(table, np.float32)
    high = table.astype(ml_dtypes.bfloat16)
    low = (table - high.astype(np.float32)).astype(ml_dtypes.bfloat16)
    return high, low


def hartley(points):
    phase = (np.arange(G)[:, None] * np.asarray(points)[None, :]) % G
    angle = phase.astype(np.float64) * (2.0 * math.pi / G)
    return np.cos(angle) + np.sin(angle)


def split2(x):
    high = x.astype(BF)
    low = (x - high.astype(F32)).astype(BF)
    return high, low


def dot_nn(a, b):
    return lax.dot_general(a, b, (((1,), (0,)), ((), ())), preferred_element_type=F32)


def dot_nt(a, b):
    return lax.dot_general(a, b, (((1,), (1,)), ((), ())), preferred_element_type=F32)


def dot3(dot, a, b):
    return dot(a[0], b[0]) + (dot(a[0], b[1]) + dot(a[1], b[0]))


def split3(x):
    one = x.astype(BF).astype(F32)
    two = (x - one).astype(BF).astype(F32)
    three = (x - one - two).astype(BF).astype(F32)
    return one, two, three


def pair_kernel(
    slots,
    live,
    left,
    own,
    right,
    radial_w,
    kind_i_w,
    kind_j_w,
    hidden_w,
    readout_w,
    energy,
    charge,
    ext,
    wcat,
    whid,
    rank_s,
    theta_s,
    env_s,
    kind_s,
    *,
    step,
):
    blocks = energy.shape[0]
    atoms = own.shape[1]
    energy[...] = jnp.zeros_like(energy)
    charge[...] = jnp.zeros_like(charge)
    ext[:, :atoms] = left[...]
    ext[:, atoms : 2 * atoms] = own[...]
    ext[:, 2 * atoms :] = right[...]
    width = hidden_w.shape[0]
    r1, r2, r3 = split3(radial_w[...])
    table = jnp.concatenate(
        [
            *(r1, r2, r3, r1, r2, r1),
            *split3(kind_j_w[...]),
            *split3(kind_i_w[...]),
            jnp.zeros((BLOCK - 12 * NBASIS, width), F32),
        ],
        axis=0,
    )
    wcat[...] = (0.5 * table).T.astype(BF)
    whid[...] = (0.5 * hidden_w[...].astype(F32)).T.astype(BF)
    wq = jnp.broadcast_to(readout_w[0:1, :], (16, width)).astype(BF)
    we = jnp.broadcast_to(readout_w[1:2, :], (16, width)).astype(BF)
    half = 0.5 * G
    row8 = lax.broadcasted_iota(jnp.int32, (NSPEC, BLOCK), 0).astype(F32)
    sub = lax.broadcasted_iota(jnp.int32, (BLOCK, BLOCK), 0)
    lane = lax.broadcasted_iota(jnp.int32, (BLOCK, BLOCK), 1)
    earlier = (lane < sub).astype(F32).astype(BF)
    spare = jnp.zeros((BLOCK - 12 * NBASIS, BLOCK), F32)

    def slot_body(slot, unused):
        bi = slots[0, slot]
        bj = slots[1, slot]
        ri = own[:, pl.ds(pl.multiple_of(bi * BLOCK, BLOCK), BLOCK)]
        rj = ext[:, pl.ds(pl.multiple_of(bj * BLOCK, BLOCK), BLOCK)]
        total = jnp.zeros((BLOCK, BLOCK), F32)
        for c in range(3):
            sep = jnp.broadcast_to(rj[c : c + 1, :], (BLOCK, BLOCK)).T - ri[c : c + 1, :]
            sep = jnp.where(sep > half, sep - G, jnp.where(sep < -half, sep + G, sep))
            total = total + sep * sep
        scaled = jnp.sqrt(total) / CUTOFF
        inside = 1.0 - scaled * scaled
        env = jnp.where(scaled < 1.0, inside * inside, 0.0)
        env = jnp.where((sub == lane) & (bj == blocks + bi), 0.0, env)
        used = (env > 0.0).astype(F32)
        rank_s[...] = jnp.where(env > 0.0, dot_nn(earlier, used.astype(BF)), -1.0)
        theta_s[...] = math.pi * jnp.minimum(scaled, 1.0)
        env_s[...] = env
        kind_s[...] = jnp.broadcast_to(rj[3:4, :], (BLOCK, BLOCK)).T
        most = jnp.max(jnp.sum(used, axis=0, keepdims=True)).astype(jnp.int32)
        kind_i = (row8 == ri[3:4, :]).astype(F32)

        def rows_body(it, sums):
            energy_sum, charge_sum = sums
            rank = rank_s[...]
            parts = []
            envs = []
            for k in range(step):
                pick = rank == (it * step + k).astype(F32)
                theta = jnp.sum(jnp.where(pick, theta_s[...], 0.0), axis=0, keepdims=True)
                kind = jnp.sum(jnp.where(pick, kind_s[...], 0.0), axis=0, keepdims=True)
                envs.append(jnp.sum(jnp.where(pick, env_s[...], 0.0), axis=0, keepdims=True))
                phase = theta * (row8 + 1.0)
                small = phase == 0.0
                rad = jnp.where(small, 1.0, jnp.sin(phase) / jnp.where(small, 1.0, phase))
                one, two, three = split3(rad)
                kind_j = (row8 == kind).astype(F32)
                parts.append(
                    jnp.concatenate(
                        [
                            *(one, one, one, two, two, three),
                            *(kind_j, kind_j, kind_j, kind_i, kind_i, kind_i),
                            spare,
                        ],
                        axis=0,
                    ).astype(BF)
                )
            feats = jnp.concatenate(parts, axis=1)
            h = dot_nn(wcat[...], feats)
            edge = (h + h * jnp.tanh(h)).astype(BF)
            cp = dot_nn(wq, edge)
            g = dot_nn(whid[...], edge)
            latent = (g + g * jnp.tanh(g)).astype(BF)
            ep = dot_nn(we, latent)
            for k in range(step):
                cut = slice(k * BLOCK, (k + 1) * BLOCK)
                charge_sum = charge_sum + envs[k] * cp[0:1, cut]
                energy_sum = energy_sum + envs[k] * ep[0:1, cut]
            return energy_sum, charge_sum

        zero = jnp.zeros((1, BLOCK), F32)
        energy_sum, charge_sum = lax.fori_loop(
            0, (most + step - 1) // step, rows_body, (zero, zero)
        )
        where = pl.ds(bi, 1)
        charge[where, :] = charge[where, :] + charge_sum
        energy[where, :] = energy[where, :] + energy_sum
        return unused

    lax.fori_loop(0, live[0], slot_body, 0)


def spline_rows(rows, first, center, frac, wrap, slopes):
    index = lax.broadcasted_iota(jnp.int32, (rows, frac.shape[1]), 0) + first
    if slopes:
        values = (frac - 0.5, -2.0 * frac, 0.5 + frac)
    else:
        values = ((0.5 - frac) * (0.5 - frac) * 0.5, 0.75 - frac * frac, (0.5 + frac) * (0.5 + frac) * 0.5)
    out = jnp.zeros((rows, frac.shape[1]), F32)
    for o in range(3):
        target = center + (o - 1)
        if wrap:
            target = jnp.where(target < 0, target + G, jnp.where(target >= G, target - G, target))
        out = jnp.where(index == target, values[o], out)
    return out


def chunk_blocks(blocks):
    per_tile = blocks // TILES_Y
    return [
        (t, [t + TILES_Y * z for z in range(2 * pair, 2 * pair + 2)])
        for t in range(TILES_Y)
        for pair in range(per_tile // 2)
    ]


def lanes_of(ref, row, pair):
    return jnp.concatenate([ref[row : row + 1, b * BLOCK : (b + 1) * BLOCK] for b in pair], axis=1)


def rows_of(ref, pair):
    return jnp.concatenate([ref[b : b + 1, :] for b in pair], axis=1)


def swap_blocks(arrays):
    arrays = list(arrays)
    count = len(arrays)
    width = BLOCK // count
    lane = lax.broadcasted_iota(jnp.int32, arrays[0].shape, arrays[0].ndim - 1)
    bit = 1
    while bit < count:
        upper = (lane // (width * bit)) % 2 == 1
        for i in range(count):
            if i & bit:
                continue
            low, high = arrays[i], arrays[i | bit]
            arrays[i] = jnp.where(upper, pltpu.roll(high, width * bit, low.ndim - 1), low)
            arrays[i | bit] = jnp.where(upper, high, pltpu.roll(low, BLOCK - width * bit, low.ndim - 1))
        bit *= 2
    return arrays


def tier_order(tiers):
    return list(range(1, tiers - 1)) + [0, tiers - 1]


def tier_cuts(tiers):
    return [cut for cut in ((0, tiers - 2), (tiers - 2, tiers)) if cut[0] < cut[1]]


def mesh_kernel(
    cell,
    frac,
    charge,
    energy,
    back,
    hz_hi,
    hz_lo,
    tz_hi,
    tz_lo,
    hy_hi,
    hy_lo,
    vy_hi,
    vy_lo,
    hx_hi,
    hx_lo,
    ix_hi,
    ix_lo,
    site,
    field,
    acc,
    halo,
    s1,
    land1,
    ready2,
    land2,
    ready3,
    land3,
    ready4,
    land4,
    green_s,
    weight_s,
    side_s,
    part_s,
    mesh_s,
    hsend,
    hrecv,
    send1,
    recv1,
    send2,
    recv2,
    send3,
    recv3,
    send4,
    recv4,
    loc1,
    loc2,
    loc3,
    loc4,
):
    groups, chunks, tiers, padded_y = s1.shape[:4]
    doms = lax.axis_size("dom")
    slab = tiers * PL
    planes = slab + 2
    quarter = G // groups
    tile = quarter // TILES_Y
    window = 24
    width_y = G // doms
    lines = doms * tiers
    order = tier_order(tiers)
    subs = tier_cuts(tiers)
    last = len(subs) - 1
    per_half = PL // groups
    me_g, me_d = lax.axis_index("grp"), lax.axis_index("dom")
    mesh_ids = pl.DeviceIdType.MESH
    barrier = pltpu.get_barrier_semaphore()
    order_g = sorted(range(1, groups), key=lambda k: abs(k - groups // 2))
    order_d = sorted(range(1, doms), key=lambda k: abs(k - doms // 2))
    for axis, me, peers, count in (("grp", me_g, order_g, groups), ("dom", me_d, order_d, doms)):
        for k in peers:
            pl.semaphore_signal(
                barrier, inc=1, device_id={axis: lax.rem(me + k, count)}, device_id_type=mesh_ids
            )

    def remote(src, dst, send_sem, recv_sem, axis, peer):
        copy = pltpu.make_async_remote_copy(
            src_ref=src,
            dst_ref=dst,
            send_sem=send_sem,
            recv_sem=recv_sem,
            device_id={axis: peer},
            device_id_type=mesh_ids,
        )
        copy.start()
        return copy

    def local_copy(src, dst, sem):
        copy = pltpu.make_async_copy(src, dst, sem)
        copy.start()
        return copy

    def arrive(entry):
        own, copies = entry
        own.wait()
        for copy in copies:
            copy.wait_recv()

    pending = []
    left = lax.rem(me_d + doms - 1, doms)
    right = lax.rem(me_d + 1, doms)
    offset_x = 1 - slab * me_d
    offset_y = 1 - quarter * me_g
    atom_chunks = chunk_blocks(charge.shape[0])

    def atoms_of(m):
        t, pair = atom_chunks[m]
        local = [
            lanes_of(cell, 0, pair) + offset_x,
            lanes_of(cell, 1, pair) + offset_y,
            lanes_of(cell, 2, pair),
        ]
        return t, pair, local, [lanes_of(frac, axis, pair) for axis in range(3)]

    acc[...] = jnp.zeros_like(acc)
    acc[1 : slab + 1, 1 : quarter + 1, :] = back[...]
    for m in range(len(atom_chunks)):
        t, pair, local, f = atoms_of(m)
        wx = spline_rows(planes, 0, local[0], f[0], False, False)
        wy = spline_rows(window, tile * t, local[1], f[1], False, False)
        wz = spline_rows(G, 0, local[2], f[2], True, False)
        wy = wy * rows_of(charge, pair)
        mix = jnp.concatenate([wx[x : x + 1, :] * wy for x in range(planes)], axis=0)
        part = dot3(dot_nt, split2(mix), split2(wz))
        acc[:, tile * t : tile * t + window, :] += part.reshape(planes, window, G)

    pl.semaphore_wait(barrier, groups + doms - 2)
    border = [
        remote(acc.at[0], halo.at[0], hsend.at[0], hrecv.at[0], "dom", left),
        remote(acc.at[slab + 1], halo.at[1], hsend.at[1], hrecv.at[1], "dom", right),
    ]
    pending += border
    forward_z = (hz_hi[...], hz_lo[...])

    def cut_tier(pos):
        base = 1 + order[pos] * PL
        rows = acc[base : base + PL].reshape(PL * padded_y, G)
        spec = dot3(dot_nn, split2(rows), forward_z)
        for h in range(2):
            cut = slice(h * BLOCK, (h + 1) * BLOCK)
            pieces = swap_blocks([spec[p * padded_y : (p + 1) * padded_y, cut] for p in range(PL)])
            for i, piece in enumerate(pieces):
                s1[i % groups, h * per_half + i // groups, pos] = piece

    def exchange_grp(src, dst, c, n, send_sem, recv_sem, loc):
        lo, hi = subs[n]
        part = pl.ds(lo, hi - lo)
        copies = []
        for k in order_g:
            peer = lax.rem(me_g + k, groups)
            copies.append(
                remote(
                    src.at[peer, c, part],
                    dst.at[me_g, c, part],
                    send_sem.at[c, n, k - 1],
                    recv_sem.at[c, n, k - 1],
                    "grp",
                    peer,
                )
            )
        pending.extend(copies)
        return local_copy(src.at[me_g, c, part], dst.at[me_g, c, part], loc.at[c, n]), copies

    first = {}
    for n, (lo, hi) in enumerate(subs):
        if n == last:
            for copy in border:
                copy.wait_recv()
            acc[1] = acc[1] + halo[1]
            acc[slab] = acc[slab] + halo[0]
        for pos in range(lo, hi):
            cut_tier(pos)
        first[0, n] = exchange_grp(s1, land1, 0, n, send1, recv1, loc1)
    for c in range(1, chunks):
        for n in range(len(subs)):
            first[c, n] = exchange_grp(s1, land1, c, n, send1, recv1, loc1)

    unit = 2.0 * math.pi / G * (2.0 * math.pi / G)
    shape = (G, 2 * BLOCK)

    def signed(m):
        return jnp.where(m < G // 2, m, m - G)

    mx = signed(lax.broadcasted_iota(jnp.int32, shape, 0))
    lanes = lax.broadcasted_iota(jnp.int32, shape, 1)

    def fill_green(c):
        mz = signed(me_g * (G // groups) + c * KC + lanes % KC)
        base_sq = mx * mx + mz * mz
        for two in range(width_y // (2 * PL)):
            my = signed(me_d * width_y + two * 2 * PL + lanes // KC)
            squares = base_sq + my * my
            wave = squares.astype(F32) * unit
            safe = jnp.where(squares > 0, wave, 1.0)
            green_s[c, two] = jnp.where(
                squares > 0, 4.0 * math.pi * jnp.exp(-wave / (4.0 * EWALD * EWALD)) / safe, 0.0
            ) * (1.0 / (G * G * G))

    def fill_weights(m):
        t, pair, local, f = atoms_of(m)
        table = (tz_hi[...], tz_lo[...])
        for kind in range(2):
            wz = spline_rows(G, 0, local[2], f[2], True, kind == 1)
            high, low = split2(dot3(dot_nn, table, split2(wz)))
            weight_s[m, kind, 0] = high
            weight_s[m, kind, 1] = low
        rows = side_s.shape[1] // 2 - window
        for kind in range(2):
            base = kind * (rows + window)
            side_s[m, base : base + rows] = spline_rows(rows, 0, local[0], f[0], False, kind == 1)
            side_s[m, base + rows : base + rows + window] = spline_rows(
                window, tile * t, local[1], f[1], False, kind == 1
            )

    def rows_at(d, pos, count):
        return pl.ds(d * (tiers * width_y) + pos * width_y, count * width_y)

    def exchange_dom(src, dst, c, n, send_sem, recv_sem, loc):
        lo, hi = subs[n]
        copies = []
        for k in order_d:
            peer = lax.rem(me_d + k, doms)
            copies.append(
                remote(
                    src.at[c, rows_at(peer, lo, hi - lo)],
                    dst.at[c, rows_at(me_d, lo, hi - lo)],
                    send_sem.at[c, n, k - 1],
                    recv_sem.at[c, n, k - 1],
                    "dom",
                    peer,
                )
            )
        pending.extend(copies)
        mine = rows_at(me_d, lo, hi - lo)
        return local_copy(src.at[c, mine], dst.at[c, mine], loc.at[c, n]), copies

    forward_y = (hy_hi[...], hy_lo[...])
    second = {}

    def stage_y(c, n):
        lo, hi = subs[n]
        arrive(first[c, n])
        column = jnp.concatenate(
            [
                jnp.concatenate([land1[g, c, t] for g in range(groups)], axis=0)
                for t in range(lo, hi)
            ],
            axis=1,
        )
        result = dot3(dot_nn, forward_y, split2(column))
        for d in range(doms):
            for t in range(lo, hi):
                ready2[c, rows_at(d, t, 1)] = result[
                    d * width_y : (d + 1) * width_y, (t - lo) * BLOCK : (t - lo + 1) * BLOCK
                ]
        second[c, n] = exchange_dom(ready2, land2, c, n, send2, recv2, loc2)

    forward_x = (hx_hi[...], hx_lo[...])
    back_x = (ix_hi[...], ix_lo[...])
    third = {}

    def stage_x(c):
        for n in range(len(subs)):
            arrive(second[c, n])
        for two in range(width_y // (2 * PL)):
            parts = []
            for h in range(2):
                base = (2 * two + h) * PL
                lines_in = [land2[c, pl.ds(base + j, lines, stride=width_y), :] for j in range(PL)]
                parts.append(jnp.concatenate(swap_blocks(lines_in), axis=0))
            column = jnp.concatenate(parts, axis=1)
            spectrum = dot3(dot_nn, forward_x, split2(column)) * green_s[c, two]
            result = dot3(dot_nn, back_x, split2(spectrum))
            for h in range(2):
                base = (2 * two + h) * PL
                half = [
                    result[p * lines : (p + 1) * lines, h * BLOCK : (h + 1) * BLOCK] for p in range(PL)
                ]
                for j, piece in enumerate(swap_blocks(half)):
                    ready3[c, pl.ds(base + j, lines, stride=width_y), :] = piece
        for n in reversed(range(len(subs))):
            third[c, n] = exchange_dom(ready3, land3, c, n, send3, recv3, loc3)

    back_y = (vy_hi[...], vy_lo[...])
    fourth = {}

    def stage_v(c, n):
        lo, hi = subs[n]
        arrive(third[c, n])
        column = jnp.concatenate(
            [
                jnp.concatenate([land3[c, rows_at(d, t, 1)] for d in range(doms)], axis=0)
                for t in range(lo, hi)
            ],
            axis=1,
        )
        result = dot3(dot_nn, back_y, split2(column))
        for g in range(groups):
            for t in range(lo, hi):
                ready4[g, c, t] = result[
                    g * padded_y : (g + 1) * padded_y, (t - lo) * BLOCK : (t - lo + 1) * BLOCK
                ]
        fourth[c, n] = exchange_grp(ready4, land4, c, n, send4, recv4, loc4)

    edges = {}

    def gather(h, n):
        lo, hi = subs[n]
        for c in range(h * per_half, (h + 1) * per_half):
            arrive(fourth[c, n])
        for pos in range(lo, hi):
            pieces = [land4[i % groups, h * per_half + i // groups, pos] for i in range(PL)]
            for p, plane in enumerate(swap_blocks(pieces)):
                mesh_s[h, 1 + order[pos] * PL + p] = plane
        if n == last:
            a, b = 2 + 2 * h, 3 + 2 * h
            edges[h] = [
                remote(mesh_s.at[h, 1], mesh_s.at[h, slab + 1], hsend.at[a], hrecv.at[a], "dom", left),
                remote(mesh_s.at[h, slab], mesh_s.at[h, 0], hsend.at[b], hrecv.at[b], "dom", right),
            ]
            pending.extend(edges[h])

    def sample(h):
        for copy in edges[h]:
            copy.wait_recv()
        rows = side_s.shape[1] // 2 - window
        half = slice(h * BLOCK, (h + 1) * BLOCK)
        for m in range(len(atom_chunks)):
            t, pair = atom_chunks[m]
            if m == 0 or t != atom_chunks[m - 1][0]:
                strip = mesh_s[h, :, tile * t : tile * t + window, :].reshape(planes * window, BLOCK)
                strip = jnp.concatenate(split2(strip), axis=1)

            def along(kind):
                high, low = weight_s[m, kind, 0, half], weight_s[m, kind, 1, half]
                return dot_nn(strip, jnp.concatenate([high, high], axis=0)) + dot_nn(
                    strip, jnp.concatenate([low, low], axis=0)
                )

            wx, wy = side_s[m, :rows], side_s[m, rows : rows + window]
            sx, sy = side_s[m, rows + window : 2 * rows + window], side_s[m, 2 * rows + window :]
            value, slope = along(0), along(1)
            value_y = jnp.zeros_like(wy)
            grad_y = jnp.zeros_like(wy)
            slope_y = jnp.zeros_like(wy)
            for x in range(planes):
                here = value[x * window : (x + 1) * window]
                value_y = value_y + wx[x : x + 1] * here
                grad_y = grad_y + sx[x : x + 1] * here
                slope_y = slope_y + wx[x : x + 1] * slope[x * window : (x + 1) * window]
            sums = jnp.concatenate(
                [
                    jnp.sum(first_factor * second_factor, axis=0, keepdims=True)
                    for first_factor, second_factor in ((wy, value_y), (wy, grad_y), (sy, value_y), (wy, slope_y))
                ],
                axis=0,
            )
            if h == 0:
                part_s[m, 0:4] = sums
                continue
            sums = sums + part_s[m, 0:4]
            result = rows_of(energy, pair) + 0.5 * rows_of(charge, pair) * sums[0:1]
            for k, b in enumerate(pair):
                cut = slice(k * BLOCK, (k + 1) * BLOCK)
                site[b : b + 1, :] = result[:, cut]
                field[:, b * BLOCK : (b + 1) * BLOCK] = -sums[1:4, cut]

    todo = list(range(len(atom_chunks)))
    for c in range(chunks):
        for n in range(len(subs)):
            stage_y(c, n)
            if todo:
                fill_weights(todo.pop(0))
        fill_green(c)
    for m in todo:
        fill_weights(m)
    for c in range(chunks):
        stage_x(c)
    for c in range(chunks):
        for n in reversed(range(len(subs))):
            stage_v(c, n)
        if c == per_half:
            for n in reversed(range(len(subs))):
                gather(0, n)
            sample(0)
    for n in reversed(range(len(subs))):
        gather(1, n)
    sample(1)
    for copy in pending:
        copy.wait_send()


VMEM_SPEC = pl.BlockSpec(memory_space=pltpu.VMEM)
SMEM_SPEC = pl.BlockSpec(memory_space=pltpu.SMEM)


def call(body, outs, scratch, scalars, args):
    specs = [SMEM_SPEC] * scalars + [VMEM_SPEC] * (len(args) - scalars)
    many = isinstance(outs, (list, tuple))
    return pl.pallas_call(
        body,
        out_shape=outs,
        in_specs=specs,
        out_specs=[VMEM_SPEC] * len(outs) if many else VMEM_SPEC,
        scratch_shapes=scratch,
        compiler_params=pltpu.CompilerParams(vmem_limit_bytes=VMEM_BYTES),
    )(*args)


def pair_call(
    pair_blocks, counts, left, record, right, species_embed, neighbour_embed, w_radial, w_hidden, w_charge, w_energy
):
    blocks = record.shape[1] // BLOCK
    width = w_charge.shape[0]
    shape = jax.ShapeDtypeStruct((blocks, BLOCK), F32)
    square = pltpu.VMEM((BLOCK, BLOCK), F32)
    return call(
        functools.partial(pair_kernel, step=4),
        [shape, shape],
        [
            pltpu.VMEM((record.shape[0], 3 * record.shape[1]), F32),
            pltpu.VMEM((width, BLOCK), BF),
            pltpu.VMEM((width, width), BF),
            *[square] * 4,
        ],
        2,
        (
            pair_blocks.T,
            counts,
            left,
            record,
            right,
            w_radial,
            species_embed,
            neighbour_embed,
            w_hidden,
            jnp.stack([w_charge, w_energy]).astype(F32),
        ),
    )


def mesh_call(cell, frac, charge, energy, back, table_list, doms, groups):
    slab = back.shape[0]
    padded_y = back.shape[1] + 8
    planes = slab + 2
    tiers = slab // PL
    chunks = G // groups // KC
    width_y = G // doms
    subs = len(tier_cuts(tiers))
    atom_chunks = len(chunk_blocks(charge.shape[0]))
    atoms = 2 * BLOCK
    side_rows = 2 * (-(-planes // 8) * 8 + 24)
    dma = pltpu.SemaphoreType.DMA
    grp_shape = pltpu.VMEM((groups, chunks, tiers, padded_y, BLOCK), F32)
    dom_shape = pltpu.VMEM((chunks, doms * tiers * width_y, BLOCK), F32)
    args = [cell, frac, charge, energy, back] + [part for table in table_list for part in table]
    return pl.pallas_call(
        mesh_kernel,
        out_shape=[jax.ShapeDtypeStruct(charge.shape, F32), jax.ShapeDtypeStruct(frac.shape, F32)],
        in_specs=[VMEM_SPEC] * len(args),
        out_specs=[VMEM_SPEC] * 2,
        scratch_shapes=[
            pltpu.VMEM((planes, padded_y, G), F32),
            pltpu.VMEM((2, padded_y, G), F32),
            *[grp_shape] * 2,
            *[dom_shape] * 4,
            *[grp_shape] * 2,
            pltpu.VMEM((chunks, width_y // (2 * PL), G, 2 * BLOCK), F32),
            pltpu.VMEM((atom_chunks, 2, 2, G, atoms), BF),
            pltpu.VMEM((atom_chunks, side_rows, atoms), F32),
            pltpu.VMEM((atom_chunks, 8, atoms), F32),
            pltpu.VMEM((2, planes, padded_y, BLOCK), F32),
            *[dma((6,))] * 2,
            *[dma((chunks, subs, groups - 1))] * 2,
            *[dma((chunks, subs, doms - 1))] * 4,
            *[dma((chunks, subs, groups - 1))] * 2,
            *[dma((chunks, subs))] * 4,
        ],
        compiler_params=pltpu.CompilerParams(
            vmem_limit_bytes=VMEM_BYTES, collective_id=0, has_side_effects=True
        ),
    )(*args)


def tables(slab, quarter, doms, groups, padded_y):
    tiers = slab // PL
    z_order = np.array(
        [g * (G // groups) + c * KC + k for c in range(G // groups // KC) for g in range(groups) for k in range(KC)]
    )
    hz = hartley(z_order)
    y_points = np.array([quarter * g - 1 + r for g in range(groups) for r in range(padded_y)]) % G
    y_used = np.array([r < quarter + 2 for g in range(groups) for r in range(padded_y)])
    hy = hartley(y_points) * y_used[None, :]
    x_points = np.array(
        [slab * d + PL * t + p for p in range(PL) for d in range(doms) for t in tier_order(tiers)]
    )
    hx = hartley(x_points)
    return [np_split(t) for t in (hz, hz.T, hy, hy.T, hx, hx.T)]


def on_device(
    cell_index,
    offsets,
    species,
    pair_blocks,
    counts,
    background,
    species_embed,
    neighbour_embed,
    w_radial,
    w_hidden,
    w_charge,
    w_energy,
):
    atoms = cell_index.shape[1]
    doms = lax.axis_size("dom")
    groups = lax.axis_size("grp")
    slab = G // doms
    quarter = G // groups
    padded_y = quarter + 8

    positions = cell_index.astype(F32) + offsets
    record = jnp.concatenate([positions, species.astype(F32)[None, :]], axis=0)
    left = lax.ppermute(record, "dom", [(i, (i + 1) % doms) for i in range(doms)])
    right = lax.ppermute(record, "dom", [((i + 1) % doms, i) for i in range(doms)])
    energies, charges = pair_call(
        pair_blocks,
        counts,
        left,
        record,
        right,
        species_embed,
        neighbour_embed,
        w_radial,
        w_hidden,
        w_charge,
        w_energy,
    )

    site, field = mesh_call(
        cell_index, offsets, charges, energies, background, tables(slab, quarter, doms, groups, padded_y), doms, groups
    )
    return (site.reshape(atoms), field, charges.reshape(atoms))


def solution(mesh):
    return jax.shard_map(
        on_device,
        mesh=mesh,
        in_specs=(
            P(None, ("grp", "dom")),
            P(None, ("grp", "dom")),
            P(("grp", "dom")),
            P(("grp", "dom"), None),
            P(("grp", "dom")),
            P("dom", "grp", None),
            P(),
            P(),
            P(),
            P(),
            P(),
            P(),
        ),
        out_specs=(P(("grp", "dom")), P(None, ("grp", "dom")), P(("grp", "dom"))),
        check_vma=False,
    )
```

```python
import functools
import math

import jax
import jax.numpy as jnp
import ml_dtypes
import numpy as np
from jax import lax
from jax.experimental import pallas as pl
from jax.experimental.pallas import tpu as pltpu
from jax.sharding import PartitionSpec as P

G = 256
NBASIS = 8
NSPEC = 8
BLOCK = 128
TILES_Y = 4
CUTOFF = 6.0
EWALD = 1.0
VMEM_BYTES = 56 << 20

BF = jnp.bfloat16
F32 = jnp.float32


def np_split(table):
    table = np.asarray(table, np.float32)
    high = table.astype(ml_dtypes.bfloat16)
    low = (table - high.astype(np.float32)).astype(ml_dtypes.bfloat16)
    return high, low


def hartley(points):
    phase = (np.arange(G)[:, None] * np.asarray(points)[None, :]) % G
    angle = phase.astype(np.float64) * (2.0 * math.pi / G)
    return np.cos(angle) + np.sin(angle)


def split2(x):
    high = x.astype(BF)
    low = (x - high.astype(F32)).astype(BF)
    return high, low


def dot_nn(a, b):
    return lax.dot_general(a, b, (((1,), (0,)), ((), ())), preferred_element_type=F32)


def dot_nt(a, b):
    return lax.dot_general(a, b, (((1,), (1,)), ((), ())), preferred_element_type=F32)


def dot3(dot, a, b):
    return dot(a[0], b[0]) + (dot(a[0], b[1]) + dot(a[1], b[0]))


def split3(x):
    one = x.astype(BF).astype(F32)
    two = (x - one).astype(BF).astype(F32)
    three = (x - one - two).astype(BF).astype(F32)
    return one, two, three


def pair_kernel(
    slots,
    live,
    left,
    own,
    right,
    radial_w,
    kind_i_w,
    kind_j_w,
    hidden_w,
    readout_w,
    energy,
    charge,
    ext,
    wcat,
    whid,
    rank_s,
    theta_s,
    env_s,
    kind_s,
    *,
    step,
):
    blocks = energy.shape[0]
    atoms = own.shape[1]
    energy[...] = jnp.zeros_like(energy)
    charge[...] = jnp.zeros_like(charge)
    ext[:, :atoms] = left[...]
    ext[:, atoms : 2 * atoms] = own[...]
    ext[:, 2 * atoms :] = right[...]
    width = hidden_w.shape[0]
    r1, r2, r3 = split3(radial_w[...])
    table = jnp.concatenate(
        [
            *(r1, r2, r3, r1, r2, r1),
            *split3(kind_j_w[...]),
            *split3(kind_i_w[...]),
            jnp.zeros((BLOCK - 12 * NBASIS, width), F32),
        ],
        axis=0,
    )
    wcat[...] = (0.5 * table).T.astype(BF)
    whid[...] = (0.5 * hidden_w[...].astype(F32)).T.astype(BF)
    wq = jnp.broadcast_to(readout_w[0:1, :], (16, width)).astype(BF)
    we = jnp.broadcast_to(readout_w[1:2, :], (16, width)).astype(BF)
    half = 0.5 * G
    row8 = lax.broadcasted_iota(jnp.int32, (NSPEC, BLOCK), 0).astype(F32)
    sub = lax.broadcasted_iota(jnp.int32, (BLOCK, BLOCK), 0)
    lane = lax.broadcasted_iota(jnp.int32, (BLOCK, BLOCK), 1)
    earlier = (lane < sub).astype(F32).astype(BF)
    spare = jnp.zeros((BLOCK - 12 * NBASIS, BLOCK), F32)

    def slot_body(slot, unused):
        bi = slots[0, slot]
        bj = slots[1, slot]
        ri = own[:, pl.ds(pl.multiple_of(bi * BLOCK, BLOCK), BLOCK)]
        rj = ext[:, pl.ds(pl.multiple_of(bj * BLOCK, BLOCK), BLOCK)]
        total = jnp.zeros((BLOCK, BLOCK), F32)
        for c in range(3):
            sep = jnp.broadcast_to(rj[c : c + 1, :], (BLOCK, BLOCK)).T - ri[c : c + 1, :]
            sep = jnp.where(sep > half, sep - G, jnp.where(sep < -half, sep + G, sep))
            total = total + sep * sep
        scaled = jnp.sqrt(total) / CUTOFF
        inside = 1.0 - scaled * scaled
        env = jnp.where(scaled < 1.0, inside * inside, 0.0)
        env = jnp.where((sub == lane) & (bj == blocks + bi), 0.0, env)
        used = (env > 0.0).astype(F32)
        rank_s[...] = jnp.where(env > 0.0, dot_nn(earlier, used.astype(BF)), -1.0)
        theta_s[...] = math.pi * jnp.minimum(scaled, 1.0)
        env_s[...] = env
        kind_s[...] = jnp.broadcast_to(rj[3:4, :], (BLOCK, BLOCK)).T
        most = jnp.max(jnp.sum(used, axis=0, keepdims=True)).astype(jnp.int32)
        kind_i = (row8 == ri[3:4, :]).astype(F32)

        def rows_body(it, sums):
            energy_sum, charge_sum = sums
            rank = rank_s[...]
            parts = []
            envs = []
            for k in range(step):
                pick = rank == (it * step + k).astype(F32)
                theta = jnp.sum(jnp.where(pick, theta_s[...], 0.0), axis=0, keepdims=True)
                kind = jnp.sum(jnp.where(pick, kind_s[...], 0.0), axis=0, keepdims=True)
                envs.append(jnp.sum(jnp.where(pick, env_s[...], 0.0), axis=0, keepdims=True))
                phase = theta * (row8 + 1.0)
                small = phase == 0.0
                rad = jnp.where(small, 1.0, jnp.sin(phase) / jnp.where(small, 1.0, phase))
                one, two, three = split3(rad)
                kind_j = (row8 == kind).astype(F32)
                parts.append(
                    jnp.concatenate(
                        [
                            *(one, one, one, two, two, three),
                            *(kind_j, kind_j, kind_j, kind_i, kind_i, kind_i),
                            spare,
                        ],
                        axis=0,
                    ).astype(BF)
                )
            feats = jnp.concatenate(parts, axis=1)
            h = dot_nn(wcat[...], feats)
            edge = (h + h * jnp.tanh(h)).astype(BF)
            cp = dot_nn(wq, edge)
            g = dot_nn(whid[...], edge)
            latent = (g + g * jnp.tanh(g)).astype(BF)
            ep = dot_nn(we, latent)
            for k in range(step):
                cut = slice(k * BLOCK, (k + 1) * BLOCK)
                charge_sum = charge_sum + envs[k] * cp[0:1, cut]
                energy_sum = energy_sum + envs[k] * ep[0:1, cut]
            return energy_sum, charge_sum

        zero = jnp.zeros((1, BLOCK), F32)
        energy_sum, charge_sum = lax.fori_loop(
            0, (most + step - 1) // step, rows_body, (zero, zero)
        )
        where = pl.ds(bi, 1)
        charge[where, :] = charge[where, :] + charge_sum
        energy[where, :] = energy[where, :] + energy_sum
        return unused

    lax.fori_loop(0, live[0], slot_body, 0)


def spline_rows(rows, first, center, frac, wrap, slopes):
    index = lax.broadcasted_iota(jnp.int32, (rows, frac.shape[1]), 0) + first
    if slopes:
        values = (frac - 0.5, -2.0 * frac, 0.5 + frac)
    else:
        values = ((0.5 - frac) * (0.5 - frac) * 0.5, 0.75 - frac * frac, (0.5 + frac) * (0.5 + frac) * 0.5)
    out = jnp.zeros((rows, frac.shape[1]), F32)
    for o in range(3):
        target = center + (o - 1)
        if wrap:
            target = jnp.where(target < 0, target + G, jnp.where(target >= G, target - G, target))
        out = jnp.where(index == target, values[o], out)
    return out


def chunk_blocks(blocks):
    per_tile = blocks // TILES_Y
    return [
        (t, [t + TILES_Y * z for z in range(2 * pair, 2 * pair + 2)])
        for t in range(TILES_Y)
        for pair in range(per_tile // 2)
    ]


def lanes_of(ref, row, pair):
    return jnp.concatenate([ref[row : row + 1, b * BLOCK : (b + 1) * BLOCK] for b in pair], axis=1)


def rows_of(ref, pair):
    return jnp.concatenate([ref[b : b + 1, :] for b in pair], axis=1)


def swap_blocks(arrays):
    arrays = list(arrays)
    count = len(arrays)
    width = BLOCK // count
    lane = lax.broadcasted_iota(jnp.int32, arrays[0].shape, arrays[0].ndim - 1)
    bit = 1
    while bit < count:
        upper = (lane // (width * bit)) % 2 == 1
        for i in range(count):
            if i & bit:
                continue
            low, high = arrays[i], arrays[i | bit]
            arrays[i] = jnp.where(upper, pltpu.roll(high, width * bit, low.ndim - 1), low)
            arrays[i | bit] = jnp.where(upper, high, pltpu.roll(low, BLOCK - width * bit, low.ndim - 1))
        bit *= 2
    return arrays


VMEM_SPEC = pl.BlockSpec(memory_space=pltpu.VMEM)
SMEM_SPEC = pl.BlockSpec(memory_space=pltpu.SMEM)


def call(body, outs, scratch, scalars, args):
    specs = [SMEM_SPEC] * scalars + [VMEM_SPEC] * (len(args) - scalars)
    many = isinstance(outs, (list, tuple))
    return pl.pallas_call(
        body,
        out_shape=outs,
        in_specs=specs,
        out_specs=[VMEM_SPEC] * len(outs) if many else VMEM_SPEC,
        scratch_shapes=scratch,
        compiler_params=pltpu.CompilerParams(vmem_limit_bytes=VMEM_BYTES),
    )(*args)


def pair_call(
    pair_blocks, counts, left, record, right, species_embed, neighbour_embed, w_radial, w_hidden, w_charge, w_energy
):
    blocks = record.shape[1] // BLOCK
    width = w_charge.shape[0]
    shape = jax.ShapeDtypeStruct((blocks, BLOCK), F32)
    square = pltpu.VMEM((BLOCK, BLOCK), F32)
    return call(
        functools.partial(pair_kernel, step=4),
        [shape, shape],
        [
            pltpu.VMEM((record.shape[0], 3 * record.shape[1]), F32),
            pltpu.VMEM((width, BLOCK), BF),
            pltpu.VMEM((width, width), BF),
            *[square] * 4,
        ],
        2,
        (
            pair_blocks.T,
            counts,
            left,
            record,
            right,
            w_radial,
            species_embed,
            neighbour_embed,
            w_hidden,
            jnp.stack([w_charge, w_energy]).astype(F32),
        ),
    )


def tile_order(slab):
    quads = slab // 4
    order = list(range(1, quads - 1)) + [0, quads - 1]
    return [2 * q + half for q in order for half in range(2)]


def cuts_out(tiles, c):
    return [(0, tiles - 4), (tiles - 4, tiles)] if c == 0 and tiles > 4 else [(0, tiles)]


def cuts_home(tiles, c, chunks):
    return [(tiles - 4, tiles), (0, tiles - 4)] if c == chunks - 1 and tiles > 4 else [(0, tiles)]


def mesh_kernel(
    cell,
    frac,
    charge,
    back,
    tz_hi,
    tz_lo,
    hy_hi,
    hy_lo,
    hx_hi,
    hx_lo,
    ix_hi,
    ix_lo,
    pot,
    grad,
    acc,
    halo,
    row_send,
    row_land,
    edge_send,
    edge_land,
    ready_x,
    land_x,
    ready_y,
    land_y,
    ready_b,
    land_b,
    ready_h,
    land_h,
    green_s,
    weight_s,
    side_s,
    part_s,
    mesh_s,
    hsend,
    hrecv,
    rsend,
    rrecv,
    send_x,
    recv_x,
    send_y,
    recv_y,
    send_b,
    recv_b,
    send_h,
    recv_h,
    loc_x,
    loc_y,
    loc_b,
    loc_h,
):
    chunks, groups, cols, wide = ready_y.shape
    doms = lax.axis_size("dom")
    slab = G // doms
    planes = slab + 2
    quarter = G // groups
    tiles = slab // 2
    tile = quarter // TILES_Y
    window = 24
    lines = doms * tiles
    order = tile_order(slab)
    strips = [divmod(i, doms) for i in range(G // 8)]
    me_g, me_d = lax.axis_index("grp"), lax.axis_index("dom")
    mesh_ids = pl.DeviceIdType.MESH
    barrier = pltpu.get_barrier_semaphore()
    order_g = sorted(range(1, groups), key=lambda k: abs(k - groups // 2))
    order_d = sorted(range(1, doms), key=lambda k: abs(k - doms // 2))
    for h in range(2):
        for base in (0, quarter):
            mesh_s[h, :, base : base + 8, :] = jnp.zeros((planes, 8, BLOCK), F32)
    for axis, me, peers, count in (("grp", me_g, order_g, groups), ("dom", me_d, order_d, doms)):
        for k in peers:
            pl.semaphore_signal(
                barrier, inc=1, device_id={axis: lax.rem(me + k, count)}, device_id_type=mesh_ids
            )

    pending = []

    def remote(src, dst, send_sem, recv_sem, axis, peer):
        copy = pltpu.make_async_remote_copy(
            src_ref=src,
            dst_ref=dst,
            send_sem=send_sem,
            recv_sem=recv_sem,
            device_id={axis: peer},
            device_id_type=mesh_ids,
        )
        copy.start()
        pending.append(copy)
        return copy

    def local_copy(src, dst, sem):
        copy = pltpu.make_async_copy(src, dst, sem)
        copy.start()
        return copy

    def arrive(entry):
        own, copies = entry
        own.wait()
        for copy in copies:
            copy.wait_recv()

    def to_sides(axis, me, count, low, high, low_dst, high_dst, sends, recvs, base):
        before, after = lax.rem(me + count - 1, count), lax.rem(me + 1, count)
        return [
            remote(low, low_dst, sends.at[base], recvs.at[base], axis, before),
            remote(high, high_dst, sends.at[base + 1], recvs.at[base + 1], axis, after),
        ]

    offset_x = 1 - slab * me_d
    offset_y = 1 - quarter * me_g
    atom_chunks = chunk_blocks(charge.shape[0])
    outer = [m for m, (t, _) in enumerate(atom_chunks) if t in (0, TILES_Y - 1)]
    inner = [m for m in range(len(atom_chunks)) if m not in outer]

    def atoms_of(m):
        t, pair = atom_chunks[m]
        local = [
            lanes_of(cell, 0, pair) + offset_x,
            lanes_of(cell, 1, pair) + offset_y,
            lanes_of(cell, 2, pair),
        ]
        return t, pair, local, [lanes_of(frac, axis, pair) for axis in range(3)]

    acc[...] = jnp.zeros_like(acc)
    acc[1 : slab + 1, 1 : quarter + 1, :] = back[...]

    def spread(m):
        t, pair, local, f = atoms_of(m)
        wx = spline_rows(planes, 0, local[0], f[0], False, False)
        wy = spline_rows(window, tile * t, local[1], f[1], False, False)
        wz = spline_rows(G, 0, local[2], f[2], True, False)
        wy = wy * rows_of(charge, pair)
        mix = jnp.concatenate([wx[x : x + 1, :] * wy for x in range(planes)], axis=0)
        part = dot3(dot_nt, split2(mix), split2(wz))
        acc[:, tile * t : tile * t + window, :] += part.reshape(planes, window, G)

    for m in outer:
        spread(m)
    row_send[0] = acc[:, 0, :]
    row_send[1] = acc[:, quarter + 1, :]
    pl.semaphore_wait(barrier, groups + doms - 2)
    rows = to_sides(
        "grp", me_g, groups, row_send.at[0], row_send.at[1], row_land.at[0], row_land.at[1], rsend, rrecv, 0
    )
    for m in inner:
        spread(m)
    for copy in rows:
        copy.wait_recv()
    acc[:, quarter, :] = acc[:, quarter, :] + row_land[0]
    acc[:, 1, :] = acc[:, 1, :] + row_land[1]
    border = to_sides(
        "dom", me_d, doms, acc.at[0], acc.at[slab + 1], halo.at[0], halo.at[1], hsend, hrecv, 0
    )
    table_z = (tz_hi[...], tz_lo[...])

    def transform_z(j):
        base = 1 + 2 * order[j]
        values = acc[base : base + 4, 1 : quarter + 1, :].reshape(4 * quarter, G)
        spec = dot3(dot_nt, table_z, split2(values))
        for c in range(chunks):
            for d in range(doms):
                row = 8 * (c * doms + d)
                for i in range(2):
                    ready_x[c, pl.ds((d * tiles + j + i) * 8, 8)] = spec[
                        row : row + 8, i * BLOCK : (i + 1) * BLOCK
                    ]

    def exchange_dom(src, dst, c, n, cut, send_sem, recv_sem, loc):
        lo, hi = cut

        def at(d):
            return pl.ds((d * tiles + lo) * 8, (hi - lo) * 8)

        copies = []
        for k in order_d:
            peer = lax.rem(me_d + k, doms)
            copies.append(
                remote(
                    src.at[c, at(peer)],
                    dst.at[c, at(me_d)],
                    send_sem.at[c, n, k - 1],
                    recv_sem.at[c, n, k - 1],
                    "dom",
                    peer,
                )
            )
        return local_copy(src.at[c, at(me_d)], dst.at[c, at(me_d)], loc.at[c, n]), copies

    def exchange_grp(src, dst, c, send_sem, recv_sem, loc):
        copies = []
        for k in order_g:
            peer = lax.rem(me_g + k, groups)
            copies.append(
                remote(
                    src.at[c, peer], dst.at[c, me_g], send_sem.at[c, k - 1], recv_sem.at[c, k - 1], "grp", peer
                )
            )
        return local_copy(src.at[c, me_g], dst.at[c, me_g], loc.at[c]), copies

    out_x = {}
    for n, cut in enumerate(cuts_out(tiles, 0)):
        if cut[1] == tiles:
            for copy in border:
                copy.wait_recv()
            acc[1] = acc[1] + halo[1]
            acc[slab] = acc[slab] + halo[0]
        for j in range(cut[0], cut[1], 2):
            transform_z(j)
        out_x[0, n] = exchange_dom(ready_x, land_x, 0, n, cut, send_x, recv_x, loc_x)
    for c in range(1, chunks):
        for n, cut in enumerate(cuts_out(tiles, c)):
            out_x[c, n] = exchange_dom(ready_x, land_x, c, n, cut, send_x, recv_x, loc_x)

    unit = 2.0 * math.pi / G * (2.0 * math.pi / G)
    shape = (8 * cols, G)

    def signed(m):
        return jnp.where(m < G // 2, m, m - G)

    row_id = lax.broadcasted_iota(jnp.int32, shape, 0)
    my = signed(lax.broadcasted_iota(jnp.int32, shape, 1))

    def fill_green(c):
        mz = signed(me_d * (G // doms) + c * 8 + row_id // cols)
        mx = signed(me_g * cols + row_id % cols)
        squares = mx * mx + my * my + mz * mz
        wave = squares.astype(F32) * unit
        safe = jnp.where(squares > 0, wave, 1.0)
        green_s[c] = jnp.where(
            squares > 0, 4.0 * math.pi * jnp.exp(-wave / (4.0 * EWALD * EWALD)) / safe, 0.0
        ) * (1.0 / (G * G * G))

    side_rows = side_s.shape[1] // 2 - window

    def fill_weights(m):
        t, pair, local, f = atoms_of(m)
        for kind in range(2):
            wz = spline_rows(G, 0, local[2], f[2], True, kind == 1)
            high, low = split2(dot3(dot_nn, table_z, split2(wz)))
            weight_s[m, kind, 0] = high
            weight_s[m, kind, 1] = low
            base = kind * (side_rows + window)
            side_s[m, base : base + side_rows] = spline_rows(side_rows, 0, local[0], f[0], False, kind == 1)
            side_s[m, base + side_rows : base + side_rows + window] = spline_rows(
                window, tile * t, local[1], f[1], False, kind == 1
            )

    forward_x = (hx_hi[...], hx_lo[...])
    back_x = (ix_hi[...], ix_lo[...])
    table_y = (hy_hi[...], hy_lo[...])
    out_y, home_b, home_h = {}, {}, {}

    def stage_x(c):
        for n in range(len(cuts_out(tiles, c))):
            arrive(out_x[c, n])
        for two in range(2):
            parts = []
            for kp in (2 * two, 2 * two + 1):
                loaded = [land_x[c, pl.ds(2 * kp + i, lines, stride=8), :] for i in range(2)]
                parts.append(jnp.concatenate(swap_blocks(loaded), axis=0))
            result = dot3(dot_nn, forward_x, split2(jnp.concatenate(parts, axis=1)))
            for g in range(groups):
                ready_y[c, g, :, two * G : (two + 1) * G] = result[g * cols : (g + 1) * cols]
        out_y[c] = exchange_grp(ready_y, land_y, c, send_y, recv_y, loc_y)

    def stage_y(c):
        arrive(out_y[c])
        rows = []
        for kp in range(4):
            cut = slice(kp * BLOCK, (kp + 1) * BLOCK)
            pairs = [
                swap_blocks([land_y[c, g, :, cut], land_y[c, g + 1, :, cut]]) for g in range(0, groups, 2)
            ]
            for i in range(2):
                rows.append(jnp.concatenate([pair[i] for pair in pairs], axis=1))
        spectrum = dot3(dot_nn, split2(jnp.concatenate(rows, axis=0)), table_y) * green_s[c]
        result = dot3(dot_nn, split2(spectrum), table_y)
        for kp in range(4):
            for g in range(0, groups, 2):
                cut = slice(g * quarter, (g + 2) * quarter)
                both = [result[(2 * kp + i) * cols : (2 * kp + i + 1) * cols, cut] for i in range(2)]
                for i, piece in enumerate(swap_blocks(both)):
                    ready_b[c, g + i, :, kp * BLOCK : (kp + 1) * BLOCK] = piece
        home_b[c] = exchange_grp(ready_b, land_b, c, send_b, recv_b, loc_b)

    def stage_h(c):
        arrive(home_b[c])
        for two in range(2):
            column = jnp.concatenate(
                [land_b[c, g, :, two * G : (two + 1) * G] for g in range(groups)], axis=0
            )
            result = dot3(dot_nn, back_x, split2(column))
            for i in range(2):
                cut = slice(i * BLOCK, (i + 1) * BLOCK)
                both = swap_blocks([result[:lines, cut], result[lines:, cut]])
                for k, piece in enumerate(both):
                    ready_h[c, pl.ds(2 * (2 * two + i) + k, lines, stride=8), :] = piece
        for n, cut in enumerate(cuts_home(tiles, c, chunks)):
            home_h[c, n] = exchange_dom(ready_h, land_h, c, n, cut, send_h, recv_h, loc_h)

    edges = {}

    def gather(h, lo, hi):
        for j in range(lo, hi):
            block = jnp.concatenate(
                [land_h[c, pl.ds((d * tiles + j) * 8, 8)] for c, d in strips[16 * h : 16 * (h + 1)]],
                axis=0,
            )
            turned = block.T
            base = 1 + 2 * order[j]
            for i in range(2):
                mesh_s[h, base + i, 1 : quarter + 1, :] = turned[i * quarter : (i + 1) * quarter]

    def send_edges(h):
        edges[h] = to_sides(
            "dom",
            me_d,
            doms,
            mesh_s.at[h, 1],
            mesh_s.at[h, slab],
            mesh_s.at[h, slab + 1],
            mesh_s.at[h, 0],
            hsend,
            hrecv,
            2 + 2 * h,
        )

    def send_rows(h):
        for copy in edges[h]:
            copy.wait()
            pending[:] = [other for other in pending if other is not copy]
        edge_send[h, 0] = mesh_s[h, :, 1, :]
        edge_send[h, 1] = mesh_s[h, :, quarter, :]
        return to_sides(
            "grp",
            me_g,
            groups,
            edge_send.at[h, 0],
            edge_send.at[h, 1],
            edge_land.at[h, 0],
            edge_land.at[h, 1],
            rsend,
            rrecv,
            2 + 2 * h,
        )

    def sample(h, chosen):
        half = slice(h * BLOCK, (h + 1) * BLOCK)
        known = None
        for m in chosen:
            t, pair = atom_chunks[m]
            if t != known:
                strip = mesh_s[h, :, tile * t : tile * t + window, :].reshape(planes * window, BLOCK)
                strip = jnp.concatenate(split2(strip), axis=1)
                known = t

            def along(kind):
                high, low = weight_s[m, kind, 0, half], weight_s[m, kind, 1, half]
                return dot_nn(strip, jnp.concatenate([high, high], axis=0)) + dot_nn(
                    strip, jnp.concatenate([low, low], axis=0)
                )

            wx, wy = side_s[m, :side_rows], side_s[m, side_rows : side_rows + window]
            sx = side_s[m, side_rows + window : 2 * side_rows + window]
            sy = side_s[m, 2 * side_rows + window :]
            value, slope = along(0), along(1)
            value_y = jnp.zeros_like(wy)
            grad_y = jnp.zeros_like(wy)
            slope_y = jnp.zeros_like(wy)
            for x in range(planes):
                here = value[x * window : (x + 1) * window]
                value_y = value_y + wx[x : x + 1] * here
                grad_y = grad_y + sx[x : x + 1] * here
                slope_y = slope_y + wx[x : x + 1] * slope[x * window : (x + 1) * window]
            sums = jnp.concatenate(
                [
                    jnp.sum(one * two, axis=0, keepdims=True)
                    for one, two in ((wy, value_y), (wy, grad_y), (sy, value_y), (wy, slope_y))
                ],
                axis=0,
            )
            if h == 0:
                part_s[m, 0:4] = sums
                continue
            sums = sums + part_s[m, 0:4]
            for k, b in enumerate(pair):
                cut = slice(k * BLOCK, (k + 1) * BLOCK)
                pot[b : b + 1, :] = sums[0:1, cut]
                grad[:, b * BLOCK : (b + 1) * BLOCK] = sums[1:4, cut]

    def finish(h):
        rows = send_rows(h)
        sample(h, inner)
        for copy in rows:
            copy.wait_recv()
        mesh_s[h, :, quarter + 1, :] = edge_land[h, 0]
        mesh_s[h, :, 0, :] = edge_land[h, 1]
        sample(h, outer)

    for m in range(len(atom_chunks)):
        fill_weights(m)
    for c in range(chunks):
        fill_green(c)
    for c in range(chunks):
        stage_x(c)
        if c:
            stage_h(c - 1)
        stage_y(c)
    stage_h(chunks - 1)
    for h in range(2):
        needed = sorted({c for c, _ in strips[16 * h : 16 * (h + 1)]})
        for n, (lo, hi) in enumerate(cuts_home(tiles, needed[-1], chunks)):
            for c in needed:
                for key in [(c, i) for i in range(n + 1)]:
                    if key in home_h:
                        arrive(home_h.pop(key))
            gather(h, lo, hi)
            if hi == tiles:
                send_edges(h)
        finish(h)
    for copy in pending:
        copy.wait_send()


def mesh_call(cell, frac, charge, back, table_list, doms, groups):
    slab = back.shape[0]
    quarter = back.shape[1]
    padded_y = quarter + 8
    planes = slab + 2
    tiles = slab // 2
    chunks = G // doms // 8
    atom_chunks = len(chunk_blocks(charge.shape[0]))
    atoms = 2 * BLOCK
    side_rows = 2 * (-(-planes // 8) * 8 + 24)
    dma = pltpu.SemaphoreType.DMA
    dom_shape = pltpu.VMEM((chunks, doms * tiles * 8, BLOCK), F32)
    grp_shape = pltpu.VMEM((chunks, groups, G // groups, 8 * quarter), F32)
    row_shape = pltpu.VMEM((2, planes, G), F32)
    edge_shape = pltpu.VMEM((2, 2, planes, BLOCK), F32)
    args = [cell, frac, charge, back] + [part for table in table_list for part in table]
    return pl.pallas_call(
        mesh_kernel,
        out_shape=[jax.ShapeDtypeStruct(charge.shape, F32), jax.ShapeDtypeStruct(frac.shape, F32)],
        in_specs=[VMEM_SPEC] * len(args),
        out_specs=[VMEM_SPEC] * 2,
        scratch_shapes=[
            pltpu.VMEM((planes, padded_y, G), F32),
            pltpu.VMEM((2, padded_y, G), F32),
            *[row_shape] * 2,
            *[edge_shape] * 2,
            *[dom_shape] * 2,
            *[grp_shape] * 4,
            *[dom_shape] * 2,
            pltpu.VMEM((chunks, 8 * (G // groups), G), F32),
            pltpu.VMEM((atom_chunks, 2, 2, G, atoms), BF),
            pltpu.VMEM((atom_chunks, side_rows, atoms), F32),
            pltpu.VMEM((atom_chunks, 8, atoms), F32),
            pltpu.VMEM((2, planes, padded_y, BLOCK), F32),
            *[dma((6,))] * 4,
            *[dma((chunks, 2, doms - 1))] * 2,
            *[dma((chunks, groups - 1))] * 4,
            *[dma((chunks, 2, doms - 1))] * 2,
            dma((chunks, 2)),
            dma((chunks,)),
            dma((chunks,)),
            dma((chunks, 2)),
        ],
        compiler_params=pltpu.CompilerParams(
            vmem_limit_bytes=VMEM_BYTES, collective_id=0, has_side_effects=True
        ),
    )(*args)


def tables(slab, doms):
    chunks = G // doms // 8
    plain = hartley(np.arange(G))
    z_order = np.array([d * (G // doms) + c * 8 + k for c in range(chunks) for d in range(doms) for k in range(8)])
    hz = hartley(z_order)
    x_points = np.array([slab * d + 2 * t + i for i in range(2) for d in range(doms) for t in tile_order(slab)])
    hx = hartley(x_points)
    return [np_split(t) for t in (hz.T, plain, hx, hx.T)]


def on_device(
    cell_index,
    offsets,
    species,
    pair_blocks,
    counts,
    background,
    species_embed,
    neighbour_embed,
    w_radial,
    w_hidden,
    w_charge,
    w_energy,
):
    atoms = cell_index.shape[1]
    doms = lax.axis_size("dom")
    groups = lax.axis_size("grp")
    positions = cell_index.astype(F32) + offsets
    record = jnp.concatenate([positions, species.astype(F32)[None, :]], axis=0)
    left = lax.ppermute(record, "dom", [(i, (i + 1) % doms) for i in range(doms)])
    right = lax.ppermute(record, "dom", [((i + 1) % doms, i) for i in range(doms)])
    energies, charges = pair_call(
        pair_blocks,
        counts,
        left,
        record,
        right,
        species_embed,
        neighbour_embed,
        w_radial,
        w_hidden,
        w_charge,
        w_energy,
    )

    potential, gradient = mesh_call(
        cell_index, offsets, charges, background, tables(G // doms, doms), doms, groups
    )
    site = energies + 0.5 * charges * potential
    return (site.reshape(atoms), -gradient, charges.reshape(atoms))


def solution(mesh):
    return jax.shard_map(
        on_device,
        mesh=mesh,
        in_specs=(
            P(None, ("grp", "dom")),
            P(None, ("grp", "dom")),
            P(("grp", "dom")),
            P(("grp", "dom"), None),
            P(("grp", "dom")),
            P("dom", "grp", None),
            P(),
            P(),
            P(),
            P(),
            P(),
            P(),
        ),
        out_specs=(P(("grp", "dom")), P(None, ("grp", "dom")), P(("grp", "dom"))),
        check_vma=False,
    )
```

```python
import functools
import math

import jax
import jax.numpy as jnp
import ml_dtypes
import numpy as np
from jax import lax
from jax.experimental import pallas as pl
from jax.experimental.pallas import tpu as pltpu
from jax.sharding import PartitionSpec as P

G = 256
NBASIS = 8
NSPEC = 8
BLOCK = 128
TILES_Y = 4
CUTOFF = 6.0
EWALD = 1.0
VMEM_BYTES = 56 << 20

BF = jnp.bfloat16
F32 = jnp.float32


def np_split(table):
    table = np.asarray(table, np.float32)
    high = table.astype(ml_dtypes.bfloat16)
    low = (table - high.astype(np.float32)).astype(ml_dtypes.bfloat16)
    return high, low


def hartley(points):
    phase = (np.arange(G)[:, None] * np.asarray(points)[None, :]) % G
    angle = phase.astype(np.float64) * (2.0 * math.pi / G)
    return np.cos(angle) + np.sin(angle)


def split2(x):
    high = x.astype(BF)
    low = (x - high.astype(F32)).astype(BF)
    return high, low


def dot_nn(a, b):
    return lax.dot_general(a, b, (((1,), (0,)), ((), ())), preferred_element_type=F32)


def dot_nt(a, b):
    return lax.dot_general(a, b, (((1,), (1,)), ((), ())), preferred_element_type=F32)


def dot3(dot, a, b):
    return dot(a[0], b[0]) + (dot(a[0], b[1]) + dot(a[1], b[0]))


def split3(x):
    one = x.astype(BF).astype(F32)
    two = (x - one).astype(BF).astype(F32)
    three = (x - one - two).astype(BF).astype(F32)
    return one, two, three


def pair_kernel(
    slots,
    live,
    ext,
    radial_w,
    kind_i_w,
    kind_j_w,
    hidden_w,
    charge_w,
    energy_w,
    energy,
    charge,
    wcat,
    whid,
    rank_s,
    theta_s,
    env_s,
    kind_s,
    *,
    step,
):
    blocks = energy.shape[0]
    atoms = ext.shape[1] // 3
    energy[...] = jnp.zeros_like(energy)
    charge[...] = jnp.zeros_like(charge)
    width = hidden_w.shape[0]
    r1, r2, r3 = split3(radial_w[...])
    table = jnp.concatenate(
        [
            *(r1, r2, r3, r1, r2, r1),
            *split3(kind_j_w[...]),
            *split3(kind_i_w[...]),
            jnp.zeros((BLOCK - 12 * NBASIS, width), F32),
        ],
        axis=0,
    )
    wcat[...] = (0.5 * table).T.astype(BF)
    whid[...] = (0.5 * hidden_w[...].astype(F32)).T.astype(BF)

    def spread_row(ref):
        rows = ref[...].astype(F32)
        row = jnp.concatenate([rows[i : i + 1] for i in range(rows.shape[0])], axis=1)
        return jnp.broadcast_to(row, (16, width)).astype(BF)

    wq = spread_row(charge_w)
    we = spread_row(energy_w)
    half = 0.5 * G
    row8 = lax.broadcasted_iota(jnp.int32, (NSPEC, BLOCK), 0).astype(F32)
    sub = lax.broadcasted_iota(jnp.int32, (BLOCK, BLOCK), 0)
    lane = lax.broadcasted_iota(jnp.int32, (BLOCK, BLOCK), 1)
    earlier = (lane < sub).astype(F32).astype(BF)
    spare = jnp.zeros((BLOCK - 12 * NBASIS, BLOCK), F32)

    def slot_body(slot, unused):
        bi = slots[0, slot]
        bj = slots[1, slot]
        ri = ext[:, pl.ds(pl.multiple_of(atoms + bi * BLOCK, BLOCK), BLOCK)]
        rj = ext[:, pl.ds(pl.multiple_of(bj * BLOCK, BLOCK), BLOCK)]
        total = jnp.zeros((BLOCK, BLOCK), F32)
        for c in range(3):
            sep = jnp.broadcast_to(rj[c : c + 1, :], (BLOCK, BLOCK)).T - ri[c : c + 1, :]
            sep = jnp.where(sep > half, sep - G, jnp.where(sep < -half, sep + G, sep))
            total = total + sep * sep
        scaled = jnp.sqrt(total) / CUTOFF
        inside = 1.0 - scaled * scaled
        env = jnp.where(scaled < 1.0, inside * inside, 0.0)
        env = jnp.where((sub == lane) & (bj == blocks + bi), 0.0, env)
        used = (env > 0.0).astype(F32)
        rank_s[...] = jnp.where(env > 0.0, dot_nn(earlier, used.astype(BF)), -1.0)
        theta_s[...] = math.pi * jnp.minimum(scaled, 1.0)
        env_s[...] = env
        kind_s[...] = jnp.broadcast_to(rj[3:4, :], (BLOCK, BLOCK)).T
        most = jnp.max(jnp.sum(used, axis=0, keepdims=True)).astype(jnp.int32)
        kind_i = (row8 == ri[3:4, :]).astype(F32)

        def rows_body(it, sums):
            energy_sum, charge_sum = sums
            rank = rank_s[...]
            parts = []
            envs = []
            for k in range(step):
                pick = rank == (it * step + k).astype(F32)
                theta = jnp.sum(jnp.where(pick, theta_s[...], 0.0), axis=0, keepdims=True)
                kind = jnp.sum(jnp.where(pick, kind_s[...], 0.0), axis=0, keepdims=True)
                envs.append(jnp.sum(jnp.where(pick, env_s[...], 0.0), axis=0, keepdims=True))
                phase = theta * (row8 + 1.0)
                small = phase == 0.0
                rad = jnp.where(small, 1.0, jnp.sin(phase) / jnp.where(small, 1.0, phase))
                one, two, three = split3(rad)
                kind_j = (row8 == kind).astype(F32)
                parts.append(
                    jnp.concatenate(
                        [
                            *(one, one, one, two, two, three),
                            *(kind_j, kind_j, kind_j, kind_i, kind_i, kind_i),
                            spare,
                        ],
                        axis=0,
                    ).astype(BF)
                )
            feats = jnp.concatenate(parts, axis=1)
            h = dot_nn(wcat[...], feats)
            edge = (h + h * jnp.tanh(h)).astype(BF)
            cp = dot_nn(wq, edge)
            g = dot_nn(whid[...], edge)
            latent = (g + g * jnp.tanh(g)).astype(BF)
            ep = dot_nn(we, latent)
            for k in range(step):
                cut = slice(k * BLOCK, (k + 1) * BLOCK)
                charge_sum = charge_sum + envs[k] * cp[0:1, cut]
                energy_sum = energy_sum + envs[k] * ep[0:1, cut]
            return energy_sum, charge_sum

        zero = jnp.zeros((1, BLOCK), F32)
        energy_sum, charge_sum = lax.fori_loop(
            0, (most + step - 1) // step, rows_body, (zero, zero)
        )
        where = pl.ds(bi, 1)
        charge[where, :] = charge[where, :] + charge_sum
        energy[where, :] = energy[where, :] + energy_sum
        return unused

    lax.fori_loop(0, live[0], slot_body, 0)


def spline_rows(rows, first, center, frac, wrap, slopes):
    index = lax.broadcasted_iota(jnp.int32, (rows, frac.shape[1]), 0) + first
    if slopes:
        values = (frac - 0.5, -2.0 * frac, 0.5 + frac)
    else:
        values = ((0.5 - frac) * (0.5 - frac) * 0.5, 0.75 - frac * frac, (0.5 + frac) * (0.5 + frac) * 0.5)
    out = jnp.zeros((rows, frac.shape[1]), F32)
    for o in range(3):
        target = center + (o - 1)
        if wrap:
            target = jnp.where(target < 0, target + G, jnp.where(target >= G, target - G, target))
        out = jnp.where(index == target, values[o], out)
    return out


def chunk_blocks(blocks):
    per_tile = blocks // TILES_Y
    return [
        (t, [t + TILES_Y * z for z in range(2 * pair, 2 * pair + 2)])
        for t in range(TILES_Y)
        for pair in range(per_tile // 2)
    ]


def lanes_of(ref, row, pair):
    return jnp.concatenate([ref[row : row + 1, b * BLOCK : (b + 1) * BLOCK] for b in pair], axis=1)


def rows_of(ref, pair):
    return jnp.concatenate([ref[b : b + 1, :] for b in pair], axis=1)


def swap_blocks(arrays):
    arrays = list(arrays)
    count = len(arrays)
    width = BLOCK // count
    lane = lax.broadcasted_iota(jnp.int32, arrays[0].shape, arrays[0].ndim - 1)
    bit = 1
    while bit < count:
        upper = (lane // (width * bit)) % 2 == 1
        for i in range(count):
            if i & bit:
                continue
            low, high = arrays[i], arrays[i | bit]
            arrays[i] = jnp.where(upper, pltpu.roll(high, width * bit, low.ndim - 1), low)
            arrays[i | bit] = jnp.where(upper, high, pltpu.roll(low, BLOCK - width * bit, low.ndim - 1))
        bit *= 2
    return arrays


VMEM_SPEC = pl.BlockSpec(memory_space=pltpu.VMEM)
SMEM_SPEC = pl.BlockSpec(memory_space=pltpu.SMEM)


def call(body, outs, scratch, scalars, args):
    specs = [SMEM_SPEC] * scalars + [VMEM_SPEC] * (len(args) - scalars)
    many = isinstance(outs, (list, tuple))
    return pl.pallas_call(
        body,
        out_shape=outs,
        in_specs=specs,
        out_specs=[VMEM_SPEC] * len(outs) if many else VMEM_SPEC,
        scratch_shapes=scratch,
        compiler_params=pltpu.CompilerParams(vmem_limit_bytes=VMEM_BYTES),
    )(*args)


def share_kernel(cell, frac, kind, ext, sends, recvs):
    atoms = cell.shape[1]
    doms = lax.axis_size("dom")
    me = lax.axis_index("dom")
    mesh_ids = pl.DeviceIdType.MESH
    left, right = lax.rem(me + doms - 1, doms), lax.rem(me + 1, doms)
    barrier = pltpu.get_barrier_semaphore()
    for side in (left, right):
        pl.semaphore_signal(barrier, inc=1, device_id={"dom": side}, device_id_type=mesh_ids)
    own = pl.ds(atoms, atoms)
    ext[0:3, own] = cell[...].astype(F32) + frac[...]
    ext[3:4, own] = kind[...].astype(F32)
    pl.semaphore_wait(barrier, 2)
    copies = []
    for i, (side, slot) in enumerate(((left, 2), (right, 0))):
        copy = pltpu.make_async_remote_copy(
            src_ref=ext.at[:, own],
            dst_ref=ext.at[:, pl.ds(slot * atoms, atoms)],
            send_sem=sends.at[i],
            recv_sem=recvs.at[i],
            device_id={"dom": side},
            device_id_type=mesh_ids,
        )
        copy.start()
        copies.append(copy)
    for copy in copies:
        copy.wait()


def share_call(cell, frac, kind):
    return pl.pallas_call(
        share_kernel,
        out_shape=jax.ShapeDtypeStruct((4, 3 * cell.shape[1]), F32),
        in_specs=[VMEM_SPEC] * 3,
        out_specs=VMEM_SPEC,
        scratch_shapes=[pltpu.SemaphoreType.DMA((2,))] * 2,
        compiler_params=pltpu.CompilerParams(
            vmem_limit_bytes=VMEM_BYTES, collective_id=1, has_side_effects=True
        ),
    )(cell, frac, kind[None, :])


def pair_call(
    pair_blocks, counts, ext, species_embed, neighbour_embed, w_radial, w_hidden, w_charge, w_energy
):
    blocks = ext.shape[1] // (3 * BLOCK)
    width = w_charge.shape[0]
    shape = jax.ShapeDtypeStruct((blocks, BLOCK), F32)
    square = pltpu.VMEM((BLOCK, BLOCK), F32)
    return call(
        functools.partial(pair_kernel, step=4),
        [shape, shape],
        [
            pltpu.VMEM((width, BLOCK), BF),
            pltpu.VMEM((width, width), BF),
            *[square] * 4,
        ],
        2,
        (
            pair_blocks.T,
            counts,
            ext,
            w_radial,
            species_embed,
            neighbour_embed,
            w_hidden,
            w_charge.reshape(-1, BLOCK),
            w_energy.reshape(-1, BLOCK),
        ),
    )


def tile_order(slab):
    quads = slab // 4
    order = list(range(1, quads - 1)) + [0, quads - 1]
    return [2 * q + half for q in order for half in range(2)]


def tile_cuts(tiles):
    return [(0, tiles // 2), (tiles // 2, tiles)]


def mesh_kernel(
    cell,
    frac,
    charge,
    back,
    tz_hi,
    tz_lo,
    hy_hi,
    hy_lo,
    hx_hi,
    hx_lo,
    ix_hi,
    ix_lo,
    pot,
    grad,
    acc,
    halo,
    row_send,
    row_land,
    edge_send,
    edge_land,
    ready_x,
    land_x,
    ready_y,
    land_y,
    ready_b,
    land_b,
    ready_h,
    land_h,
    green_s,
    weight_s,
    side_s,
    part_s,
    mesh_s,
    hsend,
    hrecv,
    rsend,
    rrecv,
    send_x,
    recv_x,
    send_y,
    recv_y,
    send_b,
    recv_b,
    send_h,
    recv_h,
    loc_x,
    loc_y,
    loc_b,
    loc_h,
):
    halves, groups, cols, wide = ready_y.shape
    chunks = halves // 2
    doms = lax.axis_size("dom")
    slab = G // doms
    planes = slab + 2
    quarter = G // groups
    tiles = slab // 2
    tile = quarter // TILES_Y
    window = 24
    lines = doms * tiles
    order = tile_order(slab)
    strips = [divmod(i, doms) for i in range(G // 8)]
    me_g, me_d = lax.axis_index("grp"), lax.axis_index("dom")
    mesh_ids = pl.DeviceIdType.MESH
    barrier = pltpu.get_barrier_semaphore()
    order_g = sorted(range(1, groups), key=lambda k: abs(k - groups // 2))
    order_d = sorted(range(1, doms), key=lambda k: abs(k - doms // 2))
    for h in range(2):
        for base in (0, quarter):
            mesh_s[h, :, base : base + 8, :] = jnp.zeros((planes, 8, BLOCK), F32)
    for axis, me, peers, count in (("grp", me_g, order_g, groups), ("dom", me_d, order_d, doms)):
        for k in peers:
            pl.semaphore_signal(
                barrier, inc=1, device_id={axis: lax.rem(me + k, count)}, device_id_type=mesh_ids
            )

    pending = []

    def remote(src, dst, send_sem, recv_sem, axis, peer):
        copy = pltpu.make_async_remote_copy(
            src_ref=src,
            dst_ref=dst,
            send_sem=send_sem,
            recv_sem=recv_sem,
            device_id={axis: peer},
            device_id_type=mesh_ids,
        )
        copy.start()
        pending.append(copy)
        return copy

    def local_copy(src, dst, sem):
        copy = pltpu.make_async_copy(src, dst, sem)
        copy.start()
        return copy

    def arrive(entry):
        own, copies = entry
        own.wait()
        for copy in copies:
            copy.wait_recv()

    def to_sides(axis, me, count, low, high, low_dst, high_dst, sends, recvs, base):
        before, after = lax.rem(me + count - 1, count), lax.rem(me + 1, count)
        return [
            remote(low, low_dst, sends.at[base], recvs.at[base], axis, before),
            remote(high, high_dst, sends.at[base + 1], recvs.at[base + 1], axis, after),
        ]

    offset_x = 1 - slab * me_d
    offset_y = 1 - quarter * me_g
    atom_chunks = chunk_blocks(charge.shape[0])
    outer = [m for m, (t, _) in enumerate(atom_chunks) if t in (0, TILES_Y - 1)]
    inner = [m for m in range(len(atom_chunks)) if m not in outer]

    def atoms_of(m):
        t, pair = atom_chunks[m]
        local = [
            lanes_of(cell, 0, pair) + offset_x,
            lanes_of(cell, 1, pair) + offset_y,
            lanes_of(cell, 2, pair),
        ]
        return t, pair, local, [lanes_of(frac, axis, pair) for axis in range(3)]

    acc[...] = jnp.zeros_like(acc)
    acc[1 : slab + 1, 1 : quarter + 1, :] = back[...]

    def spread(m):
        t, pair, local, f = atoms_of(m)
        wx = spline_rows(planes, 0, local[0], f[0], False, False)
        wy = spline_rows(window, tile * t, local[1], f[1], False, False)
        wz = spline_rows(G, 0, local[2], f[2], True, False)
        wy = wy * rows_of(charge, pair)
        mix = jnp.concatenate([wx[x : x + 1, :] * wy for x in range(planes)], axis=0)
        part = dot3(dot_nt, split2(mix), split2(wz))
        acc[:, tile * t : tile * t + window, :] += part.reshape(planes, window, G)

    for m in outer:
        spread(m)
    row_send[0] = acc[:, 0, :]
    row_send[1] = acc[:, quarter + 1, :]
    pl.semaphore_wait(barrier, groups + doms - 2)
    rows = to_sides(
        "grp", me_g, groups, row_send.at[0], row_send.at[1], row_land.at[0], row_land.at[1], rsend, rrecv, 0
    )
    for m in inner:
        spread(m)
    for copy in rows:
        copy.wait_recv()
    acc[:, quarter, :] = acc[:, quarter, :] + row_land[0]
    acc[:, 1, :] = acc[:, 1, :] + row_land[1]
    border = to_sides(
        "dom", me_d, doms, acc.at[0], acc.at[slab + 1], halo.at[0], halo.at[1], hsend, hrecv, 0
    )
    table_z = (tz_hi[...], tz_lo[...])

    def transform_z(j):
        base = 1 + 2 * order[j]
        values = acc[base : base + 4, 1 : quarter + 1, :].reshape(4 * quarter, G)
        spec = dot3(dot_nt, table_z, split2(values))
        for c in range(chunks):
            for d in range(doms):
                row = 8 * (c * doms + d)
                for i in range(2):
                    ready_x[c, pl.ds((d * tiles + j + i) * 8, 8)] = spec[
                        row : row + 8, i * BLOCK : (i + 1) * BLOCK
                    ]

    def exchange_dom(src, dst, c, n, cut, send_sem, recv_sem, loc):
        lo, hi = cut

        def at(d):
            return pl.ds((d * tiles + lo) * 8, (hi - lo) * 8)

        copies = []
        for k in order_d:
            peer = lax.rem(me_d + k, doms)
            copies.append(
                remote(
                    src.at[c, at(peer)],
                    dst.at[c, at(me_d)],
                    send_sem.at[c, n, k - 1],
                    recv_sem.at[c, n, k - 1],
                    "dom",
                    peer,
                )
            )
        return local_copy(src.at[c, at(me_d)], dst.at[c, at(me_d)], loc.at[c, n]), copies

    def exchange_grp(src, dst, c, send_sem, recv_sem, loc):
        copies = []
        for k in order_g:
            peer = lax.rem(me_g + k, groups)
            copies.append(
                remote(
                    src.at[c, peer], dst.at[c, me_g], send_sem.at[c, k - 1], recv_sem.at[c, k - 1], "grp", peer
                )
            )
        return local_copy(src.at[c, me_g], dst.at[c, me_g], loc.at[c]), copies

    cuts = tile_cuts(tiles)
    pieces = [(c, n) for c in range(chunks) for n in range(2)]
    out_x = {}
    left_out = set()

    def send_out(c, n):
        out_x[c, n] = exchange_dom(ready_x, land_x, c, n, cuts[n], send_x, recv_x, loc_x)

    def advance(depth):
        at = len(out_x)
        if at == len(pieces):
            return
        done = [] if at - depth in left_out else out_x[pieces[at - depth]][1]
        left_out.add(at - depth)
        for copy in done:
            copy.wait_send()
        pending[:] = [other for other in pending if all(other is not copy for copy in done)]
        send_out(*pieces[at])

    joined = False
    for n, (lo, hi) in enumerate(cuts):
        if hi > tiles - 4 and not joined:
            for copy in border:
                copy.wait_recv()
            acc[1] = acc[1] + halo[1]
            acc[slab] = acc[slab] + halo[0]
            joined = True
        for j in range(lo, hi, 2):
            transform_z(j)
        send_out(0, n)

    unit = 2.0 * math.pi / G * (2.0 * math.pi / G)
    shape = (4 * cols, G)

    def signed(m):
        return jnp.where(m < G // 2, m, m - G)

    row_id = lax.broadcasted_iota(jnp.int32, shape, 0)
    my = signed(lax.broadcasted_iota(jnp.int32, shape, 1))

    def fill_green(part):
        mz = signed(me_d * (G // doms) + part * 4 + row_id // cols)
        mx = signed(me_g * cols + row_id % cols)
        squares = mx * mx + my * my + mz * mz
        wave = squares.astype(F32) * unit
        safe = jnp.where(squares > 0, wave, 1.0)
        green_s[part] = jnp.where(
            squares > 0, 4.0 * math.pi * jnp.exp(-wave / (4.0 * EWALD * EWALD)) / safe, 0.0
        ) * (1.0 / (G * G * G))

    side_rows = side_s.shape[1] // 2 - window

    def fill_weights(m):
        t, pair, local, f = atoms_of(m)
        for kind in range(2):
            wz = spline_rows(G, 0, local[2], f[2], True, kind == 1)
            high, low = split2(dot3(dot_nn, table_z, split2(wz)))
            weight_s[m, kind, 0] = high
            weight_s[m, kind, 1] = low
            base = kind * (side_rows + window)
            side_s[m, base : base + side_rows] = spline_rows(side_rows, 0, local[0], f[0], False, kind == 1)
            side_s[m, base + side_rows : base + side_rows + window] = spline_rows(
                window, tile * t, local[1], f[1], False, kind == 1
            )

    forward_x = (hx_hi[...], hx_lo[...])
    back_x = (ix_hi[...], ix_lo[...])
    table_y = (hy_hi[...], hy_lo[...])
    out_y, home_b, home_h = {}, {}, {}

    def stage_x(c):
        for n in range(2):
            arrive(out_x[c, n])
        for two in range(2):
            parts = []
            for kp in (2 * two, 2 * two + 1):
                loaded = [land_x[c, pl.ds(2 * kp + i, lines, stride=8), :] for i in range(2)]
                parts.append(jnp.concatenate(swap_blocks(loaded), axis=0))
            result = dot3(dot_nn, forward_x, split2(jnp.concatenate(parts, axis=1)))
            part = 2 * c + two
            for g in range(groups):
                ready_y[part, g] = result[g * cols : (g + 1) * cols]
            out_y[part] = exchange_grp(ready_y, land_y, part, send_y, recv_y, loc_y)

    def stage_y(part):
        arrive(out_y[part])
        rows = []
        for kp in range(2):
            cut = slice(kp * BLOCK, (kp + 1) * BLOCK)
            pairs = [
                swap_blocks([land_y[part, g, :, cut], land_y[part, g + 1, :, cut]])
                for g in range(0, groups, 2)
            ]
            for i in range(2):
                rows.append(jnp.concatenate([pair[i] for pair in pairs], axis=1))
        spectrum = dot3(dot_nn, split2(jnp.concatenate(rows, axis=0)), table_y) * green_s[part]
        result = dot3(dot_nn, split2(spectrum), table_y)
        for kp in range(2):
            for g in range(0, groups, 2):
                cut = slice(g * quarter, (g + 2) * quarter)
                both = [result[(2 * kp + i) * cols : (2 * kp + i + 1) * cols, cut] for i in range(2)]
                for i, piece in enumerate(swap_blocks(both)):
                    ready_b[part, g + i, :, kp * BLOCK : (kp + 1) * BLOCK] = piece
        home_b[part] = exchange_grp(ready_b, land_b, part, send_b, recv_b, loc_b)

    def stage_h(c):
        for two in range(2):
            arrive(home_b[2 * c + two])
            column = jnp.concatenate([land_b[2 * c + two, g] for g in range(groups)], axis=0)
            result = dot3(dot_nn, back_x, split2(column))
            for i in range(2):
                cut = slice(i * BLOCK, (i + 1) * BLOCK)
                both = swap_blocks([result[:lines, cut], result[lines:, cut]])
                for k, piece in enumerate(both):
                    ready_h[c, pl.ds(2 * (2 * two + i) + k, lines, stride=8), :] = piece
        for n, cut in enumerate(reversed(cuts)):
            home_h[c, n] = exchange_dom(ready_h, land_h, c, n, cut, send_h, recv_h, loc_h)

    edges = {}

    def gather(h, lo, hi):
        for j in range(lo, hi):
            block = jnp.concatenate(
                [land_h[c, pl.ds((d * tiles + j) * 8, 8)] for c, d in strips[16 * h : 16 * (h + 1)]],
                axis=0,
            )
            turned = block.T
            base = 1 + 2 * order[j]
            for i in range(2):
                mesh_s[h, base + i, 1 : quarter + 1, :] = turned[i * quarter : (i + 1) * quarter]

    def send_edges(h):
        edges[h] = to_sides(
            "dom",
            me_d,
            doms,
            mesh_s.at[h, 1],
            mesh_s.at[h, slab],
            mesh_s.at[h, slab + 1],
            mesh_s.at[h, 0],
            hsend,
            hrecv,
            2 + 2 * h,
        )

    def send_rows(h):
        for copy in edges[h]:
            copy.wait()
            pending[:] = [other for other in pending if other is not copy]
        edge_send[h, 0] = mesh_s[h, :, 1, :]
        edge_send[h, 1] = mesh_s[h, :, quarter, :]
        return to_sides(
            "grp",
            me_g,
            groups,
            edge_send.at[h, 0],
            edge_send.at[h, 1],
            edge_land.at[h, 0],
            edge_land.at[h, 1],
            rsend,
            rrecv,
            2 + 2 * h,
        )

    def sample(h, chosen):
        half = slice(h * BLOCK, (h + 1) * BLOCK)
        known = None
        for m in chosen:
            t, pair = atom_chunks[m]
            if t != known:
                strip = mesh_s[h, :, tile * t : tile * t + window, :].reshape(planes * window, BLOCK)
                strip = jnp.concatenate(split2(strip), axis=1)
                known = t

            def along(kind):
                high, low = weight_s[m, kind, 0, half], weight_s[m, kind, 1, half]
                return dot_nn(strip, jnp.concatenate([high, high], axis=0)) + dot_nn(
                    strip, jnp.concatenate([low, low], axis=0)
                )

            wx, wy = side_s[m, :side_rows], side_s[m, side_rows : side_rows + window]
            sx = side_s[m, side_rows + window : 2 * side_rows + window]
            sy = side_s[m, 2 * side_rows + window :]
            value, slope = along(0), along(1)
            value_y = jnp.zeros_like(wy)
            grad_y = jnp.zeros_like(wy)
            slope_y = jnp.zeros_like(wy)
            for x in range(planes):
                here = value[x * window : (x + 1) * window]
                value_y = value_y + wx[x : x + 1] * here
                grad_y = grad_y + sx[x : x + 1] * here
                slope_y = slope_y + wx[x : x + 1] * slope[x * window : (x + 1) * window]
            sums = jnp.concatenate(
                [
                    jnp.sum(one * two, axis=0, keepdims=True)
                    for one, two in ((wy, value_y), (wy, grad_y), (sy, value_y), (wy, slope_y))
                ],
                axis=0,
            )
            if h == 0:
                part_s[m, 0:4] = sums
                continue
            sums = sums + part_s[m, 0:4]
            for k, b in enumerate(pair):
                cut = slice(k * BLOCK, (k + 1) * BLOCK)
                pot[b : b + 1, :] = sums[0:1, cut]
                grad[:, b * BLOCK : (b + 1) * BLOCK] = sums[1:4, cut]

    def finish(h):
        rows = send_rows(h)
        sample(h, inner)
        for copy in rows:
            copy.wait_recv()
        mesh_s[h, :, quarter + 1, :] = edge_land[h, 0]
        mesh_s[h, :, 0, :] = edge_land[h, 1]
        sample(h, outer)

    fills = [functools.partial(fill_weights, m) for m in range(len(atom_chunks))]
    fills += [functools.partial(fill_green, part) for part in range(halves)]
    for i, fill in enumerate(fills):
        fill()
        if i == len(fills) // 2:
            advance(2)
    advance(2)
    for c in range(chunks):
        stage_x(c)
        advance(3)
        if c:
            stage_h(c - 1)
        else:
            advance(3)
        stage_y(2 * c)
        advance(3)
        stage_y(2 * c + 1)
    stage_h(chunks - 1)
    for h in range(2):
        needed = sorted({c for c, _ in strips[16 * h : 16 * (h + 1)]})
        for n, (lo, hi) in enumerate(reversed(cuts)):
            for c in needed:
                if (c, n) in home_h:
                    arrive(home_h.pop((c, n)))
            gather(h, lo, hi)
            if h not in edges and lo <= tiles - 4:
                send_edges(h)
        finish(h)
    for copy in pending:
        copy.wait_send()


def mesh_call(cell, frac, charge, back, table_list, doms, groups):
    slab = back.shape[0]
    quarter = back.shape[1]
    padded_y = quarter + 8
    planes = slab + 2
    tiles = slab // 2
    chunks = G // doms // 8
    atom_chunks = len(chunk_blocks(charge.shape[0]))
    atoms = 2 * BLOCK
    side_rows = 2 * (-(-planes // 8) * 8 + 24)
    dma = pltpu.SemaphoreType.DMA
    dom_shape = pltpu.VMEM((chunks, doms * tiles * 8, BLOCK), F32)
    grp_shape = pltpu.VMEM((2 * chunks, groups, G // groups, 4 * quarter), F32)
    row_shape = pltpu.VMEM((2, planes, G), F32)
    edge_shape = pltpu.VMEM((2, 2, planes, BLOCK), F32)
    args = [cell, frac, charge, back] + [part for table in table_list for part in table]
    return pl.pallas_call(
        mesh_kernel,
        out_shape=[jax.ShapeDtypeStruct(charge.shape, F32), jax.ShapeDtypeStruct(frac.shape, F32)],
        in_specs=[VMEM_SPEC] * len(args),
        out_specs=[VMEM_SPEC] * 2,
        scratch_shapes=[
            pltpu.VMEM((planes, padded_y, G), F32),
            pltpu.VMEM((2, padded_y, G), F32),
            *[row_shape] * 2,
            *[edge_shape] * 2,
            *[dom_shape] * 2,
            *[grp_shape] * 4,
            *[dom_shape] * 2,
            pltpu.VMEM((2 * chunks, 4 * (G // groups), G), F32),
            pltpu.VMEM((atom_chunks, 2, 2, G, atoms), BF),
            pltpu.VMEM((atom_chunks, side_rows, atoms), F32),
            pltpu.VMEM((atom_chunks, 8, atoms), F32),
            pltpu.VMEM((2, planes, padded_y, BLOCK), F32),
            *[dma((6,))] * 4,
            *[dma((chunks, 2, doms - 1))] * 2,
            *[dma((2 * chunks, groups - 1))] * 4,
            *[dma((chunks, 2, doms - 1))] * 2,
            dma((chunks, 2)),
            dma((2 * chunks,)),
            dma((2 * chunks,)),
            dma((chunks, 2)),
        ],
        compiler_params=pltpu.CompilerParams(
            vmem_limit_bytes=VMEM_BYTES, collective_id=0, has_side_effects=True
        ),
    )(*args)


def final_kernel(potential, gradient, energy, charge, site, field):
    site[...] = energy[...] + 0.5 * charge[...] * potential[...]
    field[...] = -gradient[...]


def tables(slab, doms):
    chunks = G // doms // 8
    plain = hartley(np.arange(G))
    z_order = np.array([d * (G // doms) + c * 8 + k for c in range(chunks) for d in range(doms) for k in range(8)])
    hz = hartley(z_order)
    x_points = np.array([slab * d + 2 * t + i for i in range(2) for d in range(doms) for t in tile_order(slab)])
    hx = hartley(x_points)
    return [np_split(t) for t in (hz.T, plain, hx, hx.T)]


def on_device(
    cell_index,
    offsets,
    species,
    pair_blocks,
    counts,
    background,
    species_embed,
    neighbour_embed,
    w_radial,
    w_hidden,
    w_charge,
    w_energy,
):
    atoms = cell_index.shape[1]
    doms = lax.axis_size("dom")
    groups = lax.axis_size("grp")
    ext = share_call(cell_index, offsets, species)
    energies, charges = pair_call(
        pair_blocks,
        counts,
        ext,
        species_embed,
        neighbour_embed,
        w_radial,
        w_hidden,
        w_charge,
        w_energy,
    )

    potential, gradient = mesh_call(
        cell_index, offsets, charges, background, tables(G // doms, doms), doms, groups
    )
    site, field = call(
        final_kernel,
        [jax.ShapeDtypeStruct(energies.shape, F32), jax.ShapeDtypeStruct(gradient.shape, F32)],
        [],
        0,
        (potential, gradient, energies, charges),
    )
    return (site.reshape(atoms), field, charges.reshape(atoms))


def solution(mesh):
    return jax.shard_map(
        on_device,
        mesh=mesh,
        in_specs=(
            P(None, ("grp", "dom")),
            P(None, ("grp", "dom")),
            P(("grp", "dom")),
            P(("grp", "dom"), None),
            P(("grp", "dom")),
            P("dom", "grp", None),
            P(),
            P(),
            P(),
            P(),
            P(),
            P(),
        ),
        out_specs=(P(("grp", "dom")), P(None, ("grp", "dom")), P(("grp", "dom"))),
        check_vma=False,
    )
```

```python
import functools
import math

import jax
import jax.numpy as jnp
import ml_dtypes
import numpy as np
from jax import lax
from jax.experimental import pallas as pl
from jax.experimental.pallas import tpu as pltpu
from jax.sharding import PartitionSpec as P

G = 256
NBASIS = 8
NSPEC = 8
BLOCK = 128
TILES_Y = 4
CUTOFF = 6.0
EWALD = 1.0
VMEM_BYTES = 56 << 20

BF = jnp.bfloat16
F32 = jnp.float32


def np_split(table):
    table = np.asarray(table, np.float32)
    high = table.astype(ml_dtypes.bfloat16)
    low = (table - high.astype(np.float32)).astype(ml_dtypes.bfloat16)
    return high, low


def hartley(points):
    phase = (np.arange(G)[:, None] * np.asarray(points)[None, :]) % G
    angle = phase.astype(np.float64) * (2.0 * math.pi / G)
    return np.cos(angle) + np.sin(angle)


def split2(x):
    high = x.astype(BF)
    low = (x - high.astype(F32)).astype(BF)
    return high, low


def dot_nn(a, b):
    return lax.dot_general(a, b, (((1,), (0,)), ((), ())), preferred_element_type=F32)


def dot_nt(a, b):
    return lax.dot_general(a, b, (((1,), (1,)), ((), ())), preferred_element_type=F32)


def dot3(dot, a, b):
    return dot(a[0], b[0]) + (dot(a[0], b[1]) + dot(a[1], b[0]))


def split3(x):
    one = x.astype(BF).astype(F32)
    two = (x - one).astype(BF).astype(F32)
    three = (x - one - two).astype(BF).astype(F32)
    return one, two, three


def pair_kernel(
    slots,
    live,
    ext,
    radial_w,
    kind_i_w,
    kind_j_w,
    hidden_w,
    charge_w,
    energy_w,
    energy,
    charge,
    wcat,
    whid,
    rank_s,
    theta_s,
    env_s,
    kind_s,
    *,
    step,
):
    blocks = energy.shape[0]
    atoms = ext.shape[1] // 3
    energy[...] = jnp.zeros_like(energy)
    charge[...] = jnp.zeros_like(charge)
    width = hidden_w.shape[0]
    r1, r2, r3 = split3(radial_w[...])
    table = jnp.concatenate(
        [
            *(r1, r2, r3, r1, r2, r1),
            *split3(kind_j_w[...]),
            *split3(kind_i_w[...]),
            jnp.zeros((BLOCK - 12 * NBASIS, width), F32),
        ],
        axis=0,
    )
    wcat[...] = (0.5 * table).T.astype(BF)
    whid[...] = (0.5 * hidden_w[...].astype(F32)).T.astype(BF)

    def spread_row(ref):
        rows = ref[...].astype(F32)
        row = jnp.concatenate([rows[i : i + 1] for i in range(rows.shape[0])], axis=1)
        return jnp.broadcast_to(row, (16, width)).astype(BF)

    wq = spread_row(charge_w)
    we = spread_row(energy_w)
    half = 0.5 * G
    row8 = lax.broadcasted_iota(jnp.int32, (NSPEC, BLOCK), 0).astype(F32)
    sub = lax.broadcasted_iota(jnp.int32, (BLOCK, BLOCK), 0)
    lane = lax.broadcasted_iota(jnp.int32, (BLOCK, BLOCK), 1)
    earlier = (lane < sub).astype(F32).astype(BF)
    spare = jnp.zeros((BLOCK - 12 * NBASIS, BLOCK), F32)

    def slot_body(slot, unused):
        bi = slots[0, slot]
        bj = slots[1, slot]
        ri = ext[:, pl.ds(pl.multiple_of(atoms + bi * BLOCK, BLOCK), BLOCK)]
        rj = ext[:, pl.ds(pl.multiple_of(bj * BLOCK, BLOCK), BLOCK)]
        total = jnp.zeros((BLOCK, BLOCK), F32)
        for c in range(3):
            sep = jnp.broadcast_to(rj[c : c + 1, :], (BLOCK, BLOCK)).T - ri[c : c + 1, :]
            sep = jnp.where(sep > half, sep - G, jnp.where(sep < -half, sep + G, sep))
            total = total + sep * sep
        scaled = jnp.sqrt(total) / CUTOFF
        inside = 1.0 - scaled * scaled
        env = jnp.where(scaled < 1.0, inside * inside, 0.0)
        env = jnp.where((sub == lane) & (bj == blocks + bi), 0.0, env)
        used = (env > 0.0).astype(F32)
        rank_s[...] = jnp.where(env > 0.0, dot_nn(earlier, used.astype(BF)), -1.0)
        theta_s[...] = math.pi * jnp.minimum(scaled, 1.0)
        env_s[...] = env
        kind_s[...] = jnp.broadcast_to(rj[3:4, :], (BLOCK, BLOCK)).T
        most = jnp.max(jnp.sum(used, axis=0, keepdims=True)).astype(jnp.int32)
        kind_i = (row8 == ri[3:4, :]).astype(F32)

        def rows_body(it, sums):
            energy_sum, charge_sum = sums
            rank = rank_s[...]
            parts = []
            envs = []
            for k in range(step):
                pick = rank == (it * step + k).astype(F32)
                theta = jnp.sum(jnp.where(pick, theta_s[...], 0.0), axis=0, keepdims=True)
                kind = jnp.sum(jnp.where(pick, kind_s[...], 0.0), axis=0, keepdims=True)
                envs.append(jnp.sum(jnp.where(pick, env_s[...], 0.0), axis=0, keepdims=True))
                phase = theta * (row8 + 1.0)
                small = phase == 0.0
                rad = jnp.where(small, 1.0, jnp.sin(phase) / jnp.where(small, 1.0, phase))
                one, two, three = split3(rad)
                kind_j = (row8 == kind).astype(F32)
                parts.append(
                    jnp.concatenate(
                        [
                            *(one, one, one, two, two, three),
                            *(kind_j, kind_j, kind_j, kind_i, kind_i, kind_i),
                            spare,
                        ],
                        axis=0,
                    ).astype(BF)
                )
            feats = jnp.concatenate(parts, axis=1)
            h = dot_nn(wcat[...], feats)
            edge = (h + h * jnp.tanh(h)).astype(BF)
            cp = dot_nn(wq, edge)
            g = dot_nn(whid[...], edge)
            latent = (g + g * jnp.tanh(g)).astype(BF)
            ep = dot_nn(we, latent)
            for k in range(step):
                cut = slice(k * BLOCK, (k + 1) * BLOCK)
                charge_sum = charge_sum + envs[k] * cp[0:1, cut]
                energy_sum = energy_sum + envs[k] * ep[0:1, cut]
            return energy_sum, charge_sum

        zero = jnp.zeros((1, BLOCK), F32)
        energy_sum, charge_sum = lax.fori_loop(
            0, (most + step - 1) // step, rows_body, (zero, zero)
        )
        where = pl.ds(bi, 1)
        charge[where, :] = charge[where, :] + charge_sum
        energy[where, :] = energy[where, :] + energy_sum
        return unused

    lax.fori_loop(0, live[0], slot_body, 0)


def spline_rows(rows, first, center, frac, wrap, slopes):
    index = lax.broadcasted_iota(jnp.int32, (rows, frac.shape[1]), 0) + first
    if slopes:
        values = (frac - 0.5, -2.0 * frac, 0.5 + frac)
    else:
        values = ((0.5 - frac) * (0.5 - frac) * 0.5, 0.75 - frac * frac, (0.5 + frac) * (0.5 + frac) * 0.5)
    out = jnp.zeros((rows, frac.shape[1]), F32)
    for o in range(3):
        target = center + (o - 1)
        if wrap:
            target = jnp.where(target < 0, target + G, jnp.where(target >= G, target - G, target))
        out = jnp.where(index == target, values[o], out)
    return out


def chunk_blocks(blocks):
    per_tile = blocks // TILES_Y
    return [
        (t, [t + TILES_Y * z for z in range(2 * pair, 2 * pair + 2)])
        for t in range(TILES_Y)
        for pair in range(per_tile // 2)
    ]


def lanes_of(ref, row, pair):
    return jnp.concatenate([ref[row : row + 1, b * BLOCK : (b + 1) * BLOCK] for b in pair], axis=1)


def rows_of(ref, pair):
    return jnp.concatenate([ref[b : b + 1, :] for b in pair], axis=1)


def swap_blocks(arrays):
    arrays = list(arrays)
    count = len(arrays)
    width = BLOCK // count
    lane = lax.broadcasted_iota(jnp.int32, arrays[0].shape, arrays[0].ndim - 1)
    bit = 1
    while bit < count:
        upper = (lane // (width * bit)) % 2 == 1
        for i in range(count):
            if i & bit:
                continue
            low, high = arrays[i], arrays[i | bit]
            arrays[i] = jnp.where(upper, pltpu.roll(high, width * bit, low.ndim - 1), low)
            arrays[i | bit] = jnp.where(upper, high, pltpu.roll(low, BLOCK - width * bit, low.ndim - 1))
        bit *= 2
    return arrays


VMEM_SPEC = pl.BlockSpec(memory_space=pltpu.VMEM)
SMEM_SPEC = pl.BlockSpec(memory_space=pltpu.SMEM)


def call(body, outs, scratch, scalars, args):
    specs = [SMEM_SPEC] * scalars + [VMEM_SPEC] * (len(args) - scalars)
    many = isinstance(outs, (list, tuple))
    return pl.pallas_call(
        body,
        out_shape=outs,
        in_specs=specs,
        out_specs=[VMEM_SPEC] * len(outs) if many else VMEM_SPEC,
        scratch_shapes=scratch,
        compiler_params=pltpu.CompilerParams(vmem_limit_bytes=VMEM_BYTES),
    )(*args)


def share_kernel(cell, frac, kind, ext, sends, recvs):
    atoms = cell.shape[1]
    doms = lax.axis_size("dom")
    me = lax.axis_index("dom")
    mesh_ids = pl.DeviceIdType.MESH
    left, right = lax.rem(me + doms - 1, doms), lax.rem(me + 1, doms)
    barrier = pltpu.get_barrier_semaphore()
    for side in (left, right):
        pl.semaphore_signal(barrier, inc=1, device_id={"dom": side}, device_id_type=mesh_ids)
    own = pl.ds(atoms, atoms)
    ext[0:3, own] = cell[...].astype(F32) + frac[...]
    ext[3:4, own] = kind[...].astype(F32)
    pl.semaphore_wait(barrier, 2)
    copies = []
    for i, (side, slot) in enumerate(((left, 2), (right, 0))):
        copy = pltpu.make_async_remote_copy(
            src_ref=ext.at[:, own],
            dst_ref=ext.at[:, pl.ds(slot * atoms, atoms)],
            send_sem=sends.at[i],
            recv_sem=recvs.at[i],
            device_id={"dom": side},
            device_id_type=mesh_ids,
        )
        copy.start()
        copies.append(copy)
    for copy in copies:
        copy.wait()


def share_call(cell, frac, kind):
    return pl.pallas_call(
        share_kernel,
        out_shape=jax.ShapeDtypeStruct((4, 3 * cell.shape[1]), F32),
        in_specs=[VMEM_SPEC] * 3,
        out_specs=VMEM_SPEC,
        scratch_shapes=[pltpu.SemaphoreType.DMA((2,))] * 2,
        compiler_params=pltpu.CompilerParams(
            vmem_limit_bytes=VMEM_BYTES, collective_id=1, has_side_effects=True
        ),
    )(cell, frac, kind[None, :])


def pair_call(
    pair_blocks, counts, ext, species_embed, neighbour_embed, w_radial, w_hidden, w_charge, w_energy
):
    blocks = ext.shape[1] // (3 * BLOCK)
    width = w_charge.shape[0]
    shape = jax.ShapeDtypeStruct((blocks, BLOCK), F32)
    square = pltpu.VMEM((BLOCK, BLOCK), F32)
    return call(
        functools.partial(pair_kernel, step=4),
        [shape, shape],
        [
            pltpu.VMEM((width, BLOCK), BF),
            pltpu.VMEM((width, width), BF),
            *[square] * 4,
        ],
        2,
        (
            pair_blocks.T,
            counts,
            ext,
            w_radial,
            species_embed,
            neighbour_embed,
            w_hidden,
            w_charge.reshape(-1, BLOCK),
            w_energy.reshape(-1, BLOCK),
        ),
    )


def tile_order(slab):
    quads = slab // 4
    order = list(range(1, quads - 1)) + [0, quads - 1]
    return [2 * q + half for q in order for half in range(2)]


def tile_cuts(tiles):
    return [(0, tiles // 2), (tiles // 2, tiles)]


def mesh_kernel(
    cell,
    frac,
    charge,
    *refs,
):
    sources, (pot, grad, acc, back, table_s, lsem), refs = refs[:9], refs[9:15], refs[15:]
    (
        halo,
        row_send,
        row_land,
        edge_send,
        edge_land,
        ready_x,
        land_x,
        ready_y,
        land_y,
        ready_b,
        land_b,
        ready_h,
        land_h,
        green_s,
        weight_s,
        side_s,
        part_s,
        mesh_s,
        hsend,
        hrecv,
        rsend,
        rrecv,
        send_x,
        recv_x,
        send_y,
        recv_y,
        send_b,
        recv_b,
        send_h,
        recv_h,
        loc_x,
        loc_y,
        loc_b,
        loc_h,
    ) = refs
    halves, groups, cols, wide = ready_y.shape
    chunks = halves // 2
    doms = lax.axis_size("dom")
    slab = G // doms
    planes = slab + 2
    quarter = G // groups
    tiles = slab // 2
    tile = quarter // TILES_Y
    window = 24
    lines = doms * tiles
    order = tile_order(slab)
    strips = [divmod(i, doms) for i in range(G // 8)]
    me_g, me_d = lax.axis_index("grp"), lax.axis_index("dom")
    mesh_ids = pl.DeviceIdType.MESH
    barrier = pltpu.get_barrier_semaphore()
    order_g = sorted(range(1, groups), key=lambda k: abs(k - groups // 2))
    order_d = sorted(range(1, doms), key=lambda k: abs(k - doms // 2))
    for h in range(2):
        for base in (0, quarter):
            mesh_s[h, :, base : base + 8, :] = jnp.zeros((planes, 8, BLOCK), F32)
    for axis, me, peers, count in (("grp", me_g, order_g, groups), ("dom", me_d, order_d, doms)):
        for k in peers:
            pl.semaphore_signal(
                barrier, inc=1, device_id={axis: lax.rem(me + k, count)}, device_id_type=mesh_ids
            )

    pending = []

    def remote(src, dst, send_sem, recv_sem, axis, peer):
        copy = pltpu.make_async_remote_copy(
            src_ref=src,
            dst_ref=dst,
            send_sem=send_sem,
            recv_sem=recv_sem,
            device_id={axis: peer},
            device_id_type=mesh_ids,
        )
        copy.start()
        pending.append(copy)
        return copy

    def local_copy(src, dst, sem):
        copy = pltpu.make_async_copy(src, dst, sem)
        copy.start()
        return copy

    loads = [
        local_copy(source, back if i == 0 else table_s.at[i - 1], lsem.at[i]) for i, source in enumerate(sources)
    ]

    def arrive(entry):
        own, copies = entry
        own.wait()
        for copy in copies:
            copy.wait_recv()

    def to_sides(axis, me, count, low, high, low_dst, high_dst, sends, recvs, base):
        before, after = lax.rem(me + count - 1, count), lax.rem(me + 1, count)
        return [
            remote(low, low_dst, sends.at[base], recvs.at[base], axis, before),
            remote(high, high_dst, sends.at[base + 1], recvs.at[base + 1], axis, after),
        ]

    offset_x = 1 - slab * me_d
    offset_y = 1 - quarter * me_g
    atom_chunks = chunk_blocks(charge.shape[0])
    outer = [m for m, (t, _) in enumerate(atom_chunks) if t in (0, TILES_Y - 1)]
    inner = [m for m in range(len(atom_chunks)) if m not in outer]

    def atoms_of(m):
        t, pair = atom_chunks[m]
        local = [
            lanes_of(cell, 0, pair) + offset_x,
            lanes_of(cell, 1, pair) + offset_y,
            lanes_of(cell, 2, pair),
        ]
        return t, pair, local, [lanes_of(frac, axis, pair) for axis in range(3)]

    acc[...] = jnp.zeros_like(acc)

    def spread(m):
        t, pair, local, f = atoms_of(m)
        wx = spline_rows(planes, 0, local[0], f[0], False, False)
        wy = spline_rows(window, tile * t, local[1], f[1], False, False)
        wz = spline_rows(G, 0, local[2], f[2], True, False)
        wy = wy * rows_of(charge, pair)
        mix = jnp.concatenate([wx[x : x + 1, :] * wy for x in range(planes)], axis=0)
        part = dot3(dot_nt, split2(mix), split2(wz))
        acc[:, tile * t : tile * t + window, :] += part.reshape(planes, window, G)

    for m in outer:
        spread(m)
    row_send[0] = acc[:, 0, :]
    row_send[1] = acc[:, quarter + 1, :]
    pl.semaphore_wait(barrier, groups + doms - 2)
    rows = to_sides(
        "grp", me_g, groups, row_send.at[0], row_send.at[1], row_land.at[0], row_land.at[1], rsend, rrecv, 0
    )
    for m in inner:
        spread(m)
    for copy in rows:
        copy.wait_recv()
    acc[:, quarter, :] = acc[:, quarter, :] + row_land[0]
    acc[:, 1, :] = acc[:, 1, :] + row_land[1]
    border = to_sides(
        "dom", me_d, doms, acc.at[0], acc.at[slab + 1], halo.at[0], halo.at[1], hsend, hrecv, 0
    )
    for load in loads:
        load.wait()
    table_z = (table_s[0], table_s[1])

    def transform_z(j):
        base = 1 + 2 * order[j]
        values = acc[base : base + 4, 1 : quarter + 1, :] + back[base - 1 : base + 3]
        spec = dot3(dot_nt, table_z, split2(values.reshape(4 * quarter, G)))
        for c in range(chunks):
            for d in range(doms):
                row = 8 * (c * doms + d)
                for i in range(2):
                    ready_x[c, pl.ds((d * tiles + j + i) * 8, 8)] = spec[
                        row : row + 8, i * BLOCK : (i + 1) * BLOCK
                    ]

    def exchange_dom(src, dst, c, n, cut, send_sem, recv_sem, loc):
        lo, hi = cut

        def at(d):
            return pl.ds((d * tiles + lo) * 8, (hi - lo) * 8)

        copies = []
        for k in order_d:
            peer = lax.rem(me_d + k, doms)
            copies.append(
                remote(
                    src.at[c, at(peer)],
                    dst.at[c, at(me_d)],
                    send_sem.at[c, n, k - 1],
                    recv_sem.at[c, n, k - 1],
                    "dom",
                    peer,
                )
            )
        return local_copy(src.at[c, at(me_d)], dst.at[c, at(me_d)], loc.at[c, n]), copies

    def exchange_grp(src, dst, c, send_sem, recv_sem, loc):
        copies = []
        for k in order_g:
            peer = lax.rem(me_g + k, groups)
            copies.append(
                remote(
                    src.at[c, peer], dst.at[c, me_g], send_sem.at[c, k - 1], recv_sem.at[c, k - 1], "grp", peer
                )
            )
        return local_copy(src.at[c, me_g], dst.at[c, me_g], loc.at[c]), copies

    cuts = tile_cuts(tiles)
    pieces = [(c, n) for c in range(chunks) for n in range(2)]
    out_x = {}
    left_out = set()

    def send_out(c, n):
        out_x[c, n] = exchange_dom(ready_x, land_x, c, n, cuts[n], send_x, recv_x, loc_x)

    def advance(depth):
        at = len(out_x)
        if at == len(pieces):
            return
        done = [] if at - depth in left_out else out_x[pieces[at - depth]][1]
        left_out.add(at - depth)
        for copy in done:
            copy.wait_send()
        pending[:] = [other for other in pending if all(other is not copy for copy in done)]
        send_out(*pieces[at])

    joined = False
    for n, (lo, hi) in enumerate(cuts):
        if hi > tiles - 4 and not joined:
            for copy in border:
                copy.wait_recv()
            acc[1] = acc[1] + halo[1]
            acc[slab] = acc[slab] + halo[0]
            joined = True
        for j in range(lo, hi, 2):
            transform_z(j)
        send_out(0, n)

    unit = 2.0 * math.pi / G * (2.0 * math.pi / G)
    shape = (4 * cols, G)

    def signed(m):
        return jnp.where(m < G // 2, m, m - G)

    row_id = lax.broadcasted_iota(jnp.int32, shape, 0)
    my = signed(lax.broadcasted_iota(jnp.int32, shape, 1))

    def fill_green(part):
        mz = signed(me_d * (G // doms) + part * 4 + row_id // cols)
        mx = signed(me_g * cols + row_id % cols)
        squares = mx * mx + my * my + mz * mz
        wave = squares.astype(F32) * unit
        safe = jnp.where(squares > 0, wave, 1.0)
        green_s[part] = jnp.where(
            squares > 0, 4.0 * math.pi * jnp.exp(-wave / (4.0 * EWALD * EWALD)) / safe, 0.0
        ) * (1.0 / (G * G * G))

    side_rows = side_s.shape[1] // 2 - window

    def fill_weights(m):
        t, pair, local, f = atoms_of(m)
        for kind in range(2):
            wz = spline_rows(G, 0, local[2], f[2], True, kind == 1)
            high, low = split2(dot3(dot_nn, table_z, split2(wz)))
            weight_s[m, kind, 0] = high
            weight_s[m, kind, 1] = low
            base = kind * (side_rows + window)
            side_s[m, base : base + side_rows] = spline_rows(side_rows, 0, local[0], f[0], False, kind == 1)
            side_s[m, base + side_rows : base + side_rows + window] = spline_rows(
                window, tile * t, local[1], f[1], False, kind == 1
            )

    table_y = (table_s[2], table_s[3])
    forward_x = (table_s[4], table_s[5])
    back_x = (table_s[6], table_s[7])
    out_y, home_b, home_h = {}, {}, {}

    def stage_x(c):
        for n in range(2):
            arrive(out_x[c, n])
        for two in range(2):
            parts = []
            for kp in (2 * two, 2 * two + 1):
                loaded = [land_x[c, pl.ds(2 * kp + i, lines, stride=8), :] for i in range(2)]
                parts.append(jnp.concatenate(swap_blocks(loaded), axis=0))
            result = dot3(dot_nn, forward_x, split2(jnp.concatenate(parts, axis=1)))
            part = 2 * c + two
            for g in range(groups):
                ready_y[part, g] = result[g * cols : (g + 1) * cols]
            out_y[part] = exchange_grp(ready_y, land_y, part, send_y, recv_y, loc_y)

    def stage_y(part):
        arrive(out_y[part])
        rows = []
        for kp in range(2):
            cut = slice(kp * BLOCK, (kp + 1) * BLOCK)
            pairs = [
                swap_blocks([land_y[part, g, :, cut], land_y[part, g + 1, :, cut]])
                for g in range(0, groups, 2)
            ]
            for i in range(2):
                rows.append(jnp.concatenate([pair[i] for pair in pairs], axis=1))
        spectrum = dot3(dot_nn, split2(jnp.concatenate(rows, axis=0)), table_y) * green_s[part]
        result = dot3(dot_nn, split2(spectrum), table_y)
        for kp in range(2):
            for g in range(0, groups, 2):
                cut = slice(g * quarter, (g + 2) * quarter)
                both = [result[(2 * kp + i) * cols : (2 * kp + i + 1) * cols, cut] for i in range(2)]
                for i, piece in enumerate(swap_blocks(both)):
                    ready_b[part, g + i, :, kp * BLOCK : (kp + 1) * BLOCK] = piece
        home_b[part] = exchange_grp(ready_b, land_b, part, send_b, recv_b, loc_b)

    def stage_h(c):
        for two in range(2):
            arrive(home_b[2 * c + two])
            column = jnp.concatenate([land_b[2 * c + two, g] for g in range(groups)], axis=0)
            result = dot3(dot_nn, back_x, split2(column))
            for i in range(2):
                cut = slice(i * BLOCK, (i + 1) * BLOCK)
                both = swap_blocks([result[:lines, cut], result[lines:, cut]])
                for k, piece in enumerate(both):
                    ready_h[c, pl.ds(2 * (2 * two + i) + k, lines, stride=8), :] = piece
        for n, cut in enumerate(reversed(cuts)):
            home_h[c, n] = exchange_dom(ready_h, land_h, c, n, cut, send_h, recv_h, loc_h)

    edges = {}

    def gather(h, lo, hi):
        for j in range(lo, hi):
            block = jnp.concatenate(
                [land_h[c, pl.ds((d * tiles + j) * 8, 8)] for c, d in strips[16 * h : 16 * (h + 1)]],
                axis=0,
            )
            turned = block.T
            base = 1 + 2 * order[j]
            for i in range(2):
                mesh_s[h, base + i, 1 : quarter + 1, :] = turned[i * quarter : (i + 1) * quarter]

    def send_edges(h):
        edges[h] = to_sides(
            "dom",
            me_d,
            doms,
            mesh_s.at[h, 1],
            mesh_s.at[h, slab],
            mesh_s.at[h, slab + 1],
            mesh_s.at[h, 0],
            hsend,
            hrecv,
            2 + 2 * h,
        )

    def send_rows(h):
        for copy in edges[h]:
            copy.wait()
            pending[:] = [other for other in pending if other is not copy]
        edge_send[h, 0] = mesh_s[h, :, 1, :]
        edge_send[h, 1] = mesh_s[h, :, quarter, :]
        return to_sides(
            "grp",
            me_g,
            groups,
            edge_send.at[h, 0],
            edge_send.at[h, 1],
            edge_land.at[h, 0],
            edge_land.at[h, 1],
            rsend,
            rrecv,
            2 + 2 * h,
        )

    def sample(h, chosen):
        half = slice(h * BLOCK, (h + 1) * BLOCK)
        known = None
        for m in chosen:
            t, pair = atom_chunks[m]
            if t != known:
                strip = mesh_s[h, :, tile * t : tile * t + window, :].reshape(planes * window, BLOCK)
                strip = jnp.concatenate(split2(strip), axis=1)
                known = t

            def along(kind):
                high, low = weight_s[m, kind, 0, half], weight_s[m, kind, 1, half]
                return dot_nn(strip, jnp.concatenate([high, high], axis=0)) + dot_nn(
                    strip, jnp.concatenate([low, low], axis=0)
                )

            wx, wy = side_s[m, :side_rows], side_s[m, side_rows : side_rows + window]
            sx = side_s[m, side_rows + window : 2 * side_rows + window]
            sy = side_s[m, 2 * side_rows + window :]
            value, slope = along(0), along(1)
            value_y = jnp.zeros_like(wy)
            grad_y = jnp.zeros_like(wy)
            slope_y = jnp.zeros_like(wy)
            for x in range(planes):
                here = value[x * window : (x + 1) * window]
                value_y = value_y + wx[x : x + 1] * here
                grad_y = grad_y + sx[x : x + 1] * here
                slope_y = slope_y + wx[x : x + 1] * slope[x * window : (x + 1) * window]
            sums = jnp.concatenate(
                [
                    jnp.sum(one * two, axis=0, keepdims=True)
                    for one, two in ((wy, value_y), (wy, grad_y), (sy, value_y), (wy, slope_y))
                ],
                axis=0,
            )
            if h == 0:
                part_s[m, 0:4] = sums
                continue
            sums = sums + part_s[m, 0:4]
            for k, b in enumerate(pair):
                cut = slice(k * BLOCK, (k + 1) * BLOCK)
                pot[b : b + 1, :] = sums[0:1, cut]
                grad[:, b * BLOCK : (b + 1) * BLOCK] = sums[1:4, cut]

    def finish(h):
        rows = send_rows(h)
        sample(h, inner)
        for copy in rows:
            copy.wait_recv()
        mesh_s[h, :, quarter + 1, :] = edge_land[h, 0]
        mesh_s[h, :, 0, :] = edge_land[h, 1]
        sample(h, outer)

    fills = [functools.partial(fill_weights, m) for m in range(len(atom_chunks))]
    fills += [functools.partial(fill_green, part) for part in range(halves)]
    for i, fill in enumerate(fills):
        fill()
        if i == len(fills) // 2:
            advance(2)
    advance(2)
    for c in range(chunks):
        stage_x(c)
        advance(3)
        if c:
            stage_h(c - 1)
        else:
            advance(3)
        stage_y(2 * c)
        advance(3)
        stage_y(2 * c + 1)
    stage_h(chunks - 1)
    for h in range(2):
        needed = sorted({c for c, _ in strips[16 * h : 16 * (h + 1)]})
        for n, (lo, hi) in enumerate(reversed(cuts)):
            for c in needed:
                if (c, n) in home_h:
                    arrive(home_h.pop((c, n)))
            gather(h, lo, hi)
            if h not in edges and lo <= tiles - 4:
                send_edges(h)
        finish(h)
    for copy in pending:
        copy.wait_send()


def mesh_call(cell, frac, charge, back, table_list, doms, groups):
    slab = back.shape[0]
    quarter = back.shape[1]
    padded_y = quarter + 8
    planes = slab + 2
    tiles = slab // 2
    chunks = G // doms // 8
    atom_chunks = len(chunk_blocks(charge.shape[0]))
    atoms = 2 * BLOCK
    side_rows = 2 * (-(-planes // 8) * 8 + 24)
    dma = pltpu.SemaphoreType.DMA
    dom_shape = pltpu.VMEM((chunks, doms * tiles * 8, BLOCK), F32)
    grp_shape = pltpu.VMEM((2 * chunks, groups, G // groups, 4 * quarter), F32)
    row_shape = pltpu.VMEM((2, planes, G), F32)
    edge_shape = pltpu.VMEM((2, 2, planes, BLOCK), F32)
    args = [cell, frac, charge, back] + [part for table in table_list for part in table]
    return pl.pallas_call(
        mesh_kernel,
        out_shape=[jax.ShapeDtypeStruct(charge.shape, F32), jax.ShapeDtypeStruct(frac.shape, F32)],
        in_specs=[VMEM_SPEC] * 3 + [pl.BlockSpec(memory_space=pl.ANY)] * (len(args) - 3),
        out_specs=[VMEM_SPEC] * 2,
        scratch_shapes=[
            pltpu.VMEM((planes, padded_y, G), F32),
            pltpu.VMEM(back.shape, F32),
            pltpu.VMEM((8, G, G), BF),
            dma((9,)),
            pltpu.VMEM((2, padded_y, G), F32),
            *[row_shape] * 2,
            *[edge_shape] * 2,
            *[dom_shape] * 2,
            *[grp_shape] * 4,
            *[dom_shape] * 2,
            pltpu.VMEM((2 * chunks, 4 * (G // groups), G), F32),
            pltpu.VMEM((atom_chunks, 2, 2, G, atoms), BF),
            pltpu.VMEM((atom_chunks, side_rows, atoms), F32),
            pltpu.VMEM((atom_chunks, 8, atoms), F32),
            pltpu.VMEM((2, planes, padded_y, BLOCK), F32),
            *[dma((6,))] * 4,
            *[dma((chunks, 2, doms - 1))] * 2,
            *[dma((2 * chunks, groups - 1))] * 4,
            *[dma((chunks, 2, doms - 1))] * 2,
            dma((chunks, 2)),
            dma((2 * chunks,)),
            dma((2 * chunks,)),
            dma((chunks, 2)),
        ],
        compiler_params=pltpu.CompilerParams(
            vmem_limit_bytes=VMEM_BYTES, collective_id=0, has_side_effects=True
        ),
    )(*args)


def final_kernel(potential, gradient, energy, charge, site, field):
    site[...] = energy[...] + 0.5 * charge[...] * potential[...]
    field[...] = -gradient[...]


def tables(slab, doms):
    chunks = G // doms // 8
    plain = hartley(np.arange(G))
    z_order = np.array([d * (G // doms) + c * 8 + k for c in range(chunks) for d in range(doms) for k in range(8)])
    hz = hartley(z_order)
    x_points = np.array([slab * d + 2 * t + i for i in range(2) for d in range(doms) for t in tile_order(slab)])
    hx = hartley(x_points)
    return [np_split(t) for t in (hz.T, plain, hx, hx.T)]


def on_device(
    cell_index,
    offsets,
    species,
    pair_blocks,
    counts,
    background,
    species_embed,
    neighbour_embed,
    w_radial,
    w_hidden,
    w_charge,
    w_energy,
):
    atoms = cell_index.shape[1]
    doms = lax.axis_size("dom")
    groups = lax.axis_size("grp")
    ext = share_call(cell_index, offsets, species)
    energies, charges = pair_call(
        pair_blocks,
        counts,
        ext,
        species_embed,
        neighbour_embed,
        w_radial,
        w_hidden,
        w_charge,
        w_energy,
    )

    potential, gradient = mesh_call(
        cell_index, offsets, charges, background, tables(G // doms, doms), doms, groups
    )
    site, field = call(
        final_kernel,
        [jax.ShapeDtypeStruct(energies.shape, F32), jax.ShapeDtypeStruct(gradient.shape, F32)],
        [],
        0,
        (potential, gradient, energies, charges),
    )
    return (site.reshape(atoms), field, charges.reshape(atoms))


def solution(mesh):
    return jax.shard_map(
        on_device,
        mesh=mesh,
        in_specs=(
            P(None, ("grp", "dom")),
            P(None, ("grp", "dom")),
            P(("grp", "dom")),
            P(("grp", "dom"), None),
            P(("grp", "dom")),
            P("dom", "grp", None),
            P(),
            P(),
            P(),
            P(),
            P(),
            P(),
        ),
        out_specs=(P(("grp", "dom")), P(None, ("grp", "dom")), P(("grp", "dom"))),
        check_vma=False,
    )
```

```python
import functools
import math

import jax
import jax.numpy as jnp
import ml_dtypes
import numpy as np
from jax import lax
from jax.experimental import pallas as pl
from jax.experimental.pallas import tpu as pltpu
from jax.sharding import PartitionSpec as P

G = 256
NBASIS = 8
NSPEC = 8
BLOCK = 128
TILES_Y = 4
CUTOFF = 6.0
EWALD = 1.0
VMEM_BYTES = 56 << 20

BF = jnp.bfloat16
F32 = jnp.float32


def np_split(table):
    table = np.asarray(table, np.float32)
    high = table.astype(ml_dtypes.bfloat16)
    low = (table - high.astype(np.float32)).astype(ml_dtypes.bfloat16)
    return high, low


def hartley(points):
    phase = (np.arange(G)[:, None] * np.asarray(points)[None, :]) % G
    angle = phase.astype(np.float64) * (2.0 * math.pi / G)
    return np.cos(angle) + np.sin(angle)


def split2(x):
    high = x.astype(BF)
    low = (x - high.astype(F32)).astype(BF)
    return high, low


def dot_nn(a, b):
    return lax.dot_general(a, b, (((1,), (0,)), ((), ())), preferred_element_type=F32)


def dot_nt(a, b):
    return lax.dot_general(a, b, (((1,), (1,)), ((), ())), preferred_element_type=F32)


def dot3(dot, a, b):
    return dot(a[0], b[0]) + (dot(a[0], b[1]) + dot(a[1], b[0]))


def split3(x):
    one = x.astype(BF).astype(F32)
    two = (x - one).astype(BF).astype(F32)
    three = (x - one - two).astype(BF).astype(F32)
    return one, two, three


def pair_kernel(
    slots,
    live,
    ext,
    radial_w,
    kind_i_w,
    kind_j_w,
    hidden_w,
    charge_w,
    energy_w,
    energy,
    charge,
    wcat,
    whid,
    rank_s,
    theta_s,
    env_s,
    kind_s,
    *,
    step,
):
    blocks = energy.shape[0]
    atoms = ext.shape[1] // 3
    energy[...] = jnp.zeros_like(energy)
    charge[...] = jnp.zeros_like(charge)
    width = hidden_w.shape[0]
    r1, r2, r3 = split3(radial_w[...])
    table = jnp.concatenate(
        [
            *(r1, r2, r3, r1, r2, r1),
            *split3(kind_j_w[...]),
            *split3(kind_i_w[...]),
            jnp.zeros((BLOCK - 12 * NBASIS, width), F32),
        ],
        axis=0,
    )
    wcat[...] = (0.5 * table).T.astype(BF)
    whid[...] = (0.5 * hidden_w[...].astype(F32)).T.astype(BF)

    def spread_row(ref):
        rows = ref[...].astype(F32)
        row = jnp.concatenate([rows[i : i + 1] for i in range(rows.shape[0])], axis=1)
        return jnp.broadcast_to(row, (16, width)).astype(BF)

    wq = spread_row(charge_w)
    we = spread_row(energy_w)
    half = 0.5 * G
    row8 = lax.broadcasted_iota(jnp.int32, (NSPEC, BLOCK), 0).astype(F32)
    sub = lax.broadcasted_iota(jnp.int32, (BLOCK, BLOCK), 0)
    lane = lax.broadcasted_iota(jnp.int32, (BLOCK, BLOCK), 1)
    earlier = (lane < sub).astype(F32).astype(BF)
    spare = jnp.zeros((BLOCK - 12 * NBASIS, BLOCK), F32)

    def slot_body(slot, unused):
        bi = slots[0, slot]
        bj = slots[1, slot]
        ri = ext[:, pl.ds(pl.multiple_of(atoms + bi * BLOCK, BLOCK), BLOCK)]
        rj = ext[:, pl.ds(pl.multiple_of(bj * BLOCK, BLOCK), BLOCK)]
        total = jnp.zeros((BLOCK, BLOCK), F32)
        for c in range(3):
            sep = jnp.broadcast_to(rj[c : c + 1, :], (BLOCK, BLOCK)).T - ri[c : c + 1, :]
            sep = jnp.where(sep > half, sep - G, jnp.where(sep < -half, sep + G, sep))
            total = total + sep * sep
        scaled = jnp.sqrt(total) / CUTOFF
        inside = 1.0 - scaled * scaled
        env = jnp.where(scaled < 1.0, inside * inside, 0.0)
        env = jnp.where((sub == lane) & (bj == blocks + bi), 0.0, env)
        used = (env > 0.0).astype(F32)
        rank_s[...] = jnp.where(env > 0.0, dot_nn(earlier, used.astype(BF)), -1.0)
        theta_s[...] = math.pi * jnp.minimum(scaled, 1.0)
        env_s[...] = env
        kind_s[...] = jnp.broadcast_to(rj[3:4, :], (BLOCK, BLOCK)).T
        most = jnp.max(jnp.sum(used, axis=0, keepdims=True)).astype(jnp.int32)
        kind_i = (row8 == ri[3:4, :]).astype(F32)

        def rows_body(it, sums):
            energy_sum, charge_sum = sums
            rank = rank_s[...]
            parts = []
            envs = []
            for k in range(step):
                pick = rank == (it * step + k).astype(F32)
                theta = jnp.sum(jnp.where(pick, theta_s[...], 0.0), axis=0, keepdims=True)
                kind = jnp.sum(jnp.where(pick, kind_s[...], 0.0), axis=0, keepdims=True)
                envs.append(jnp.sum(jnp.where(pick, env_s[...], 0.0), axis=0, keepdims=True))
                phase = theta * (row8 + 1.0)
                small = phase == 0.0
                rad = jnp.where(small, 1.0, jnp.sin(phase) / jnp.where(small, 1.0, phase))
                one, two, three = split3(rad)
                kind_j = (row8 == kind).astype(F32)
                parts.append(
                    jnp.concatenate(
                        [
                            *(one, one, one, two, two, three),
                            *(kind_j, kind_j, kind_j, kind_i, kind_i, kind_i),
                            spare,
                        ],
                        axis=0,
                    ).astype(BF)
                )
            feats = jnp.concatenate(parts, axis=1)
            h = dot_nn(wcat[...], feats)
            edge = (h + h * jnp.tanh(h)).astype(BF)
            cp = dot_nn(wq, edge)
            g = dot_nn(whid[...], edge)
            latent = (g + g * jnp.tanh(g)).astype(BF)
            ep = dot_nn(we, latent)
            for k in range(step):
                cut = slice(k * BLOCK, (k + 1) * BLOCK)
                charge_sum = charge_sum + envs[k] * cp[0:1, cut]
                energy_sum = energy_sum + envs[k] * ep[0:1, cut]
            return energy_sum, charge_sum

        zero = jnp.zeros((1, BLOCK), F32)
        energy_sum, charge_sum = lax.fori_loop(
            0, (most + step - 1) // step, rows_body, (zero, zero)
        )
        where = pl.ds(bi, 1)
        charge[where, :] = charge[where, :] + charge_sum
        energy[where, :] = energy[where, :] + energy_sum
        return unused

    lax.fori_loop(0, live[0], slot_body, 0)


def spline_rows(rows, first, center, frac, wrap, slopes):
    index = lax.broadcasted_iota(jnp.int32, (rows, frac.shape[1]), 0) + first
    if slopes:
        values = (frac - 0.5, -2.0 * frac, 0.5 + frac)
    else:
        values = ((0.5 - frac) * (0.5 - frac) * 0.5, 0.75 - frac * frac, (0.5 + frac) * (0.5 + frac) * 0.5)
    out = jnp.zeros((rows, frac.shape[1]), F32)
    for o in range(3):
        target = center + (o - 1)
        if wrap:
            target = jnp.where(target < 0, target + G, jnp.where(target >= G, target - G, target))
        out = jnp.where(index == target, values[o], out)
    return out


def chunk_blocks(blocks):
    per_tile = blocks // TILES_Y
    return [
        (t, [t + TILES_Y * z for z in range(2 * pair, 2 * pair + 2)])
        for t in range(TILES_Y)
        for pair in range(per_tile // 2)
    ]


def lanes_of(ref, row, pair):
    return jnp.concatenate([ref[row : row + 1, b * BLOCK : (b + 1) * BLOCK] for b in pair], axis=1)


def rows_of(ref, pair):
    return jnp.concatenate([ref[b : b + 1, :] for b in pair], axis=1)


def swap_blocks(arrays):
    arrays = list(arrays)
    count = len(arrays)
    width = BLOCK // count
    lane = lax.broadcasted_iota(jnp.int32, arrays[0].shape, arrays[0].ndim - 1)
    bit = 1
    while bit < count:
        upper = (lane // (width * bit)) % 2 == 1
        for i in range(count):
            if i & bit:
                continue
            low, high = arrays[i], arrays[i | bit]
            arrays[i] = jnp.where(upper, pltpu.roll(high, width * bit, low.ndim - 1), low)
            arrays[i | bit] = jnp.where(upper, high, pltpu.roll(low, BLOCK - width * bit, low.ndim - 1))
        bit *= 2
    return arrays


VMEM_SPEC = pl.BlockSpec(memory_space=pltpu.VMEM)
SMEM_SPEC = pl.BlockSpec(memory_space=pltpu.SMEM)


def call(body, outs, scratch, scalars, args):
    specs = [SMEM_SPEC] * scalars + [VMEM_SPEC] * (len(args) - scalars)
    many = isinstance(outs, (list, tuple))
    return pl.pallas_call(
        body,
        out_shape=outs,
        in_specs=specs,
        out_specs=[VMEM_SPEC] * len(outs) if many else VMEM_SPEC,
        scratch_shapes=scratch,
        compiler_params=pltpu.CompilerParams(vmem_limit_bytes=VMEM_BYTES),
    )(*args)


def share_kernel(cell, frac, kind, ext, sends, recvs):
    atoms = cell.shape[1]
    doms = lax.axis_size("dom")
    me = lax.axis_index("dom")
    mesh_ids = pl.DeviceIdType.MESH
    left, right = lax.rem(me + doms - 1, doms), lax.rem(me + 1, doms)
    barrier = pltpu.get_barrier_semaphore()
    for side in (left, right):
        pl.semaphore_signal(barrier, inc=1, device_id={"dom": side}, device_id_type=mesh_ids)
    own = pl.ds(atoms, atoms)
    ext[0:3, own] = cell[...].astype(F32) + frac[...]
    ext[3:4, own] = kind[...].astype(F32)
    pl.semaphore_wait(barrier, 2)
    copies = []
    for i, (side, slot) in enumerate(((left, 2), (right, 0))):
        copy = pltpu.make_async_remote_copy(
            src_ref=ext.at[:, own],
            dst_ref=ext.at[:, pl.ds(slot * atoms, atoms)],
            send_sem=sends.at[i],
            recv_sem=recvs.at[i],
            device_id={"dom": side},
            device_id_type=mesh_ids,
        )
        copy.start()
        copies.append(copy)
    for copy in copies:
        copy.wait()


def share_call(cell, frac, kind):
    return pl.pallas_call(
        share_kernel,
        out_shape=jax.ShapeDtypeStruct((4, 3 * cell.shape[1]), F32),
        in_specs=[VMEM_SPEC] * 3,
        out_specs=VMEM_SPEC,
        scratch_shapes=[pltpu.SemaphoreType.DMA((2,))] * 2,
        compiler_params=pltpu.CompilerParams(
            vmem_limit_bytes=VMEM_BYTES, collective_id=1, has_side_effects=True
        ),
    )(cell, frac, kind[None, :])


def pair_call(
    pair_blocks, counts, ext, species_embed, neighbour_embed, w_radial, w_hidden, w_charge, w_energy
):
    blocks = ext.shape[1] // (3 * BLOCK)
    width = w_charge.shape[0]
    shape = jax.ShapeDtypeStruct((blocks, BLOCK), F32)
    square = pltpu.VMEM((BLOCK, BLOCK), F32)
    return call(
        functools.partial(pair_kernel, step=3),
        [shape, shape],
        [
            pltpu.VMEM((width, BLOCK), BF),
            pltpu.VMEM((width, width), BF),
            *[square] * 4,
        ],
        2,
        (
            pair_blocks.T,
            counts,
            ext,
            w_radial,
            species_embed,
            neighbour_embed,
            w_hidden,
            w_charge.reshape(-1, BLOCK),
            w_energy.reshape(-1, BLOCK),
        ),
    )


def tile_order(slab):
    quads = slab // 4
    order = list(range(1, quads - 1)) + [0, quads - 1]
    return [2 * q + half for q in order for half in range(2)]


def tile_cuts(tiles):
    return [(0, tiles // 2), (tiles // 2, tiles)]


def mesh_kernel(
    cell,
    frac,
    charge,
    *refs,
):
    sources, (pot, grad, acc, back, table_s, lsem), refs = refs[:9], refs[9:15], refs[15:]
    (
        halo,
        row_send,
        row_land,
        edge_send,
        edge_land,
        ready_x,
        land_x,
        ready_y,
        land_y,
        ready_b,
        land_b,
        ready_h,
        land_h,
        green_s,
        weight_s,
        side_s,
        part_s,
        mesh_s,
        hsend,
        hrecv,
        rsend,
        rrecv,
        send_x,
        recv_x,
        send_y,
        recv_y,
        send_b,
        recv_b,
        send_h,
        recv_h,
        loc_x,
        loc_y,
        loc_b,
        loc_h,
    ) = refs
    halves, groups, cols, wide = ready_y.shape
    chunks = halves // 2
    doms = lax.axis_size("dom")
    slab = G // doms
    planes = slab + 2
    quarter = G // groups
    tiles = slab // 2
    tile = quarter // TILES_Y
    window = 24
    lines = doms * tiles
    order = tile_order(slab)
    strips = [divmod(i, doms) for i in range(G // 8)]
    me_g, me_d = lax.axis_index("grp"), lax.axis_index("dom")
    mesh_ids = pl.DeviceIdType.MESH
    barrier = pltpu.get_barrier_semaphore()
    order_g = sorted(range(1, groups), key=lambda k: abs(k - groups // 2))
    order_d = sorted(range(1, doms), key=lambda k: abs(k - doms // 2))
    for h in range(2):
        for base in (0, quarter):
            mesh_s[h, :, base : base + 8, :] = jnp.zeros((planes, 8, BLOCK), F32)
    for axis, me, peers, count in (("grp", me_g, order_g, groups), ("dom", me_d, order_d, doms)):
        for k in peers:
            pl.semaphore_signal(
                barrier, inc=1, device_id={axis: lax.rem(me + k, count)}, device_id_type=mesh_ids
            )

    pending = []

    def remote(src, dst, send_sem, recv_sem, axis, peer):
        copy = pltpu.make_async_remote_copy(
            src_ref=src,
            dst_ref=dst,
            send_sem=send_sem,
            recv_sem=recv_sem,
            device_id={axis: peer},
            device_id_type=mesh_ids,
        )
        copy.start()
        pending.append(copy)
        return copy

    def local_copy(src, dst, sem):
        copy = pltpu.make_async_copy(src, dst, sem)
        copy.start()
        return copy

    loads = [
        local_copy(source, back if i == 0 else table_s.at[i - 1], lsem.at[i]) for i, source in enumerate(sources)
    ]

    def arrive(entry):
        own, copies = entry
        own.wait()
        for copy in copies:
            copy.wait_recv()

    def to_sides(axis, me, count, low, high, low_dst, high_dst, sends, recvs, base):
        before, after = lax.rem(me + count - 1, count), lax.rem(me + 1, count)
        return [
            remote(low, low_dst, sends.at[base], recvs.at[base], axis, before),
            remote(high, high_dst, sends.at[base + 1], recvs.at[base + 1], axis, after),
        ]

    offset_x = 1 - slab * me_d
    offset_y = 1 - quarter * me_g
    atom_chunks = chunk_blocks(charge.shape[0])
    outer = [m for m, (t, _) in enumerate(atom_chunks) if t in (0, TILES_Y - 1)]
    inner = [m for m in range(len(atom_chunks)) if m not in outer]

    def atoms_of(m):
        t, pair = atom_chunks[m]
        local = [
            lanes_of(cell, 0, pair) + offset_x,
            lanes_of(cell, 1, pair) + offset_y,
            lanes_of(cell, 2, pair),
        ]
        return t, pair, local, [lanes_of(frac, axis, pair) for axis in range(3)]

    acc[...] = jnp.zeros_like(acc)

    def spread(m):
        t, pair, local, f = atoms_of(m)
        wx = spline_rows(planes, 0, local[0], f[0], False, False)
        wy = spline_rows(window, tile * t, local[1], f[1], False, False)
        wz = spline_rows(G, 0, local[2], f[2], True, False)
        wy = wy * rows_of(charge, pair)
        mix = jnp.concatenate([wx[x : x + 1, :] * wy for x in range(planes)], axis=0)
        part = dot3(dot_nt, split2(mix), split2(wz))
        acc[:, tile * t : tile * t + window, :] += part.reshape(planes, window, G)

    for m in outer:
        spread(m)
    row_send[0] = acc[:, 0, :]
    row_send[1] = acc[:, quarter + 1, :]
    pl.semaphore_wait(barrier, groups + doms - 2)
    rows = to_sides(
        "grp", me_g, groups, row_send.at[0], row_send.at[1], row_land.at[0], row_land.at[1], rsend, rrecv, 0
    )
    for m in inner:
        spread(m)
    for copy in rows:
        copy.wait_recv()
    acc[:, quarter, :] = acc[:, quarter, :] + row_land[0]
    acc[:, 1, :] = acc[:, 1, :] + row_land[1]
    border = to_sides(
        "dom", me_d, doms, acc.at[0], acc.at[slab + 1], halo.at[0], halo.at[1], hsend, hrecv, 0
    )
    for load in loads:
        load.wait()
    table_z = (table_s[0], table_s[1])

    def transform_z(j):
        base = 1 + 2 * order[j]
        values = acc[base : base + 4, 1 : quarter + 1, :] + back[base - 1 : base + 3]
        spec = dot3(dot_nt, table_z, split2(values.reshape(4 * quarter, G)))
        for c in range(chunks):
            for d in range(doms):
                row = 8 * (c * doms + d)
                for i in range(2):
                    ready_x[c, pl.ds((d * tiles + j + i) * 8, 8)] = spec[
                        row : row + 8, i * BLOCK : (i + 1) * BLOCK
                    ]

    def exchange_dom(src, dst, c, n, cut, send_sem, recv_sem, loc):
        lo, hi = cut

        def at(d):
            return pl.ds((d * tiles + lo) * 8, (hi - lo) * 8)

        copies = []
        for k in order_d:
            peer = lax.rem(me_d + k, doms)
            copies.append(
                remote(
                    src.at[c, at(peer)],
                    dst.at[c, at(me_d)],
                    send_sem.at[c, n, k - 1],
                    recv_sem.at[c, n, k - 1],
                    "dom",
                    peer,
                )
            )
        return local_copy(src.at[c, at(me_d)], dst.at[c, at(me_d)], loc.at[c, n]), copies

    def exchange_grp(src, dst, c, send_sem, recv_sem, loc):
        copies = []
        for k in order_g:
            peer = lax.rem(me_g + k, groups)
            copies.append(
                remote(
                    src.at[c, peer], dst.at[c, me_g], send_sem.at[c, k - 1], recv_sem.at[c, k - 1], "grp", peer
                )
            )
        return local_copy(src.at[c, me_g], dst.at[c, me_g], loc.at[c]), copies

    cuts = tile_cuts(tiles)
    pieces = [(c, n) for c in range(chunks) for n in range(2)]
    out_x = {}
    left_out = set()

    def send_out(c, n):
        out_x[c, n] = exchange_dom(ready_x, land_x, c, n, cuts[n], send_x, recv_x, loc_x)

    def advance(depth):
        at = len(out_x)
        if at == len(pieces):
            return
        done = [] if at - depth in left_out else out_x[pieces[at - depth]][1]
        left_out.add(at - depth)
        for copy in done:
            copy.wait_send()
        pending[:] = [other for other in pending if all(other is not copy for copy in done)]
        send_out(*pieces[at])

    joined = False
    for n, (lo, hi) in enumerate(cuts):
        if hi > tiles - 4 and not joined:
            for copy in border:
                copy.wait_recv()
            acc[1] = acc[1] + halo[1]
            acc[slab] = acc[slab] + halo[0]
            joined = True
        for j in range(lo, hi, 2):
            transform_z(j)
        send_out(0, n)

    unit = 2.0 * math.pi / G * (2.0 * math.pi / G)
    shape = (4 * cols, G)

    def signed(m):
        return jnp.where(m < G // 2, m, m - G)

    row_id = lax.broadcasted_iota(jnp.int32, shape, 0)
    my = signed(lax.broadcasted_iota(jnp.int32, shape, 1))

    def fill_green(part):
        mz = signed(me_d * (G // doms) + part * 4 + row_id // cols)
        mx = signed(me_g * cols + row_id % cols)
        squares = mx * mx + my * my + mz * mz
        wave = squares.astype(F32) * unit
        safe = jnp.where(squares > 0, wave, 1.0)
        green_s[part] = jnp.where(
            squares > 0, 4.0 * math.pi * jnp.exp(-wave / (4.0 * EWALD * EWALD)) / safe, 0.0
        ) * (1.0 / (G * G * G))

    side_rows = side_s.shape[1] // 2 - window

    def fill_weights(m):
        t, pair, local, f = atoms_of(m)
        for kind in range(2):
            wz = spline_rows(G, 0, local[2], f[2], True, kind == 1)
            high, low = split2(dot3(dot_nn, table_z, split2(wz)))
            weight_s[m, kind, 0] = high
            weight_s[m, kind, 1] = low
            base = kind * (side_rows + window)
            side_s[m, base : base + side_rows] = spline_rows(side_rows, 0, local[0], f[0], False, kind == 1)
            side_s[m, base + side_rows : base + side_rows + window] = spline_rows(
                window, tile * t, local[1], f[1], False, kind == 1
            )

    table_y = (table_s[2], table_s[3])
    forward_x = (table_s[4], table_s[5])
    back_x = (table_s[6], table_s[7])
    out_y, home_b, home_h = {}, {}, {}

    def stage_x(c):
        for n in range(2):
            arrive(out_x[c, n])
        for two in range(2):
            parts = []
            for kp in (2 * two, 2 * two + 1):
                loaded = [land_x[c, pl.ds(2 * kp + i, lines, stride=8), :] for i in range(2)]
                parts.append(jnp.concatenate(swap_blocks(loaded), axis=0))
            result = dot3(dot_nn, forward_x, split2(jnp.concatenate(parts, axis=1)))
            part = 2 * c + two
            for g in range(groups):
                ready_y[part, g] = result[g * cols : (g + 1) * cols]
            out_y[part] = exchange_grp(ready_y, land_y, part, send_y, recv_y, loc_y)

    def stage_y(part):
        arrive(out_y[part])
        rows = []
        for kp in range(2):
            cut = slice(kp * BLOCK, (kp + 1) * BLOCK)
            pairs = [
                swap_blocks([land_y[part, g, :, cut], land_y[part, g + 1, :, cut]])
                for g in range(0, groups, 2)
            ]
            for i in range(2):
                rows.append(jnp.concatenate([pair[i] for pair in pairs], axis=1))
        spectrum = dot3(dot_nn, split2(jnp.concatenate(rows, axis=0)), table_y) * green_s[part]
        result = dot3(dot_nn, split2(spectrum), table_y)
        for kp in range(2):
            for g in range(0, groups, 2):
                cut = slice(g * quarter, (g + 2) * quarter)
                both = [result[(2 * kp + i) * cols : (2 * kp + i + 1) * cols, cut] for i in range(2)]
                for i, piece in enumerate(swap_blocks(both)):
                    ready_b[part, g + i, :, kp * BLOCK : (kp + 1) * BLOCK] = piece
        home_b[part] = exchange_grp(ready_b, land_b, part, send_b, recv_b, loc_b)

    def stage_h(c):
        for two in range(2):
            arrive(home_b[2 * c + two])
            column = jnp.concatenate([land_b[2 * c + two, g] for g in range(groups)], axis=0)
            result = dot3(dot_nn, back_x, split2(column))
            for i in range(2):
                cut = slice(i * BLOCK, (i + 1) * BLOCK)
                both = swap_blocks([result[:lines, cut], result[lines:, cut]])
                for k, piece in enumerate(both):
                    ready_h[c, pl.ds(2 * (2 * two + i) + k, lines, stride=8), :] = piece
        for n, cut in enumerate(reversed(cuts)):
            home_h[c, n] = exchange_dom(ready_h, land_h, c, n, cut, send_h, recv_h, loc_h)

    edges = {}

    def gather(h, lo, hi):
        for j in range(lo, hi):
            block = jnp.concatenate(
                [land_h[c, pl.ds((d * tiles + j) * 8, 8)] for c, d in strips[16 * h : 16 * (h + 1)]],
                axis=0,
            )
            turned = block.T
            base = 1 + 2 * order[j]
            for i in range(2):
                mesh_s[h, base + i, 1 : quarter + 1, :] = turned[i * quarter : (i + 1) * quarter]

    def send_edges(h):
        edges[h] = to_sides(
            "dom",
            me_d,
            doms,
            mesh_s.at[h, 1],
            mesh_s.at[h, slab],
            mesh_s.at[h, slab + 1],
            mesh_s.at[h, 0],
            hsend,
            hrecv,
            2 + 2 * h,
        )

    def send_rows(h):
        for copy in edges[h]:
            copy.wait()
            pending[:] = [other for other in pending if other is not copy]
        edge_send[h, 0] = mesh_s[h, :, 1, :]
        edge_send[h, 1] = mesh_s[h, :, quarter, :]
        return to_sides(
            "grp",
            me_g,
            groups,
            edge_send.at[h, 0],
            edge_send.at[h, 1],
            edge_land.at[h, 0],
            edge_land.at[h, 1],
            rsend,
            rrecv,
            2 + 2 * h,
        )

    def sample(h, chosen):
        half = slice(h * BLOCK, (h + 1) * BLOCK)
        known = None
        for m in chosen:
            t, pair = atom_chunks[m]
            if t != known:
                strip = mesh_s[h, :, tile * t : tile * t + window, :].reshape(planes * window, BLOCK)
                strip = jnp.concatenate(split2(strip), axis=1)
                known = t

            def along(kind):
                high, low = weight_s[m, kind, 0, half], weight_s[m, kind, 1, half]
                return dot_nn(strip, jnp.concatenate([high, high], axis=0)) + dot_nn(
                    strip, jnp.concatenate([low, low], axis=0)
                )

            wx, wy = side_s[m, :side_rows], side_s[m, side_rows : side_rows + window]
            sx = side_s[m, side_rows + window : 2 * side_rows + window]
            sy = side_s[m, 2 * side_rows + window :]
            value, slope = along(0), along(1)
            value_y = jnp.zeros_like(wy)
            grad_y = jnp.zeros_like(wy)
            slope_y = jnp.zeros_like(wy)
            for x in range(planes):
                here = value[x * window : (x + 1) * window]
                value_y = value_y + wx[x : x + 1] * here
                grad_y = grad_y + sx[x : x + 1] * here
                slope_y = slope_y + wx[x : x + 1] * slope[x * window : (x + 1) * window]
            sums = jnp.concatenate(
                [
                    jnp.sum(one * two, axis=0, keepdims=True)
                    for one, two in ((wy, value_y), (wy, grad_y), (sy, value_y), (wy, slope_y))
                ],
                axis=0,
            )
            if h == 0:
                part_s[m, 0:4] = sums
                continue
            sums = sums + part_s[m, 0:4]
            for k, b in enumerate(pair):
                cut = slice(k * BLOCK, (k + 1) * BLOCK)
                pot[b : b + 1, :] = sums[0:1, cut]
                grad[:, b * BLOCK : (b + 1) * BLOCK] = sums[1:4, cut]

    def finish(h):
        rows = send_rows(h)
        sample(h, inner)
        for copy in rows:
            copy.wait_recv()
        mesh_s[h, :, quarter + 1, :] = edge_land[h, 0]
        mesh_s[h, :, 0, :] = edge_land[h, 1]
        sample(h, outer)

    fills = [functools.partial(fill_weights, m) for m in range(len(atom_chunks))]
    fills += [functools.partial(fill_green, part) for part in range(halves)]
    for i, fill in enumerate(fills):
        fill()
        if i == len(fills) // 2:
            advance(2)
    advance(2)
    for c in range(chunks):
        stage_x(c)
        advance(3)
        if c:
            stage_h(c - 1)
        else:
            advance(3)
        stage_y(2 * c)
        advance(3)
        stage_y(2 * c + 1)
    stage_h(chunks - 1)
    for h in range(2):
        needed = sorted({c for c, _ in strips[16 * h : 16 * (h + 1)]})
        for n, (lo, hi) in enumerate(reversed(cuts)):
            for c in needed:
                if (c, n) in home_h:
                    arrive(home_h.pop((c, n)))
            gather(h, lo, hi)
            if h not in edges and lo <= tiles - 4:
                send_edges(h)
        finish(h)
    for copy in pending:
        copy.wait_send()


def mesh_call(cell, frac, charge, back, table_list, doms, groups):
    slab = back.shape[0]
    quarter = back.shape[1]
    padded_y = quarter + 8
    planes = slab + 2
    tiles = slab // 2
    chunks = G // doms // 8
    atom_chunks = len(chunk_blocks(charge.shape[0]))
    atoms = 2 * BLOCK
    side_rows = 2 * (-(-planes // 8) * 8 + 24)
    dma = pltpu.SemaphoreType.DMA
    dom_shape = pltpu.VMEM((chunks, doms * tiles * 8, BLOCK), F32)
    grp_shape = pltpu.VMEM((2 * chunks, groups, G // groups, 4 * quarter), F32)
    row_shape = pltpu.VMEM((2, planes, G), F32)
    edge_shape = pltpu.VMEM((2, 2, planes, BLOCK), F32)
    args = [cell, frac, charge, back] + [part for table in table_list for part in table]
    return pl.pallas_call(
        mesh_kernel,
        out_shape=[jax.ShapeDtypeStruct(charge.shape, F32), jax.ShapeDtypeStruct(frac.shape, F32)],
        in_specs=[VMEM_SPEC] * 3 + [pl.BlockSpec(memory_space=pl.ANY)] * (len(args) - 3),
        out_specs=[VMEM_SPEC] * 2,
        scratch_shapes=[
            pltpu.VMEM((planes, padded_y, G), F32),
            pltpu.VMEM(back.shape, F32),
            pltpu.VMEM((8, G, G), BF),
            dma((9,)),
            pltpu.VMEM((2, padded_y, G), F32),
            *[row_shape] * 2,
            *[edge_shape] * 2,
            *[dom_shape] * 2,
            *[grp_shape] * 4,
            *[dom_shape] * 2,
            pltpu.VMEM((2 * chunks, 4 * (G // groups), G), F32),
            pltpu.VMEM((atom_chunks, 2, 2, G, atoms), BF),
            pltpu.VMEM((atom_chunks, side_rows, atoms), F32),
            pltpu.VMEM((atom_chunks, 8, atoms), F32),
            pltpu.VMEM((2, planes, padded_y, BLOCK), F32),
            *[dma((6,))] * 4,
            *[dma((chunks, 2, doms - 1))] * 2,
            *[dma((2 * chunks, groups - 1))] * 4,
            *[dma((chunks, 2, doms - 1))] * 2,
            dma((chunks, 2)),
            dma((2 * chunks,)),
            dma((2 * chunks,)),
            dma((chunks, 2)),
        ],
        compiler_params=pltpu.CompilerParams(
            vmem_limit_bytes=VMEM_BYTES, collective_id=0, has_side_effects=True
        ),
    )(*args)


def final_kernel(potential, gradient, energy, charge, site, field):
    site[...] = energy[...] + 0.5 * charge[...] * potential[...]
    field[...] = -gradient[...]


def tables(slab, doms):
    chunks = G // doms // 8
    plain = hartley(np.arange(G))
    z_order = np.array([d * (G // doms) + c * 8 + k for c in range(chunks) for d in range(doms) for k in range(8)])
    hz = hartley(z_order)
    x_points = np.array([slab * d + 2 * t + i for i in range(2) for d in range(doms) for t in tile_order(slab)])
    hx = hartley(x_points)
    return [np_split(t) for t in (hz.T, plain, hx, hx.T)]


def on_device(
    cell_index,
    offsets,
    species,
    pair_blocks,
    counts,
    background,
    species_embed,
    neighbour_embed,
    w_radial,
    w_hidden,
    w_charge,
    w_energy,
):
    atoms = cell_index.shape[1]
    doms = lax.axis_size("dom")
    groups = lax.axis_size("grp")
    ext = share_call(cell_index, offsets, species)
    energies, charges = pair_call(
        pair_blocks,
        counts,
        ext,
        species_embed,
        neighbour_embed,
        w_radial,
        w_hidden,
        w_charge,
        w_energy,
    )

    potential, gradient = mesh_call(
        cell_index, offsets, charges, background, tables(G // doms, doms), doms, groups
    )
    site, field = call(
        final_kernel,
        [jax.ShapeDtypeStruct(energies.shape, F32), jax.ShapeDtypeStruct(gradient.shape, F32)],
        [],
        0,
        (potential, gradient, energies, charges),
    )
    return (site.reshape(atoms), field, charges.reshape(atoms))


def solution(mesh):
    return jax.shard_map(
        on_device,
        mesh=mesh,
        in_specs=(
            P(None, ("grp", "dom")),
            P(None, ("grp", "dom")),
            P(("grp", "dom")),
            P(("grp", "dom"), None),
            P(("grp", "dom")),
            P("dom", "grp", None),
            P(),
            P(),
            P(),
            P(),
            P(),
            P(),
        ),
        out_specs=(P(("grp", "dom")), P(None, ("grp", "dom")), P(("grp", "dom"))),
        check_vma=False,
    )
```

```python
import functools
import math

import jax
import jax.numpy as jnp
import ml_dtypes
import numpy as np
from jax import lax
from jax.experimental import pallas as pl
from jax.experimental.pallas import tpu as pltpu
from jax.sharding import PartitionSpec as P

G = 256
NBASIS = 8
NSPEC = 8
BLOCK = 128
TILES_Y = 4
CUTOFF = 6.0
EWALD = 1.0
VMEM_BYTES = 56 << 20

BF = jnp.bfloat16
F32 = jnp.float32


def np_split(table):
    table = np.asarray(table, np.float32)
    high = table.astype(ml_dtypes.bfloat16)
    low = (table - high.astype(np.float32)).astype(ml_dtypes.bfloat16)
    return high, low


def hartley(points):
    phase = (np.arange(G)[:, None] * np.asarray(points)[None, :]) % G
    angle = phase.astype(np.float64) * (2.0 * math.pi / G)
    return np.cos(angle) + np.sin(angle)


def split2(x):
    high = x.astype(BF)
    low = (x - high.astype(F32)).astype(BF)
    return high, low


def dot_nn(a, b):
    return lax.dot_general(a, b, (((1,), (0,)), ((), ())), preferred_element_type=F32)


def dot_nt(a, b):
    return lax.dot_general(a, b, (((1,), (1,)), ((), ())), preferred_element_type=F32)


def dot3(dot, a, b):
    return dot(a[0], b[0]) + (dot(a[0], b[1]) + dot(a[1], b[0]))


def split3(x):
    one = x.astype(BF).astype(F32)
    two = (x - one).astype(BF).astype(F32)
    three = (x - one - two).astype(BF).astype(F32)
    return one, two, three


def pair_kernel(
    slots,
    live,
    ext,
    radial_w,
    kind_i_w,
    kind_j_w,
    hidden_w,
    charge_w,
    energy_w,
    energy,
    charge,
    wcat,
    whid,
    rank_s,
    theta_s,
    env_s,
    kind_s,
    *,
    step,
):
    blocks = energy.shape[0]
    atoms = ext.shape[1] // 3
    energy[...] = jnp.zeros_like(energy)
    charge[...] = jnp.zeros_like(charge)
    width = hidden_w.shape[0]
    r1, r2, r3 = split3(radial_w[...])
    table = jnp.concatenate(
        [
            *(r1, r2, r3, r1, r2, r1),
            *split3(kind_j_w[...]),
            *split3(kind_i_w[...]),
            jnp.zeros((BLOCK - 12 * NBASIS, width), F32),
        ],
        axis=0,
    )
    wcat[...] = (0.5 * table).T.astype(BF)
    whid[...] = (0.5 * hidden_w[...].astype(F32)).T.astype(BF)

    def spread_row(ref):
        rows = ref[...].astype(F32)
        row = jnp.concatenate([rows[i : i + 1] for i in range(rows.shape[0])], axis=1)
        return jnp.broadcast_to(row, (16, width)).astype(BF)

    wq = spread_row(charge_w)
    we = spread_row(energy_w)
    half = 0.5 * G
    row8 = lax.broadcasted_iota(jnp.int32, (NSPEC, BLOCK), 0).astype(F32)
    sub = lax.broadcasted_iota(jnp.int32, (BLOCK, BLOCK), 0)
    lane = lax.broadcasted_iota(jnp.int32, (BLOCK, BLOCK), 1)
    earlier = (lane < sub).astype(F32).astype(BF)
    spare = jnp.zeros((BLOCK - 12 * NBASIS, BLOCK), F32)

    def slot_body(slot, unused):
        bi = slots[0, slot]
        bj = slots[1, slot]
        ri = ext[:, pl.ds(pl.multiple_of(atoms + bi * BLOCK, BLOCK), BLOCK)]
        rj = ext[:, pl.ds(pl.multiple_of(bj * BLOCK, BLOCK), BLOCK)]
        total = jnp.zeros((BLOCK, BLOCK), F32)
        for c in range(3):
            sep = jnp.broadcast_to(rj[c : c + 1, :], (BLOCK, BLOCK)).T - ri[c : c + 1, :]
            sep = jnp.where(sep > half, sep - G, jnp.where(sep < -half, sep + G, sep))
            total = total + sep * sep
        scaled = jnp.sqrt(total) / CUTOFF
        inside = 1.0 - scaled * scaled
        env = jnp.where(scaled < 1.0, inside * inside, 0.0)
        env = jnp.where((sub == lane) & (bj == blocks + bi), 0.0, env)
        used = (env > 0.0).astype(F32)
        rank_s[...] = jnp.where(env > 0.0, dot_nn(earlier, used.astype(BF)), -1.0)
        theta_s[...] = math.pi * jnp.minimum(scaled, 1.0)
        env_s[...] = env
        kind_s[...] = jnp.broadcast_to(rj[3:4, :], (BLOCK, BLOCK)).T
        most = jnp.max(jnp.sum(used, axis=0, keepdims=True)).astype(jnp.int32)
        kind_i = (row8 == ri[3:4, :]).astype(F32)

        def rows_body(it, sums):
            energy_sum, charge_sum = sums
            rank = rank_s[...]
            parts = []
            envs = []
            for k in range(step):
                pick = rank == (it * step + k).astype(F32)
                theta = jnp.sum(jnp.where(pick, theta_s[...], 0.0), axis=0, keepdims=True)
                kind = jnp.sum(jnp.where(pick, kind_s[...], 0.0), axis=0, keepdims=True)
                envs.append(jnp.sum(jnp.where(pick, env_s[...], 0.0), axis=0, keepdims=True))
                phase = theta * (row8 + 1.0)
                small = phase == 0.0
                rad = jnp.where(small, 1.0, jnp.sin(phase) / jnp.where(small, 1.0, phase))
                one, two, three = split3(rad)
                kind_j = (row8 == kind).astype(F32)
                parts.append(
                    jnp.concatenate(
                        [
                            *(one, one, one, two, two, three),
                            *(kind_j, kind_j, kind_j, kind_i, kind_i, kind_i),
                            spare,
                        ],
                        axis=0,
                    ).astype(BF)
                )
            feats = jnp.concatenate(parts, axis=1)
            h = dot_nn(wcat[...], feats)
            edge = (h + h * jnp.tanh(h)).astype(BF)
            cp = dot_nn(wq, edge)
            g = dot_nn(whid[...], edge)
            latent = (g + g * jnp.tanh(g)).astype(BF)
            ep = dot_nn(we, latent)
            for k in range(step):
                cut = slice(k * BLOCK, (k + 1) * BLOCK)
                charge_sum = charge_sum + envs[k] * cp[0:1, cut]
                energy_sum = energy_sum + envs[k] * ep[0:1, cut]
            return energy_sum, charge_sum

        zero = jnp.zeros((1, BLOCK), F32)
        energy_sum, charge_sum = lax.fori_loop(
            0, (most + step - 1) // step, rows_body, (zero, zero)
        )
        where = pl.ds(bi, 1)
        charge[where, :] = charge[where, :] + charge_sum
        energy[where, :] = energy[where, :] + energy_sum
        return unused

    lax.fori_loop(0, live[0], slot_body, 0)


def spline_rows(rows, first, center, frac, wrap, slopes):
    index = lax.broadcasted_iota(jnp.int32, (rows, frac.shape[1]), 0) + first
    if slopes:
        values = (frac - 0.5, -2.0 * frac, 0.5 + frac)
    else:
        values = ((0.5 - frac) * (0.5 - frac) * 0.5, 0.75 - frac * frac, (0.5 + frac) * (0.5 + frac) * 0.5)
    out = jnp.zeros((rows, frac.shape[1]), F32)
    for o in range(3):
        target = center + (o - 1)
        if wrap:
            target = jnp.where(target < 0, target + G, jnp.where(target >= G, target - G, target))
        out = jnp.where(index == target, values[o], out)
    return out


def chunk_blocks(blocks):
    per_tile = blocks // TILES_Y
    return [
        (t, [t + TILES_Y * z for z in range(2 * pair, 2 * pair + 2)])
        for t in range(TILES_Y)
        for pair in range(per_tile // 2)
    ]


def lanes_of(ref, row, pair):
    return jnp.concatenate([ref[row : row + 1, b * BLOCK : (b + 1) * BLOCK] for b in pair], axis=1)


def rows_of(ref, pair):
    return jnp.concatenate([ref[b : b + 1, :] for b in pair], axis=1)


def swap_blocks(arrays):
    arrays = list(arrays)
    count = len(arrays)
    width = BLOCK // count
    lane = lax.broadcasted_iota(jnp.int32, arrays[0].shape, arrays[0].ndim - 1)
    bit = 1
    while bit < count:
        upper = (lane // (width * bit)) % 2 == 1
        for i in range(count):
            if i & bit:
                continue
            low, high = arrays[i], arrays[i | bit]
            arrays[i] = jnp.where(upper, pltpu.roll(high, width * bit, low.ndim - 1), low)
            arrays[i | bit] = jnp.where(upper, high, pltpu.roll(low, BLOCK - width * bit, low.ndim - 1))
        bit *= 2
    return arrays


VMEM_SPEC = pl.BlockSpec(memory_space=pltpu.VMEM)
SMEM_SPEC = pl.BlockSpec(memory_space=pltpu.SMEM)


def call(body, outs, scratch, scalars, args):
    specs = [SMEM_SPEC] * scalars + [VMEM_SPEC] * (len(args) - scalars)
    many = isinstance(outs, (list, tuple))
    return pl.pallas_call(
        body,
        out_shape=outs,
        in_specs=specs,
        out_specs=[VMEM_SPEC] * len(outs) if many else VMEM_SPEC,
        scratch_shapes=scratch,
        compiler_params=pltpu.CompilerParams(vmem_limit_bytes=VMEM_BYTES),
    )(*args)


def share_kernel(cell, frac, kind, ext, sends, recvs):
    atoms = cell.shape[1]
    doms = lax.axis_size("dom")
    me = lax.axis_index("dom")
    mesh_ids = pl.DeviceIdType.MESH
    left, right = lax.rem(me + doms - 1, doms), lax.rem(me + 1, doms)
    barrier = pltpu.get_barrier_semaphore()
    for side in (left, right):
        pl.semaphore_signal(barrier, inc=1, device_id={"dom": side}, device_id_type=mesh_ids)
    own = pl.ds(atoms, atoms)
    ext[0:3, own] = cell[...].astype(F32) + frac[...]
    ext[3:4, own] = kind[...].astype(F32)
    pl.semaphore_wait(barrier, 2)
    copies = []
    for i, (side, slot) in enumerate(((left, 2), (right, 0))):
        copy = pltpu.make_async_remote_copy(
            src_ref=ext.at[:, own],
            dst_ref=ext.at[:, pl.ds(slot * atoms, atoms)],
            send_sem=sends.at[i],
            recv_sem=recvs.at[i],
            device_id={"dom": side},
            device_id_type=mesh_ids,
        )
        copy.start()
        copies.append(copy)
    for copy in copies:
        copy.wait()


def share_call(cell, frac, kind):
    return pl.pallas_call(
        share_kernel,
        out_shape=jax.ShapeDtypeStruct((4, 3 * cell.shape[1]), F32),
        in_specs=[VMEM_SPEC] * 3,
        out_specs=VMEM_SPEC,
        scratch_shapes=[pltpu.SemaphoreType.DMA((2,))] * 2,
        compiler_params=pltpu.CompilerParams(
            vmem_limit_bytes=VMEM_BYTES, collective_id=1, has_side_effects=True
        ),
    )(cell, frac, kind[None, :])


def pair_call(
    pair_blocks, counts, ext, species_embed, neighbour_embed, w_radial, w_hidden, w_charge, w_energy
):
    blocks = ext.shape[1] // (3 * BLOCK)
    width = w_charge.shape[0]
    shape = jax.ShapeDtypeStruct((blocks, BLOCK), F32)
    square = pltpu.VMEM((BLOCK, BLOCK), F32)
    return call(
        functools.partial(pair_kernel, step=4),
        [shape, shape],
        [
            pltpu.VMEM((width, BLOCK), BF),
            pltpu.VMEM((width, width), BF),
            *[square] * 4,
        ],
        2,
        (
            pair_blocks.T,
            counts,
            ext,
            w_radial,
            species_embed,
            neighbour_embed,
            w_hidden,
            w_charge.reshape(-1, BLOCK),
            w_energy.reshape(-1, BLOCK),
        ),
    )


def tile_order(slab):
    quads = slab // 4
    order = list(range(1, quads - 1)) + [0, quads - 1]
    return [2 * q + half for q in order for half in range(2)]


def tile_cuts(tiles):
    return [(0, tiles // 2), (tiles // 2, tiles)]


def mesh_kernel(
    cell,
    frac,
    charge,
    *refs,
):
    sources, (pot, grad, acc, back, table_s, lsem), refs = refs[:9], refs[9:15], refs[15:]
    (
        halo,
        row_send,
        row_land,
        edge_send,
        edge_land,
        ready_x,
        land_x,
        ready_y,
        land_y,
        ready_b,
        land_b,
        ready_h,
        land_h,
        green_s,
        weight_s,
        side_s,
        part_s,
        mesh_s,
        hsend,
        hrecv,
        rsend,
        rrecv,
        send_x,
        recv_x,
        send_y,
        recv_y,
        send_b,
        recv_b,
        send_h,
        recv_h,
        loc_x,
        loc_y,
        loc_b,
        loc_h,
    ) = refs
    halves, groups, cols, wide = ready_y.shape
    chunks = halves // 2
    doms = lax.axis_size("dom")
    slab = G // doms
    planes = slab + 2
    quarter = G // groups
    tiles = slab // 2
    tile = quarter // TILES_Y
    window = 24
    lines = doms * tiles
    order = tile_order(slab)
    strips = [divmod(i, doms) for i in range(G // 8)]
    me_g, me_d = lax.axis_index("grp"), lax.axis_index("dom")
    mesh_ids = pl.DeviceIdType.MESH
    barrier = pltpu.get_barrier_semaphore()
    order_g = sorted(range(1, groups), key=lambda k: abs(k - groups // 2))
    order_d = sorted(range(1, doms), key=lambda k: abs(k - doms // 2))
    for h in range(2):
        for base in (0, quarter):
            mesh_s[h, :, base : base + 8, :] = jnp.zeros((planes, 8, BLOCK), F32)
    for axis, me, peers, count in (("grp", me_g, order_g, groups), ("dom", me_d, order_d, doms)):
        for k in peers:
            pl.semaphore_signal(
                barrier, inc=1, device_id={axis: lax.rem(me + k, count)}, device_id_type=mesh_ids
            )

    pending = []

    def remote(src, dst, send_sem, recv_sem, axis, peer):
        copy = pltpu.make_async_remote_copy(
            src_ref=src,
            dst_ref=dst,
            send_sem=send_sem,
            recv_sem=recv_sem,
            device_id={axis: peer},
            device_id_type=mesh_ids,
        )
        copy.start()
        pending.append(copy)
        return copy

    def local_copy(src, dst, sem):
        copy = pltpu.make_async_copy(src, dst, sem)
        copy.start()
        return copy

    loads = [
        local_copy(source, back if i == 0 else table_s.at[i - 1], lsem.at[i]) for i, source in enumerate(sources)
    ]

    def arrive(entry):
        own, copies = entry
        own.wait()
        for copy in copies:
            copy.wait_recv()

    def to_sides(axis, me, count, low, high, low_dst, high_dst, sends, recvs, base):
        before, after = lax.rem(me + count - 1, count), lax.rem(me + 1, count)
        return [
            remote(low, low_dst, sends.at[base], recvs.at[base], axis, before),
            remote(high, high_dst, sends.at[base + 1], recvs.at[base + 1], axis, after),
        ]

    offset_x = 1 - slab * me_d
    offset_y = 1 - quarter * me_g
    atom_chunks = chunk_blocks(charge.shape[0])
    outer = [m for m, (t, _) in enumerate(atom_chunks) if t in (0, TILES_Y - 1)]
    inner = [m for m in range(len(atom_chunks)) if m not in outer]

    def atoms_of(m):
        t, pair = atom_chunks[m]
        local = [
            lanes_of(cell, 0, pair) + offset_x,
            lanes_of(cell, 1, pair) + offset_y,
            lanes_of(cell, 2, pair),
        ]
        return t, pair, local, [lanes_of(frac, axis, pair) for axis in range(3)]

    acc[...] = jnp.zeros_like(acc)

    def spread(m):
        t, pair, local, f = atoms_of(m)
        wx = spline_rows(planes, 0, local[0], f[0], False, False)
        wy = spline_rows(window, tile * t, local[1], f[1], False, False)
        wz = spline_rows(G, 0, local[2], f[2], True, False)
        wy = wy * rows_of(charge, pair)
        mix = jnp.concatenate([wx[x : x + 1, :] * wy for x in range(planes)], axis=0)
        part = dot3(dot_nt, split2(mix), split2(wz))
        acc[:, tile * t : tile * t + window, :] += part.reshape(planes, window, G)

    for m in outer:
        spread(m)
    row_send[0] = acc[:, 0, :]
    row_send[1] = acc[:, quarter + 1, :]
    pl.semaphore_wait(barrier, groups + doms - 2)
    rows = to_sides(
        "grp", me_g, groups, row_send.at[0], row_send.at[1], row_land.at[0], row_land.at[1], rsend, rrecv, 0
    )
    for m in inner:
        spread(m)
    for copy in rows:
        copy.wait_recv()
    acc[:, quarter, :] = acc[:, quarter, :] + row_land[0]
    acc[:, 1, :] = acc[:, 1, :] + row_land[1]
    border = to_sides(
        "dom", me_d, doms, acc.at[0], acc.at[slab + 1], halo.at[0], halo.at[1], hsend, hrecv, 0
    )
    for load in loads:
        load.wait()
    table_z = (table_s[0], table_s[1])

    def transform_z(j):
        base = 1 + 2 * order[j]
        values = acc[base : base + 4, 1 : quarter + 1, :] + back[base - 1 : base + 3]
        spec = dot3(dot_nt, table_z, split2(values.reshape(4 * quarter, G)))
        for c in range(chunks):
            for d in range(doms):
                row = 8 * (c * doms + d)
                for i in range(2):
                    ready_x[c, pl.ds((d * tiles + j + i) * 8, 8)] = spec[
                        row : row + 8, i * BLOCK : (i + 1) * BLOCK
                    ]

    def exchange_dom(src, dst, c, n, cut, send_sem, recv_sem, loc):
        lo, hi = cut

        def at(d):
            return pl.ds((d * tiles + lo) * 8, (hi - lo) * 8)

        copies = []
        for k in order_d:
            peer = lax.rem(me_d + k, doms)
            copies.append(
                remote(
                    src.at[c, at(peer)],
                    dst.at[c, at(me_d)],
                    send_sem.at[c, n, k - 1],
                    recv_sem.at[c, n, k - 1],
                    "dom",
                    peer,
                )
            )
        return local_copy(src.at[c, at(me_d)], dst.at[c, at(me_d)], loc.at[c, n]), copies

    def exchange_grp(src, dst, c, send_sem, recv_sem, loc):
        copies = []
        for k in order_g:
            peer = lax.rem(me_g + k, groups)
            copies.append(
                remote(
                    src.at[c, peer], dst.at[c, me_g], send_sem.at[c, k - 1], recv_sem.at[c, k - 1], "grp", peer
                )
            )
        return local_copy(src.at[c, me_g], dst.at[c, me_g], loc.at[c]), copies

    cuts = tile_cuts(tiles)
    pieces = [(c, n) for c in range(chunks) for n in range(2)]
    out_x = {}
    left_out = set()

    def send_out(c, n):
        out_x[c, n] = exchange_dom(ready_x, land_x, c, n, cuts[n], send_x, recv_x, loc_x)

    def advance(depth):
        at = len(out_x)
        if at == len(pieces):
            return
        done = [] if at - depth in left_out else out_x[pieces[at - depth]][1]
        left_out.add(at - depth)
        for copy in done:
            copy.wait_send()
        pending[:] = [other for other in pending if all(other is not copy for copy in done)]
        send_out(*pieces[at])

    joined = False
    for n, (lo, hi) in enumerate(cuts):
        if hi > tiles - 4 and not joined:
            for copy in border:
                copy.wait_recv()
            acc[1] = acc[1] + halo[1]
            acc[slab] = acc[slab] + halo[0]
            joined = True
        for j in range(lo, hi, 2):
            transform_z(j)
        send_out(0, n)

    unit = 2.0 * math.pi / G * (2.0 * math.pi / G)
    shape = (4 * cols, G)

    def signed(m):
        return jnp.where(m < G // 2, m, m - G)

    row_id = lax.broadcasted_iota(jnp.int32, shape, 0)
    my = signed(lax.broadcasted_iota(jnp.int32, shape, 1))

    def fill_green(part):
        mz = signed(me_d * (G // doms) + part * 4 + row_id // cols)
        mx = signed(me_g * cols + row_id % cols)
        squares = mx * mx + my * my + mz * mz
        wave = squares.astype(F32) * unit
        safe = jnp.where(squares > 0, wave, 1.0)
        green_s[part] = jnp.where(
            squares > 0, 4.0 * math.pi * jnp.exp(-wave / (4.0 * EWALD * EWALD)) / safe, 0.0
        ) * (1.0 / (G * G * G))

    side_rows = side_s.shape[1] // 2 - window

    def fill_weights(m):
        t, pair, local, f = atoms_of(m)
        for kind in range(2):
            wz = spline_rows(G, 0, local[2], f[2], True, kind == 1)
            high, low = split2(dot3(dot_nn, table_z, split2(wz)))
            weight_s[m, kind, 0] = high
            weight_s[m, kind, 1] = low
            base = kind * (side_rows + window)
            side_s[m, base : base + side_rows] = spline_rows(side_rows, 0, local[0], f[0], False, kind == 1)
            side_s[m, base + side_rows : base + side_rows + window] = spline_rows(
                window, tile * t, local[1], f[1], False, kind == 1
            )

    table_y = (table_s[2], table_s[3])
    forward_x = (table_s[4], table_s[5])
    back_x = (table_s[6], table_s[7])
    out_y, home_b, home_h = {}, {}, {}

    def stage_x(c):
        for n in range(2):
            arrive(out_x[c, n])
        for two in range(2):
            parts = []
            for kp in (2 * two, 2 * two + 1):
                loaded = [land_x[c, pl.ds(2 * kp + i, lines, stride=8), :] for i in range(2)]
                parts.append(jnp.concatenate(swap_blocks(loaded), axis=0))
            result = dot3(dot_nn, forward_x, split2(jnp.concatenate(parts, axis=1)))
            part = 2 * c + two
            for g in range(groups):
                ready_y[part, g] = result[g * cols : (g + 1) * cols]
            out_y[part] = exchange_grp(ready_y, land_y, part, send_y, recv_y, loc_y)

    def stage_y(part):
        arrive(out_y[part])
        rows = []
        for kp in range(2):
            cut = slice(kp * BLOCK, (kp + 1) * BLOCK)
            pairs = [
                swap_blocks([land_y[part, g, :, cut], land_y[part, g + 1, :, cut]])
                for g in range(0, groups, 2)
            ]
            for i in range(2):
                rows.append(jnp.concatenate([pair[i] for pair in pairs], axis=1))
        spectrum = dot3(dot_nn, split2(jnp.concatenate(rows, axis=0)), table_y) * green_s[part]
        result = dot3(dot_nn, split2(spectrum), table_y)
        for kp in range(2):
            for g in range(0, groups, 2):
                cut = slice(g * quarter, (g + 2) * quarter)
                both = [result[(2 * kp + i) * cols : (2 * kp + i + 1) * cols, cut] for i in range(2)]
                for i, piece in enumerate(swap_blocks(both)):
                    ready_b[part, g + i, :, kp * BLOCK : (kp + 1) * BLOCK] = piece
        home_b[part] = exchange_grp(ready_b, land_b, part, send_b, recv_b, loc_b)

    def stage_h(c):
        for two in range(2):
            arrive(home_b[2 * c + two])
            column = jnp.concatenate([land_b[2 * c + two, g] for g in range(groups)], axis=0)
            result = dot3(dot_nn, back_x, split2(column))
            for i in range(2):
                cut = slice(i * BLOCK, (i + 1) * BLOCK)
                both = swap_blocks([result[:lines, cut], result[lines:, cut]])
                for k, piece in enumerate(both):
                    ready_h[c, pl.ds(2 * (2 * two + i) + k, lines, stride=8), :] = piece
        for n, cut in enumerate(reversed(cuts)):
            home_h[c, n] = exchange_dom(ready_h, land_h, c, n, cut, send_h, recv_h, loc_h)

    edges = {}

    def gather(h, lo, hi):
        for j in range(lo, hi):
            block = jnp.concatenate(
                [land_h[c, pl.ds((d * tiles + j) * 8, 8)] for c, d in strips[16 * h : 16 * (h + 1)]],
                axis=0,
            )
            turned = block.T
            base = 1 + 2 * order[j]
            for i in range(2):
                mesh_s[h, base + i, 1 : quarter + 1, :] = turned[i * quarter : (i + 1) * quarter]

    def send_edges(h):
        edges[h] = to_sides(
            "dom",
            me_d,
            doms,
            mesh_s.at[h, 1],
            mesh_s.at[h, slab],
            mesh_s.at[h, slab + 1],
            mesh_s.at[h, 0],
            hsend,
            hrecv,
            2 + 2 * h,
        )

    def send_rows(h):
        for copy in edges[h]:
            copy.wait()
            pending[:] = [other for other in pending if other is not copy]
        edge_send[h, 0] = mesh_s[h, :, 1, :]
        edge_send[h, 1] = mesh_s[h, :, quarter, :]
        return to_sides(
            "grp",
            me_g,
            groups,
            edge_send.at[h, 0],
            edge_send.at[h, 1],
            edge_land.at[h, 0],
            edge_land.at[h, 1],
            rsend,
            rrecv,
            2 + 2 * h,
        )

    def sample(h, chosen):
        half = slice(h * BLOCK, (h + 1) * BLOCK)
        known = None
        for m in chosen:
            t, pair = atom_chunks[m]
            if t != known:
                strip = mesh_s[h, :, tile * t : tile * t + window, :].reshape(planes * window, BLOCK)
                strip = jnp.concatenate(split2(strip), axis=1)
                known = t

            def along(kind):
                high, low = weight_s[m, kind, 0, half], weight_s[m, kind, 1, half]
                return dot_nn(strip, jnp.concatenate([high, high], axis=0)) + dot_nn(
                    strip, jnp.concatenate([low, low], axis=0)
                )

            wx, wy = side_s[m, :side_rows], side_s[m, side_rows : side_rows + window]
            sx = side_s[m, side_rows + window : 2 * side_rows + window]
            sy = side_s[m, 2 * side_rows + window :]
            value, slope = along(0), along(1)
            value_y = jnp.zeros_like(wy)
            grad_y = jnp.zeros_like(wy)
            slope_y = jnp.zeros_like(wy)
            for x in range(planes):
                here = value[x * window : (x + 1) * window]
                value_y = value_y + wx[x : x + 1] * here
                grad_y = grad_y + sx[x : x + 1] * here
                slope_y = slope_y + wx[x : x + 1] * slope[x * window : (x + 1) * window]
            sums = jnp.concatenate(
                [
                    jnp.sum(one * two, axis=0, keepdims=True)
                    for one, two in ((wy, value_y), (wy, grad_y), (sy, value_y), (wy, slope_y))
                ],
                axis=0,
            )
            if h == 0:
                part_s[m, 0:4] = sums
                continue
            sums = sums + part_s[m, 0:4]
            for k, b in enumerate(pair):
                cut = slice(k * BLOCK, (k + 1) * BLOCK)
                pot[b : b + 1, :] = sums[0:1, cut]
                grad[:, b * BLOCK : (b + 1) * BLOCK] = sums[1:4, cut]

    def finish(h):
        rows = send_rows(h)
        sample(h, inner)
        for copy in rows:
            copy.wait_recv()
        mesh_s[h, :, quarter + 1, :] = edge_land[h, 0]
        mesh_s[h, :, 0, :] = edge_land[h, 1]
        sample(h, outer)

    fills = [functools.partial(fill_weights, m) for m in range(len(atom_chunks))]
    fills += [functools.partial(fill_green, part) for part in range(halves)]
    for i, fill in enumerate(fills):
        fill()
        if i == len(fills) // 2:
            advance(2)
    advance(2)
    for c in range(chunks):
        if c:
            stage_h(c - 1)
        stage_x(c)
        advance(3)
        if not c:
            advance(3)
        stage_y(2 * c)
        advance(3)
        stage_y(2 * c + 1)
    stage_h(chunks - 1)
    for h in range(2):
        needed = sorted({c for c, _ in strips[16 * h : 16 * (h + 1)]})
        for n, (lo, hi) in enumerate(reversed(cuts)):
            for c in needed:
                if (c, n) in home_h:
                    arrive(home_h.pop((c, n)))
            gather(h, lo, hi)
            if h not in edges and lo <= tiles - 4:
                send_edges(h)
        finish(h)
    for copy in pending:
        copy.wait_send()


def mesh_call(cell, frac, charge, back, table_list, doms, groups):
    slab = back.shape[0]
    quarter = back.shape[1]
    padded_y = quarter + 8
    planes = slab + 2
    tiles = slab // 2
    chunks = G // doms // 8
    atom_chunks = len(chunk_blocks(charge.shape[0]))
    atoms = 2 * BLOCK
    side_rows = 2 * (-(-planes // 8) * 8 + 24)
    dma = pltpu.SemaphoreType.DMA
    dom_shape = pltpu.VMEM((chunks, doms * tiles * 8, BLOCK), F32)
    grp_shape = pltpu.VMEM((2 * chunks, groups, G // groups, 4 * quarter), F32)
    row_shape = pltpu.VMEM((2, planes, G), F32)
    edge_shape = pltpu.VMEM((2, 2, planes, BLOCK), F32)
    args = [cell, frac, charge, back] + [part for table in table_list for part in table]
    return pl.pallas_call(
        mesh_kernel,
        out_shape=[jax.ShapeDtypeStruct(charge.shape, F32), jax.ShapeDtypeStruct(frac.shape, F32)],
        in_specs=[VMEM_SPEC] * 3 + [pl.BlockSpec(memory_space=pl.ANY)] * (len(args) - 3),
        out_specs=[VMEM_SPEC] * 2,
        scratch_shapes=[
            pltpu.VMEM((planes, padded_y, G), F32),
            pltpu.VMEM(back.shape, F32),
            pltpu.VMEM((8, G, G), BF),
            dma((9,)),
            pltpu.VMEM((2, padded_y, G), F32),
            *[row_shape] * 2,
            *[edge_shape] * 2,
            *[dom_shape] * 2,
            *[grp_shape] * 4,
            *[dom_shape] * 2,
            pltpu.VMEM((2 * chunks, 4 * (G // groups), G), F32),
            pltpu.VMEM((atom_chunks, 2, 2, G, atoms), BF),
            pltpu.VMEM((atom_chunks, side_rows, atoms), F32),
            pltpu.VMEM((atom_chunks, 8, atoms), F32),
            pltpu.VMEM((2, planes, padded_y, BLOCK), F32),
            *[dma((6,))] * 4,
            *[dma((chunks, 2, doms - 1))] * 2,
            *[dma((2 * chunks, groups - 1))] * 4,
            *[dma((chunks, 2, doms - 1))] * 2,
            dma((chunks, 2)),
            dma((2 * chunks,)),
            dma((2 * chunks,)),
            dma((chunks, 2)),
        ],
        compiler_params=pltpu.CompilerParams(
            vmem_limit_bytes=VMEM_BYTES, collective_id=0, has_side_effects=True
        ),
    )(*args)


def final_kernel(potential, gradient, energy, charge, site, field):
    site[...] = energy[...] + 0.5 * charge[...] * potential[...]
    field[...] = -gradient[...]


def tables(slab, doms):
    chunks = G // doms // 8
    plain = hartley(np.arange(G))
    z_order = np.array([d * (G // doms) + c * 8 + k for c in range(chunks) for d in range(doms) for k in range(8)])
    hz = hartley(z_order)
    x_points = np.array([slab * d + 2 * t + i for i in range(2) for d in range(doms) for t in tile_order(slab)])
    hx = hartley(x_points)
    return [np_split(t) for t in (hz.T, plain, hx, hx.T)]


def on_device(
    cell_index,
    offsets,
    species,
    pair_blocks,
    counts,
    background,
    species_embed,
    neighbour_embed,
    w_radial,
    w_hidden,
    w_charge,
    w_energy,
):
    atoms = cell_index.shape[1]
    doms = lax.axis_size("dom")
    groups = lax.axis_size("grp")
    ext = share_call(cell_index, offsets, species)
    energies, charges = pair_call(
        pair_blocks,
        counts,
        ext,
        species_embed,
        neighbour_embed,
        w_radial,
        w_hidden,
        w_charge,
        w_energy,
    )

    potential, gradient = mesh_call(
        cell_index, offsets, charges, background, tables(G // doms, doms), doms, groups
    )
    site, field = call(
        final_kernel,
        [jax.ShapeDtypeStruct(energies.shape, F32), jax.ShapeDtypeStruct(gradient.shape, F32)],
        [],
        0,
        (potential, gradient, energies, charges),
    )
    return (site.reshape(atoms), field, charges.reshape(atoms))


def solution(mesh):
    return jax.shard_map(
        on_device,
        mesh=mesh,
        in_specs=(
            P(None, ("grp", "dom")),
            P(None, ("grp", "dom")),
            P(("grp", "dom")),
            P(("grp", "dom"), None),
            P(("grp", "dom")),
            P("dom", "grp", None),
            P(),
            P(),
            P(),
            P(),
            P(),
            P(),
        ),
        out_specs=(P(("grp", "dom")), P(None, ("grp", "dom")), P(("grp", "dom"))),
        check_vma=False,
    )
```
